128 devices in a mesh: lev: 4 (over x), row: 32 (over y, z, core).
Axes of the slice: x: 4, y: 4, z: 4, core: 2. Of those that a mesh axis runs over, the one named last changes fastest.
Arguments:
- control: float32 [16, 1536, 3072], P('lev', 'row'), may hold values from -6 to 6
- decay_lon: float32 [1536], P('row'), may hold values from 0.5 to 0.99
- decay_lat: float32 [3072], replicated, may hold values from 0.5 to 0.99
- decay_vert: float32 [1536, 3072], P('row'), may hold values from 0.5 to 0.97
Outputs:
- increment: float32 [16, 1536, 3072], P('lev', 'row')
The draws below stay inside these ranges and needn't reach their ends.
All inputs are finite; a program needn't handle non-finite values.
Results may differ from the reference program's by a relative error of at most 0.002.
Values sent between devices are 32-bit elements; how exact they have to be, the bound alone decides.
A program may use at most 192 MiB of HBM per device.

```python
import math
import jax
import jax.numpy as jnp
from jax import lax

NLON = 3072
NLAT = 1536
LEVELS = 16


def levels(stream_key, shape, pieces, low, top_value):
    level, own = 1.0, jax.random.fold_in(stream_key, 6)
    for axis_at, parts in pieces:
        draws = jnp.exp(jax.random.uniform(jax.random.fold_in(own, axis_at), (parts,), jnp.float32, low / len(pieces), top_value / len(pieces)))
        level = level * jnp.repeat(draws, shape[axis_at] // parts).reshape([-1 if axis == axis_at else 1 for axis in range(len(shape))])
    return level


def scatter_about(stream_key, shape, deviation, most, split=(), kind=jnp.bfloat16):
    values = deviation * jax.random.normal(stream_key, shape, jnp.float32)
    if split:
        values = values * levels(stream_key, shape, split, -0.22, 0.18)
    return jnp.clip(values, -most, most).astype(kind)


def setup_inputs(seed: int = 0) -> dict:
    splits = jax.random.split(jax.random.key(seed), 5)
    control = scatter_about(splits[0], (LEVELS, NLAT, NLON), 1.0, 6.0, ((0, 4), (1, 32)), jnp.float32)
    decay_lon = jnp.clip(jnp.exp(math.log(0.99) - 0.68309685 * jax.random.uniform(splits[1], (NLAT,), jnp.float32) ** levels(splits[1], (NLAT,), ((0, 32),), -0.2, 0.2)), 0.5, 0.99)
    decay_lat = jnp.clip(jnp.exp(jax.random.uniform(splits[2], (NLON,), jnp.float32, math.log(0.5), math.log(0.99))), 0.5, 0.99)
    decay_vert = jnp.clip(jnp.exp(math.log(0.97) - 0.662688 * jax.random.uniform(splits[3], (NLAT, NLON), jnp.float32) ** levels(splits[3], (NLAT, NLON), ((0, 32),), -0.2, 0.2)), 0.5, 0.97)
    return dict(control=control, decay_lon=decay_lon, decay_lat=decay_lat, decay_vert=decay_vert)


def sweep_gain(decay):
    sq = decay * decay
    return ((1.0 - sq) ** 7 / (1.0 + 9.0 * sq + 9.0 * sq * sq + sq * sq * sq)) ** 0.25


def forward_sweep(data, decay):
    gain = sweep_gain(decay)

    def step(state, row):
        first, second = state
        value = gain * row + 2.0 * decay * first - decay * decay * second
        return (value, first), value

    zeros = jnp.zeros(data.shape[1:], data.dtype)
    _, result = lax.scan(step, (zeros, zeros), data)
    return result


def line_filter(data, decay):
    ahead = forward_sweep(data, decay)
    return jnp.flip(forward_sweep(jnp.flip(ahead, 0), decay), 0)


def reference(control, decay_lon, decay_lat, decay_vert):
    lines = jnp.moveaxis(control, 2, 0)
    poles = jnp.broadcast_to(decay_lon[None, :], lines.shape[1:])
    along_lon = jnp.moveaxis(line_filter(lines, poles), 0, 2)
    lines = jnp.moveaxis(along_lon, 1, 0)
    poles = jnp.broadcast_to(decay_lat[None, :], lines.shape[1:])
    along_lat = jnp.moveaxis(line_filter(lines, poles), 0, 1)
    return line_filter(along_lat, decay_vert)
```

```python
import functools

import jax
import jax.numpy as jnp
from jax import lax
from jax.experimental import pallas as pl
from jax.experimental.pallas import tpu as pltpu
from jax.sharding import PartitionSpec as P

MESH = pl.DeviceIdType.MESH

LANES = 128
SEG = 24
ROWS = 48
LEV = 4
LINES = LEV * ROWS
BG = SEG // 8
NR = 32
MSG = 16
JC = 6
NJ = ROWS // JC
NCH = BG * NJ
CH = 2 * JC * 8
LAG = 2


def gain_sq(r):
    q = r * r
    a = (1.0 - r) * (1.0 + r)
    a2 = a * a
    a4 = a2 * a2
    return jnp.sqrt(a4 * a2 * a / (1.0 + q * (9.0 + q * (9.0 + q))))


def sums_double(q, n, qn, s0, s1, s2):
    return (
        s0 + qn * s0,
        s1 + qn * (s1 + n * s0),
        s2 + qn * (s2 + (2.0 * n) * s1 + (n * n) * s0),
    )


def sums(q, base, doublings):
    s0 = jnp.ones_like(q)
    s1 = jnp.ones_like(q)
    s2 = jnp.ones_like(q)
    qn = q
    for t in range(1, base):
        s0 = s0 + qn
        s1 = s1 + (t + 1.0) * qn
        s2 = s2 + ((t + 1.0) * (t + 1.0)) * qn
        qn = qn * q
    n = float(base)
    for _ in range(doublings):
        s0, s1, s2 = sums_double(q, n, qn, s0, s1, s2)
        qn = qn * qn
        n = 2.0 * n
    return s0, s1, s2


def power(r, base, doublings):
    p = r
    for _ in range(base - 1):
        p = p * r
    for _ in range(doublings):
        p = p * p
    return p


def kernel(ctrl, dlon, dlat, dvert, out, X, Y, Z, PV, EU, ED, EV, EW,
           SB, RB, RP, CB, SR, SL, FL, FR,
           in_sem, pv_sem, out_sem, s1_sem, r1_sem, s2_sem, r2_sem,
           sr_sem, sl_sem, fl_sem, fr_sem):
    lev = lax.axis_index("lev")
    me = lax.axis_index("row")
    barrier = pltpu.get_barrier_semaphore()

    def in_copy(b):
        return pltpu.make_async_copy(
            ctrl.at[:, pl.ds(pl.multiple_of(b * LANES, LANES), LANES)],
            X.at[pl.ds(pl.multiple_of(b * LINES, 8), LINES), :], in_sem.at[b])

    def pv_copy(b):
        return pltpu.make_async_copy(
            dvert.at[:, pl.ds(pl.multiple_of(b * LANES, LANES), LANES)],
            PV.at[pl.ds(pl.multiple_of(b * ROWS, 8), ROWS), :], pv_sem.at[b])

    def out_copy(b):
        return pltpu.make_async_copy(
            X.at[pl.ds(pl.multiple_of(b * LINES, 8), LINES), :],
            out.at[:, pl.ds(pl.multiple_of(b * LANES, LANES), LANES)], out_sem.at[b])

    def loop(n, body):
        def step(i, carry):
            body(i)
            return carry
        lax.fori_loop(0, n, step, 0)

    loop(SEG, lambda b: in_copy(b).start())
    loop(SEG, lambda b: pv_copy(b).start())

    def greet(i):
        pl.semaphore_signal(barrier, inc=1, device_id=(lev, lax.rem(me + i + 1, NR)), device_id_type=MESH)
    loop(NR - 1, greet)

    @pl.when(lev > 0)
    def _():
        pl.semaphore_signal(barrier, inc=1, device_id=(lev - 1, me), device_id_type=MESH)

    @pl.when(lev < 3)
    def _():
        pl.semaphore_signal(barrier, inc=1, device_id=(lev + 1, me), device_id_type=MESH)

    X[pl.ds(SEG * LINES, 32), :] = jnp.zeros((32, LANES), jnp.float32)

    def lon_in(b):
        in_copy(b).wait()
    loop(SEG, lon_in)

    def turn_in(b):
        for g in range(2):
            tile = X[pl.ds(pl.multiple_of(b * LINES + g * 96, 8), LANES), :]
            Y[pl.ds(g * LANES * SEG + b, LANES, stride=SEG), :] = tile.T
    loop(SEG, turn_in)

    r = dlon[0:8, :]
    zero = jnp.zeros((8, LANES), jnp.float32)
    one = jnp.ones((8, LANES), jnp.float32)
    chains = [(g, bg) for g in range(2) for bg in range(BG)]

    def at_lon(g, bg, l):
        return pl.ds(pl.multiple_of((g * LANES + l) * SEG + bg * 8, 8), 8)

    def lon_ends(l, state):
        p, pp, rest = state
        new = []
        for i, (g, bg) in enumerate(chains):
            u, d, v, w = rest[i]
            d = r * d + Y[at_lon(g, bg, l), :]
            u = r * u + d
            new.append((u, d, v + pp * u, w + p * u))
        p = r * p
        return (p, r * pp + p, tuple(new))

    init = (one, one, tuple((zero, zero, zero, zero) for _ in chains))
    _, _, ends = lax.fori_loop(0, LANES, lon_ends, init, unroll=2)
    for i, (g, bg) in enumerate(chains):
        at = pl.ds(g * SEG + bg * 8, 8)
        EU[at, :], ED[at, :], EV[at, :], EW[at, :] = ends[i]

    r2 = dlon[0:2, :]
    s0, s1, s2 = sums(r2 * r2, 1, 7)
    rn = power(r2, 1, 7)
    n = float(LANES)
    z2 = jnp.zeros((2, LANES), jnp.float32)

    def lon_fwd(b, state):
        u, d = state
        at = pl.ds(b, 2, stride=SEG)
        eu, ed = EU[at, :], ED[at, :]
        EU[at, :] = u
        ED[at, :] = d
        return (rn * (u + n * d) + eu, rn * d + ed)
    lax.fori_loop(0, SEG, lon_fwd, (z2, z2))

    def lon_bwd(i, state):
        v, w = state
        at = pl.ds(SEG - 1 - i, 2, stride=SEG)
        u, d = EU[at, :], ED[at, :]
        ev = EV[at, :] + r2 * (s1 * u + s2 * d)
        ew = EW[at, :] + r2 * (s0 * u + s1 * d)
        EV[at, :] = v
        EW[at, :] = w
        return (rn * (v + n * w) + ev, rn * w + ew)
    lax.fori_loop(0, SEG, lon_bwd, (z2, z2))

    def lon_ahead(l, state):
        new = []
        for i, (g, bg) in enumerate(chains):
            u, d = state[i]
            d = r * d + Y[at_lon(g, bg, l), :]
            u = r * u + d
            Y[at_lon(g, bg, l), :] = u
            new.append((u, d))
        return tuple(new)

    start = tuple((EU[pl.ds(g * SEG + bg * 8, 8), :], ED[pl.ds(g * SEG + bg * 8, 8), :]) for g, bg in chains)
    lax.fori_loop(0, LANES, lon_ahead, start, unroll=2)

    g_lon = gain_sq(r)

    def lon_back(i, state):
        l = LANES - 1 - i
        new = []
        for k, (g, bg) in enumerate(chains):
            v, w = state[k]
            w = r * w + Y[at_lon(g, bg, l), :]
            v = r * v + w
            Y[at_lon(g, bg, l), :] = v * g_lon
            new.append((v, w))
        return tuple(new)

    start = tuple((EV[pl.ds(g * SEG + bg * 8, 8), :], EW[pl.ds(g * SEG + bg * 8, 8), :]) for g, bg in chains)
    lax.fori_loop(0, LANES, lon_back, start, unroll=2)

    def turn_out(b):
        for g in range(2):
            tile = Y[pl.ds(g * LANES * SEG + b, LANES, stride=SEG), :].T
            for k in range(2):
                Z[pl.ds((2 * g + k) * ROWS * SEG + b, ROWS, stride=SEG), :] = tile[k * ROWS:(k + 1) * ROWS, :]
    loop(SEG, turn_out)

    def at_lat(k, j, bg):
        return pl.ds(pl.multiple_of((k * ROWS + j) * SEG + bg * 8, 8), 8)

    loop(NR, lambda i: SB.__setitem__((pl.ds(pl.multiple_of(i * MSG, 8), 8), slice(None)), zero))
    loop(NR, lambda i: SB.__setitem__((pl.ds(pl.multiple_of(i * MSG + 8, 8), 8), slice(None)), zero))
    for bg in range(BG):
        rl = dlat[bg * 8:(bg + 1) * 8, :]

        def lat_ends(j, state, rl=rl, bg=bg):
            p, pp, rest = state
            new = []
            for k in range(LEV):
                u, d, v, w = rest[k]
                d = rl * d + Z[at_lat(k, j, bg), :]
                u = rl * u + d
                new.append((u, d, v + pp * u, w + p * u))
            p = rl * p
            return (p, rl * pp + p, tuple(new))

        init = (one, one, tuple((zero, zero, zero, zero) for _ in range(LEV)))
        _, _, ends = lax.fori_loop(0, ROWS, lat_ends, init, unroll=2)
        for k in range(LEV):
            for val in range(4):
                SB[pl.ds(k * 8 * MSG + val * 4 + bg, 8, stride=MSG), :] = ends[k][val]

    neighbours = (lev > 0).astype(jnp.int32) + (lev < 3).astype(jnp.int32)
    pl.semaphore_wait(barrier, NR - 1 + neighbours)

    def slot(ref, i):
        return ref.at[pl.ds(pl.multiple_of(i * MSG, 8), MSG), :]

    def exchange(src, dst, ssem, rsem):
        def send(i):
            p = lax.rem(me + i + 1, NR)
            pltpu.make_async_remote_copy(
                src_ref=slot(src, p), dst_ref=slot(dst, me), send_sem=ssem.at[p], recv_sem=rsem.at[me],
                device_id=(lev, p), device_id_type=MESH).start()
        loop(NR - 1, send)
        at = pl.ds(pl.multiple_of(me * MSG, 8), MSG)
        dst[at, :] = src[at, :]

        def get(i):
            p = lax.rem(me + i + 1, NR)
            pltpu.make_async_remote_copy(
                src_ref=slot(src, p), dst_ref=slot(dst, p), send_sem=ssem.at[p], recv_sem=rsem.at[p],
                device_id=(lev, p), device_id_type=MESH).wait_recv()
        loop(NR - 1, get)

    def sent(src, dst, ssem, rsem):
        def one_sent(i):
            p = lax.rem(me + i + 1, NR)
            pltpu.make_async_remote_copy(
                src_ref=slot(src, p), dst_ref=slot(dst, me), send_sem=ssem.at[p], recv_sem=rsem.at[me],
                device_id=(lev, p), device_id_type=MESH).wait_send()
        loop(NR - 1, one_sent)

    exchange(SB, RB, s1_sem, r1_sem)

    ro = dlat[pl.ds(lax.rem(me, 8), 4, stride=8), :]
    o0, o1, o2 = sums(ro * ro, 3, 4)
    on = power(ro, 3, 4)
    m = float(ROWS)
    z4 = jnp.zeros((4, LANES), jnp.float32)

    def at_msg(s, val):
        return pl.ds(pl.multiple_of(s * MSG + val * 4, 4), 4)

    def own_fwd(s, state):
        u, d = state
        RP[at_msg(s, 0), :] = u
        RP[at_msg(s, 1), :] = d
        return (on * (u + m * d) + RB[at_msg(s, 0), :], on * d + RB[at_msg(s, 1), :])
    lax.fori_loop(0, NR, own_fwd, (z4, z4))

    def own_bwd(i, state):
        v, w = state
        s = NR - 1 - i
        u, d = RP[at_msg(s, 0), :], RP[at_msg(s, 1), :]
        RP[at_msg(s, 2), :] = v
        RP[at_msg(s, 3), :] = w
        ev = RB[at_msg(s, 2), :] + ro * (o1 * u + o2 * d)
        ew = RB[at_msg(s, 3), :] + ro * (o0 * u + o1 * d)
        return (on * (v + m * w) + ev, on * w + ew)
    lax.fori_loop(0, NR, own_bwd, (z4, z4))

    exchange(RP, CB, s2_sem, r2_sem)

    for bg in range(BG):
        rl = dlat[bg * 8:(bg + 1) * 8, :]
        g_lat = gain_sq(rl)

        def come(k, val, bg=bg):
            return CB[pl.ds(k * 8 * MSG + val * 4 + bg, 8, stride=MSG), :]

        def lat_ahead(j, state, rl=rl, bg=bg):
            new = []
            for k in range(LEV):
                u, d = state[k]
                d = rl * d + Z[at_lat(k, j, bg), :]
                u = rl * u + d
                Z[at_lat(k, j, bg), :] = u
                new.append((u, d))
            return tuple(new)
        lax.fori_loop(0, ROWS, lat_ahead, tuple((come(k, 0), come(k, 1)) for k in range(LEV)), unroll=2)

        def lat_back(i, state, rl=rl, bg=bg, g_lat=g_lat):
            j = ROWS - 1 - i
            new = []
            for k in range(LEV):
                v, w = state[k]
                w = rl * w + Z[at_lat(k, j, bg), :]
                v = rl * v + w
                Z[at_lat(k, j, bg), :] = v * g_lat
                new.append((v, w))
            return tuple(new)
        lax.fori_loop(0, ROWS, lat_back, tuple((come(k, 2), come(k, 3)) for k in range(LEV)), unroll=2)

    loop(SEG, lambda b: pv_copy(b).wait())

    def chunk(ref, c):
        return ref.at[pl.ds(pl.multiple_of(c * CH, 8), CH), :]

    def right(c):
        return pltpu.make_async_remote_copy(
            src_ref=chunk(SR, c), dst_ref=chunk(FL, c), send_sem=sr_sem.at[c], recv_sem=fl_sem.at[c],
            device_id=(lax.rem(lev + 1, 4), me), device_id_type=MESH)

    def left(c):
        return pltpu.make_async_remote_copy(
            src_ref=chunk(SL, c), dst_ref=chunk(FR, c), send_sem=sl_sem.at[c], recv_sem=fr_sem.at[c],
            device_id=(lax.rem(lev + 3, 4), me), device_id_type=MESH)

    def each(c, body):
        bg = c // NJ
        j0 = lax.rem(c, NJ) * JC
        for jj in range(JC):
            j = j0 + jj
            rv = PV[pl.ds(bg * 8 * ROWS + j, 8, stride=ROWS), :]

            def at(val, jj=jj):
                return pl.ds(pl.multiple_of(c * CH + (val * JC + jj) * 8, 8), 8)

            def zat(k, j=j):
                return pl.ds(pl.multiple_of((k * ROWS + j) * SEG + bg * 8, 8), 8)

            def put(vals, rv=rv, j=j):
                gv = gain_sq(rv)
                for k in range(LEV):
                    X[pl.ds(bg * 8 * LINES + k * ROWS + j, 8, stride=LINES), :] = vals[k] * gv
            body(rv, at, zat, put)

    def ahead(rv, xs, u, d):
        us = []
        for x in xs:
            d = x if d is None else rv * d + x
            u = d if u is None else rv * u + d
            us.append(u)
        return us, u, d

    def back(rv, us, v, w):
        vs = [None] * LEV
        for k in range(LEV - 1, -1, -1):
            w = us[k] if w is None else rv * w + us[k]
            v = w if v is None else rv * v + w
            vs[k] = v
        return vs, v, w

    def four(q):
        return (1.0 + q * (1.0 + q * (1.0 + q)),
                1.0 + q * (2.0 + q * (3.0 + 4.0 * q)),
                1.0 + q * (4.0 + q * (9.0 + 16.0 * q)))

    def send_out(c):
        @pl.when(lax.rem(c, NJ) == NJ - 1)
        def _():
            loop(8, lambda b: out_copy((c // NJ) * 8 + b).start())

    @pl.when(lev == 0)
    def _():
        def first(c):
            def body(rv, at, zat, put):
                us, u, d = ahead(rv, [Z[zat(k), :] for k in range(LEV)], None, None)
                for k in range(LEV):
                    Z[zat(k), :] = us[k]
                SR[at(0), :] = u
                SR[at(1), :] = d
            each(c, body)
            right(c).start()
        loop(NCH, first)

        def second(c):
            left(c).wait_recv()

            def body(rv, at, zat, put):
                vs, _, _ = back(rv, [Z[zat(k), :] for k in range(LEV)], FR[at(0), :], FR[at(1), :])
                put(vs)
            each(c, body)
            send_out(c)
        loop(NCH, second)
        loop(NCH, lambda c: right(c).wait_send())

    @pl.when(lev == 3)
    def _():
        def first(c):
            def body(rv, at, zat, put):
                us, _, _ = ahead(rv, [Z[zat(k), :] for k in range(LEV)], None, None)
                _, v, w = back(rv, us, None, None)
                SL[at(0), :] = v
                SL[at(1), :] = w
            each(c, body)
            left(c).start()
        loop(NCH, first)

        def second(c):
            right(c).wait_recv()

            def body(rv, at, zat, put):
                us, _, _ = ahead(rv, [Z[zat(k), :] for k in range(LEV)], FL[at(0), :], FL[at(1), :])
                vs, _, _ = back(rv, us, None, None)
                put(vs)
            each(c, body)
            send_out(c)
        loop(NCH, second)
        loop(NCH, lambda c: left(c).wait_send())

    def staged(first, second):
        def step(i):
            @pl.when(i < NCH)
            def _():
                first(i)

            @pl.when(i >= LAG)
            def _():
                second(i - LAG)
        loop(NCH + LAG, step)
        loop(NCH, lambda c: right(c).wait_send())
        loop(NCH, lambda c: left(c).wait_send())

    @pl.when(lev == 1)
    def _():
        def first(c):
            right(c).wait_recv()

            def body(rv, at, zat, put):
                us, u, d = ahead(rv, [Z[zat(k), :] for k in range(LEV)], FL[at(0), :], FL[at(1), :])
                for k in range(LEV):
                    Z[zat(k), :] = us[k]
                SR[at(0), :] = u
                SR[at(1), :] = d
            each(c, body)
            right(c).start()

        def second(c):
            left(c).wait_recv()

            def body(rv, at, zat, put):
                q = rv * rv
                q2 = q * q
                e0, e1, e2 = sums_double(q, 4.0, q2 * q2, *four(q))
                u, d = SR[at(0), :], SR[at(1), :]
                v = FR[at(0), :] + rv * (e1 * u + e2 * d)
                w = FR[at(1), :] + rv * (e0 * u + e1 * d)
                vs, v, w = back(rv, [Z[zat(k), :] for k in range(LEV)], v, w)
                SL[at(0), :] = v
                SL[at(1), :] = w
                put(vs)
            each(c, body)
            left(c).start()
            send_out(c)
        staged(first, second)

    @pl.when(lev == 2)
    def _():
        def first(c):
            left(c).wait_recv()

            def body(rv, at, zat, put):
                us, u, d = ahead(rv, [Z[zat(k), :] for k in range(LEV)], None, None)
                e0, e1, e2 = four(rv * rv)
                v = FR[at(0), :] + rv * (e1 * u + e2 * d)
                w = FR[at(1), :] + rv * (e0 * u + e1 * d)
                _, v, w = back(rv, us, v, w)
                SL[at(0), :] = v
                SL[at(1), :] = w
            each(c, body)
            left(c).start()

        def second(c):
            right(c).wait_recv()

            def body(rv, at, zat, put):
                us, u, d = ahead(rv, [Z[zat(k), :] for k in range(LEV)], FL[at(0), :], FL[at(1), :])
                SR[at(0), :] = u
                SR[at(1), :] = d
                e0, e1, e2 = four(rv * rv)
                v = FR[at(0), :] + rv * (e1 * u + e2 * d)
                w = FR[at(1), :] + rv * (e0 * u + e1 * d)
                vs, _, _ = back(rv, us, v, w)
                put(vs)
            each(c, body)
            right(c).start()
            send_out(c)
        staged(first, second)

    loop(SEG, lambda b: out_copy(b).wait())
    sent(SB, RB, s1_sem, r1_sem)
    sent(RP, CB, s2_sem, r2_sem)


def per_device(control, decay_lon, decay_lat, decay_vert):
    lines = control.reshape(LINES, SEG * LANES)
    lon = jnp.concatenate([decay_lon, decay_lon, decay_lon[:32]])
    lon = jnp.broadcast_to(lon[None, :], (8, LANES))
    lat = jnp.concatenate([decay_lat.reshape(SEG, LANES), jnp.full((8, LANES), 0.5, jnp.float32)])
    any_space = pl.BlockSpec(memory_space=pl.ANY)
    vmem = pl.BlockSpec(memory_space=pltpu.VMEM)
    f32 = jnp.float32
    dma = pltpu.SemaphoreType.DMA
    filtered = pl.pallas_call(
        kernel,
        out_shape=jax.ShapeDtypeStruct((LINES, SEG * LANES), f32),
        in_specs=[any_space, vmem, vmem, any_space],
        out_specs=any_space,
        scratch_shapes=[
            pltpu.VMEM((SEG * LINES + 32, LANES), f32),
            pltpu.VMEM((2 * LANES * SEG, LANES), f32),
            pltpu.VMEM((LINES * SEG, LANES), f32),
            pltpu.VMEM((SEG * ROWS, LANES), f32),
        ] + [pltpu.VMEM((2 * SEG, LANES), f32)] * 4
        + [pltpu.VMEM((NR * MSG, LANES), f32)] * 4
        + [pltpu.VMEM((NCH * CH, LANES), f32)] * 4
        + [dma((SEG,))] * 3 + [dma((NR,))] * 4 + [dma((NCH,))] * 4,
        compiler_params=pltpu.CompilerParams(
            collective_id=0, has_side_effects=True, vmem_limit_bytes=48 * 1024 * 1024),
        name="filters",
    )(lines, lon, lat, decay_vert)
    return filtered.reshape(LEV, ROWS, SEG * LANES)


def solution(mesh):
    in_specs = (P("lev", "row", None), P("row"), P(), P("row", None))
    out_specs = P("lev", "row", None)
    return jax.shard_map(
        per_device, mesh=mesh, in_specs=in_specs, out_specs=out_specs, check_vma=False
    )
```

```python
import functools

import jax
import jax.numpy as jnp
from jax import lax
from jax.experimental import pallas as pl
from jax.experimental.pallas import tpu as pltpu
from jax.sharding import PartitionSpec as P

MESH = pl.DeviceIdType.MESH

LANES = 128
SEG = 24
ROWS = 48
LEV = 4
LINES = LEV * ROWS
BG = SEG // 8
NR = 32
MSG = 8
JC = 4
NJ = ROWS // JC
NCH = BG * NJ
CH = 2 * JC * 8
LAG = 4


def gain_sq(r):
    q = r * r
    a = (1.0 - r) * (1.0 + r)
    a2 = a * a
    a4 = a2 * a2
    return jnp.sqrt(a4 * a2 * a / (1.0 + q * (9.0 + q * (9.0 + q))))


def sums_double(q, n, qn, s0, s1, s2):
    return (
        s0 + qn * s0,
        s1 + qn * (s1 + n * s0),
        s2 + qn * (s2 + (2.0 * n) * s1 + (n * n) * s0),
    )


def sums(q, base, doublings):
    s0 = jnp.ones_like(q)
    s1 = jnp.ones_like(q)
    s2 = jnp.ones_like(q)
    qn = q
    for t in range(1, base):
        s0 = s0 + qn
        s1 = s1 + (t + 1.0) * qn
        s2 = s2 + ((t + 1.0) * (t + 1.0)) * qn
        qn = qn * q
    n = float(base)
    for _ in range(doublings):
        s0, s1, s2 = sums_double(q, n, qn, s0, s1, s2)
        qn = qn * qn
        n = 2.0 * n
    return s0, s1, s2


def power(r, base, doublings):
    p = r
    for _ in range(base - 1):
        p = p * r
    for _ in range(doublings):
        p = p * p
    return p


def sublanes():
    return lax.broadcasted_iota(jnp.int32, (8, LANES), 0)


def carry_powers(rn):
    one, two, four = rn, rn * rn, (rn * rn) * (rn * rn)

    def by(idx):
        p = jnp.where(idx % 2 == 1, one, 1.0)
        p = p * jnp.where((idx // 2) % 2 == 1, two, 1.0)
        return p * jnp.where(idx // 4 == 1, four, 1.0)
    return one, two, four, four * four, by(sublanes()), by(7 - sublanes())


def block_carries(us, ds, powers, n, rev):
    r1, r2, r4, r8, up, down = powers
    idx = 7 - sublanes() if rev else sublanes()
    along = down if rev else up
    far = (n * idx.astype(jnp.float32))

    def shifted(x, t):
        return jnp.where(idx >= t, pltpu.roll(x, 8 - t if rev else t, 0), 0.0)

    def last(x):
        row = x[0:1, :] if rev else x[7:8, :]
        return jnp.broadcast_to(row, (8, LANES))

    cu = jnp.zeros((8, LANES), jnp.float32)
    cd = cu
    out = [None] * len(us)
    order = range(len(us))
    for i in (reversed(order) if rev else order):
        u, d = us[i], ds[i]
        for t, rt in ((1, r1), (2, r2), (4, r4)):
            su, sd = shifted(u, t), shifted(d, t)
            u = u + rt * (su + (n * t) * sd)
            d = d + rt * sd
        out[i] = (shifted(u, 1) + along * (cu + far * cd), shifted(d, 1) + along * cd)
        cu, cd = r8 * (cu + (8.0 * n) * cd) + last(u), r8 * cd + last(d)
    return out


def kernel(ctrl, dlon, dlat, dvert, out, X, Y, Z, PV, DN, DL,
           SB, RB, RP, CB, SR, SL, FL, FR,
           in_sem, pv_sem, dn_sem, dl_sem, s1_sem, r1_sem, s2_sem, r2_sem,
           sr_sem, sl_sem, fl_sem, fr_sem):
    lev = lax.axis_index("lev")
    me = lax.axis_index("row")
    barrier = pltpu.get_barrier_semaphore()

    def in_copy(b):
        return pltpu.make_async_copy(
            ctrl.at[:, pl.ds(pl.multiple_of(b * LANES, LANES), LANES)],
            X.at[pl.ds(pl.multiple_of(b * LINES, 8), LINES), :], in_sem.at[b])

    def pv_copy(b):
        return pltpu.make_async_copy(
            dvert.at[:, pl.ds(pl.multiple_of(b * LANES, LANES), LANES)],
            PV.at[pl.ds(pl.multiple_of(b * ROWS, 8), ROWS), :], pv_sem.at[b])

    dn_copy = pltpu.make_async_copy(dlon, DN, dn_sem)
    dl_copy = pltpu.make_async_copy(dlat, DL, dl_sem)

    def loop(n, body, unroll=1):
        def step(i, carry):
            body(i)
            return carry
        lax.fori_loop(0, n, step, 0, unroll=unroll)

    dn_copy.start()
    loop(SEG, lambda b: in_copy(b).start())
    dl_copy.start()
    loop(SEG, lambda b: pv_copy(b).start())

    def greet(i):
        pl.semaphore_signal(barrier, inc=1, device_id=(lev, lax.rem(me + i + 1, NR)), device_id_type=MESH)
    loop(NR - 1, greet)

    @pl.when(lev > 0)
    def _():
        pl.semaphore_signal(barrier, inc=1, device_id=(lev - 1, me), device_id_type=MESH)

    @pl.when(lev < 3)
    def _():
        pl.semaphore_signal(barrier, inc=1, device_id=(lev + 1, me), device_id_type=MESH)

    zero = jnp.zeros((8, LANES), jnp.float32)
    one = jnp.ones((8, LANES), jnp.float32)
    rest = jnp.zeros((LANES - 96, LANES), jnp.float32)
    loop(BG * NR, lambda i: SB.__setitem__((pl.ds(pl.multiple_of(i * MSG, 8), 8), slice(None)), zero))

    def turn_in(i):
        for k in range(4):
            in_copy(4 * i + k).wait()
        for k in range(4):
            b = 4 * i + k
            for g in range(2):
                tile = X[pl.ds(pl.multiple_of(b * LINES + g * 96, 8), 96), :]
                Y[pl.ds(g * LANES * SEG + b, LANES, stride=SEG), :] = jnp.concatenate([tile, rest]).T
    loop(SEG // 4, turn_in)

    dn_copy.wait()
    line = DN[...]
    line = jnp.concatenate([line, line, line[:, :32]], axis=1)
    r = jnp.broadcast_to(line, (8, LANES))
    chains = [(g, bg) for g in range(2) for bg in range(BG)]
    BLK = 4

    def at_lon(g, bg, l):
        return pl.ds(pl.multiple_of((g * LANES + l) * SEG + bg * 8, 8), 8)

    def lon_ends(l, state):
        p, pp, rest = state
        new = []
        for i, (g, bg) in enumerate(chains):
            u, d, v, w = rest[i]
            d = r * d + Y[at_lon(g, bg, l), :]
            u = r * u + d
            new.append((u, d, v + pp * u, w + p * u))
        p = r * p
        return (p, r * pp + p, tuple(new))

    init = (one, one, tuple((zero, zero, zero, zero) for _ in chains))
    _, _, ends = lax.fori_loop(0, LANES, lon_ends, init, unroll=4)

    s0, s1, s2 = sums(r * r, 1, 7)
    lon_powers = carry_powers(power(r, 1, 7))
    n = float(LANES)
    ahead_in, back_in = {}, {}
    for g in range(2):
        of = [ends[g * BG + bg] for bg in range(BG)]
        states = block_carries([e[0] for e in of], [e[1] for e in of], lon_powers, n, False)
        vs = [e[2] + r * (s1 * u + s2 * d) for e, (u, d) in zip(of, states)]
        ws = [e[3] + r * (s0 * u + s1 * d) for e, (u, d) in zip(of, states)]
        backs = block_carries(vs, ws, lon_powers, n, True)
        for bg in range(BG):
            ahead_in[g, bg] = states[bg]
            back_in[g, bg] = backs[bg]

    def lon_ahead(i, state):
        l0 = i * BLK
        xs = [[Y[at_lon(g, bg, l0 + q), :] for g, bg in chains] for q in range(BLK)]
        state = list(state)
        for q in range(BLK):
            for k in range(len(chains)):
                u, d = state[k]
                d = r * d + xs[q][k]
                u = r * u + d
                state[k] = (u, d)
                xs[q][k] = u
        for q in range(BLK):
            for k, (g, bg) in enumerate(chains):
                Y[at_lon(g, bg, l0 + q), :] = xs[q][k]
        return tuple(state)

    lax.fori_loop(0, LANES // BLK, lon_ahead, tuple(ahead_in[ch] for ch in chains))

    g_lon = gain_sq(r)

    def at_lat(k, j, bg):
        return pl.ds(pl.multiple_of((k * ROWS + j) * SEG + bg * 8, 8), 8)

    def slot(ref, bg, i):
        return ref.at[pl.ds(pl.multiple_of((bg * NR + i) * MSG, 8), MSG), :]

    def message(src, dst, ssem, rsem, bg, p, at):
        return pltpu.make_async_remote_copy(
            src_ref=slot(src, bg, p), dst_ref=slot(dst, bg, at), send_sem=ssem.at[bg * NR + p],
            recv_sem=rsem.at[bg * NR + at], device_id=(lev, p), device_id_type=MESH)

    def send(src, dst, ssem, rsem, bg):
        def to(i):
            p = lax.rem(me + i + 1, NR)
            message(src, dst, ssem, rsem, bg, p, me).start()
        loop(NR - 1, to)
        at = pl.ds(pl.multiple_of((bg * NR + me) * MSG, 8), MSG)
        dst[at, :] = src[at, :]

    def get(src, dst, ssem, rsem, bg):
        def of(i):
            p = lax.rem(me + i + 1, NR)
            message(src, dst, ssem, rsem, bg, p, p).wait_recv()
        loop(NR - 1, of)

    def sent(src, dst, ssem, rsem, bg):
        def to(i):
            p = lax.rem(me + i + 1, NR)
            message(src, dst, ssem, rsem, bg, p, me).wait_send()
        loop(NR - 1, to)

    for bg in range(BG):
        def lon_back(i, state, bg=bg):
            l0 = LANES - BLK - i * BLK
            xs = [[Y[at_lon(g, bg, l0 + q), :] for g in range(2)] for q in range(BLK)]
            state = list(state)
            for q in range(BLK - 1, -1, -1):
                for g in range(2):
                    v, w = state[g]
                    w = r * w + xs[q][g]
                    v = r * v + w
                    state[g] = (v, w)
                    xs[q][g] = v * g_lon
            for q in range(BLK):
                for g in range(2):
                    Y[at_lon(g, bg, l0 + q), :] = xs[q][g]
            return tuple(state)

        lax.fori_loop(0, LANES // BLK, lon_back, (back_in[0, bg], back_in[1, bg]), unroll=2)

        def turn_out(i, bg=bg):
            for q in range(4):
                b = bg * 8 + i * 4 + q
                for g in range(2):
                    tile = Y[pl.ds(g * LANES * SEG + b, LANES, stride=SEG), :].T
                    for k in range(2):
                        Z[pl.ds((2 * g + k) * ROWS * SEG + b, ROWS, stride=SEG), :] = tile[k * ROWS:(k + 1) * ROWS, :]
        loop(2, turn_out)

        if bg == 0:
            dl_copy.wait()
        rl = DL[bg * 8:(bg + 1) * 8, :]

        def lat_ends(j, state, rl=rl, bg=bg):
            p, pp, rest = state
            new = []
            for k in range(LEV):
                u, d, v, w = rest[k]
                d = rl * d + Z[at_lat(k, j, bg), :]
                u = rl * u + d
                new.append((u, d, v + pp * u, w + p * u))
            p = rl * p
            return (p, rl * pp + p, tuple(new))

        init = (one, one, tuple((zero, zero, zero, zero) for _ in range(LEV)))
        _, _, ends = lax.fori_loop(0, ROWS, lat_ends, init, unroll=4)
        for k in range(LEV):
            for val in range(4):
                SB[pl.ds((bg * NR + k * 8) * MSG + val, 8, stride=MSG), :] = ends[k][val]
        if bg == 0:
            neighbours = (lev > 0).astype(jnp.int32) + (lev < 3).astype(jnp.int32)
            pl.semaphore_wait(barrier, NR - 1 + neighbours)
        send(SB, RB, s1_sem, r1_sem, bg)

    m = float(ROWS)
    for bg in range(BG):
        ro = jnp.broadcast_to(DL[pl.ds(bg * 8 + lax.rem(me, 8), 1), :], (8, LANES))
        o0, o1, o2 = sums(ro * ro, 3, 4)
        own_powers = carry_powers(power(ro, 3, 4))
        get(SB, RB, s1_sem, r1_sem, bg)

        def rows_of(q, val, bg=bg):
            return pl.ds((bg * NR + q * 8) * MSG + val, 8, stride=MSG)

        def had(val):
            return [RB[rows_of(q, val), :] for q in range(NR // 8)]
        states = block_carries(had(0), had(1), own_powers, m, False)
        vs = [e + ro * (o1 * u + o2 * d) for e, (u, d) in zip(had(2), states)]
        ws = [e + ro * (o0 * u + o1 * d) for e, (u, d) in zip(had(3), states)]
        backs = block_carries(vs, ws, own_powers, m, True)
        for q in range(NR // 8):
            RP[rows_of(q, 0), :], RP[rows_of(q, 1), :] = states[q]
            RP[rows_of(q, 2), :], RP[rows_of(q, 3), :] = backs[q]
            for val in range(4, MSG):
                RP[rows_of(q, val), :] = zero
        send(RP, CB, s2_sem, r2_sem, bg)

    def lat_finish(bg):
        get(RP, CB, s2_sem, r2_sem, bg)
        rl = DL[pl.ds(pl.multiple_of(bg * 8, 8), 8), :]
        g_lat = gain_sq(rl)

        def come(k, val):
            return CB[pl.ds((bg * NR + k * 8) * MSG + val, 8, stride=MSG), :]

        def lat_ahead(i, state):
            xs = [[Z[at_lat(k, i * BLK + q, bg), :] for k in range(LEV)] for q in range(BLK)]
            state = list(state)
            for q in range(BLK):
                for k in range(LEV):
                    u, d = state[k]
                    d = rl * d + xs[q][k]
                    u = rl * u + d
                    state[k] = (u, d)
                    xs[q][k] = u
            for q in range(BLK):
                for k in range(LEV):
                    Z[at_lat(k, i * BLK + q, bg), :] = xs[q][k]
            return tuple(state)
        lax.fori_loop(0, ROWS // BLK, lat_ahead, tuple((come(k, 0), come(k, 1)) for k in range(LEV)))

        def lat_back(i, state):
            j0 = ROWS - BLK - i * BLK
            xs = [[Z[at_lat(k, j0 + q, bg), :] for k in range(LEV)] for q in range(BLK)]
            state = list(state)
            for q in range(BLK - 1, -1, -1):
                for k in range(LEV):
                    v, w = state[k]
                    w = rl * w + xs[q][k]
                    v = rl * v + w
                    state[k] = (v, w)
                    xs[q][k] = v * g_lat
            for q in range(BLK):
                for k in range(LEV):
                    Z[at_lat(k, j0 + q, bg), :] = xs[q][k]
            return tuple(state)
        lax.fori_loop(0, ROWS // BLK, lat_back, tuple((come(k, 2), come(k, 3)) for k in range(LEV)))

    loop(SEG, lambda b: pv_copy(b).wait())

    def chunk(ref, c):
        return ref.at[pl.ds(pl.multiple_of(c * CH, 8), CH), :]

    def right(c):
        return pltpu.make_async_remote_copy(
            src_ref=chunk(SR, c), dst_ref=chunk(FL, c), send_sem=sr_sem.at[c], recv_sem=fl_sem.at[c],
            device_id=(lax.rem(lev + 1, 4), me), device_id_type=MESH)

    def left(c):
        return pltpu.make_async_remote_copy(
            src_ref=chunk(SL, c), dst_ref=chunk(FR, c), send_sem=sl_sem.at[c], recv_sem=fr_sem.at[c],
            device_id=(lax.rem(lev + 3, 4), me), device_id_type=MESH)

    def each(c, body):
        bg = c // NJ
        j0 = lax.rem(c, NJ) * JC
        for jj in range(JC):
            j = j0 + jj
            rv = PV[pl.ds(bg * 8 * ROWS + j, 8, stride=ROWS), :]

            def at(val, jj=jj):
                return pl.ds(pl.multiple_of(c * CH + (val * JC + jj) * 8, 8), 8)

            def zat(k, j=j):
                return pl.ds(pl.multiple_of((k * ROWS + j) * SEG + bg * 8, 8), 8)

            def put(vals, rv=rv, j=j):
                gv = gain_sq(rv)
                for k in range(LEV):
                    X[pl.ds(bg * 8 * LINES + k * ROWS + j, 8, stride=LINES), :] = vals[k] * gv
            body(rv, at, zat, put)

    def ahead(rv, xs, u, d):
        us = []
        for x in xs:
            d = x if d is None else rv * d + x
            u = d if u is None else rv * u + d
            us.append(u)
        return us, u, d

    def back(rv, us, v, w):
        vs = [None] * LEV
        for k in range(LEV - 1, -1, -1):
            w = us[k] if w is None else rv * w + us[k]
            v = w if v is None else rv * v + w
            vs[k] = v
        return vs, v, w

    def four(q):
        return (1.0 + q * (1.0 + q * (1.0 + q)),
                1.0 + q * (2.0 + q * (3.0 + 4.0 * q)),
                1.0 + q * (4.0 + q * (9.0 + 16.0 * q)))

    def send_out(c):
        @pl.when(lax.rem(c, 2) == 1)
        def _():
            bg = c // NJ
            j0 = lax.rem(c - 1, NJ) * JC
            for k in range(LEV):
                for b in range(8):
                    at = pl.ds(pl.multiple_of((bg * 8 + b) * LINES + k * ROWS + j0, 8), 8)
                    out[pl.ds(pl.multiple_of(k * ROWS + j0, 8), 8),
                        pl.ds(pl.multiple_of((bg * 8 + b) * LANES, LANES), LANES)] = X[at, :]

    def ready(c):
        @pl.when(lax.rem(c, NJ) == 0)
        def _():
            lat_finish(c // NJ)

    @pl.when(lev == 0)
    def _():
        def first(c):
            ready(c)

            def body(rv, at, zat, put):
                us, u, d = ahead(rv, [Z[zat(k), :] for k in range(LEV)], None, None)
                for k in range(LEV):
                    Z[zat(k), :] = us[k]
                SR[at(0), :] = u
                SR[at(1), :] = d
            each(c, body)
            right(c).start()
        loop(NCH, first)

        def second(c):
            left(c).wait_recv()

            def body(rv, at, zat, put):
                vs, _, _ = back(rv, [Z[zat(k), :] for k in range(LEV)], FR[at(0), :], FR[at(1), :])
                put(vs)
            each(c, body)
            send_out(c)
        loop(NCH, second)
        loop(NCH, lambda c: right(c).wait_send())

    @pl.when(lev == 3)
    def _():
        def first(c):
            ready(c)

            def body(rv, at, zat, put):
                us, _, _ = ahead(rv, [Z[zat(k), :] for k in range(LEV)], None, None)
                _, v, w = back(rv, us, None, None)
                SL[at(0), :] = v
                SL[at(1), :] = w
            each(c, body)
            left(c).start()
        loop(NCH, first)

        def second(c):
            right(c).wait_recv()

            def body(rv, at, zat, put):
                us, _, _ = ahead(rv, [Z[zat(k), :] for k in range(LEV)], FL[at(0), :], FL[at(1), :])
                vs, _, _ = back(rv, us, None, None)
                put(vs)
            each(c, body)
            send_out(c)
        loop(NCH, second)
        loop(NCH, lambda c: left(c).wait_send())

    def staged(first, second):
        def step(i):
            @pl.when(i < NCH)
            def _():
                first(i)

            @pl.when(i >= LAG)
            def _():
                second(i - LAG)
        loop(NCH + LAG, step)
        loop(NCH, lambda c: right(c).wait_send())
        loop(NCH, lambda c: left(c).wait_send())

    @pl.when(lev == 1)
    def _():
        def first(c):
            ready(c)

            right(c).wait_recv()

            def body(rv, at, zat, put):
                us, u, d = ahead(rv, [Z[zat(k), :] for k in range(LEV)], FL[at(0), :], FL[at(1), :])
                for k in range(LEV):
                    Z[zat(k), :] = us[k]
                SR[at(0), :] = u
                SR[at(1), :] = d
            each(c, body)
            right(c).start()

        def second(c):
            left(c).wait_recv()

            def body(rv, at, zat, put):
                q = rv * rv
                q2 = q * q
                e0, e1, e2 = sums_double(q, 4.0, q2 * q2, *four(q))
                u, d = SR[at(0), :], SR[at(1), :]
                v = FR[at(0), :] + rv * (e1 * u + e2 * d)
                w = FR[at(1), :] + rv * (e0 * u + e1 * d)
                vs, v, w = back(rv, [Z[zat(k), :] for k in range(LEV)], v, w)
                SL[at(0), :] = v
                SL[at(1), :] = w
                put(vs)
            each(c, body)
            left(c).start()
            send_out(c)
        staged(first, second)

    @pl.when(lev == 2)
    def _():
        def first(c):
            ready(c)

            left(c).wait_recv()

            def body(rv, at, zat, put):
                us, u, d = ahead(rv, [Z[zat(k), :] for k in range(LEV)], None, None)
                e0, e1, e2 = four(rv * rv)
                v = FR[at(0), :] + rv * (e1 * u + e2 * d)
                w = FR[at(1), :] + rv * (e0 * u + e1 * d)
                _, v, w = back(rv, us, v, w)
                SL[at(0), :] = v
                SL[at(1), :] = w
            each(c, body)
            left(c).start()

        def second(c):
            right(c).wait_recv()

            def body(rv, at, zat, put):
                us, u, d = ahead(rv, [Z[zat(k), :] for k in range(LEV)], FL[at(0), :], FL[at(1), :])
                SR[at(0), :] = u
                SR[at(1), :] = d
                e0, e1, e2 = four(rv * rv)
                v = FR[at(0), :] + rv * (e1 * u + e2 * d)
                w = FR[at(1), :] + rv * (e0 * u + e1 * d)
                vs, _, _ = back(rv, us, v, w)
                put(vs)
            each(c, body)
            right(c).start()
            send_out(c)
        staged(first, second)

    for bg in range(BG):
        sent(SB, RB, s1_sem, r1_sem, bg)
        sent(RP, CB, s2_sem, r2_sem, bg)


def per_device(control, decay_lon, decay_lat, decay_vert):
    lines = control.reshape(LINES, SEG * LANES)
    hbm = pl.BlockSpec(memory_space=pltpu.HBM)
    vmem = pl.BlockSpec(memory_space=pltpu.VMEM)
    f32 = jnp.float32
    dma = pltpu.SemaphoreType.DMA
    filtered = pl.pallas_call(
        kernel,
        out_shape=jax.ShapeDtypeStruct((LINES, SEG * LANES), f32),
        in_specs=[hbm] * 4,
        out_specs=vmem,
        scratch_shapes=[
            pltpu.VMEM((SEG * LINES, LANES), f32),
            pltpu.VMEM((2 * LANES * SEG, LANES), f32),
            pltpu.VMEM((LINES * SEG, LANES), f32),
            pltpu.VMEM((SEG * ROWS, LANES), f32),
            pltpu.VMEM((1, ROWS), f32),
            pltpu.VMEM((SEG, LANES), f32),
        ] + [pltpu.VMEM((BG * NR * MSG, LANES), f32)] * 4
        + [pltpu.VMEM((NCH * CH, LANES), f32)] * 4
        + [dma((SEG,))] * 2 + [dma] * 2 + [dma((BG * NR,))] * 4 + [dma((NCH,))] * 4,
        compiler_params=pltpu.CompilerParams(
            collective_id=0, has_side_effects=True, vmem_limit_bytes=48 * 1024 * 1024),
        name="filters",
    )(lines, decay_lon.reshape(1, ROWS), decay_lat.reshape(SEG, LANES), decay_vert)
    return filtered.reshape(LEV, ROWS, SEG * LANES)


def solution(mesh):
    in_specs = (P("lev", "row", None), P("row"), P(), P("row", None))
    out_specs = P("lev", "row", None)
    return jax.shard_map(
        per_device, mesh=mesh, in_specs=in_specs, out_specs=out_specs, check_vma=False
    )
```

```python
import functools

import jax
import jax.numpy as jnp
from jax import lax
from jax.experimental import pallas as pl
from jax.experimental.pallas import tpu as pltpu
from jax.sharding import PartitionSpec as P

MESH = pl.DeviceIdType.MESH

LANES = 128
SEG = 24
ROWS = 48
LEV = 4
LINES = LEV * ROWS
BG = SEG // 8
NR = 32
MSG = 8
JC = 4
NJ = ROWS // JC
NCH = BG * NJ
CH = 2 * JC * 8
LAG = 6


def gain_sq(r):
    q = r * r
    a = (1.0 - r) * (1.0 + r)
    a2 = a * a
    a4 = a2 * a2
    return jnp.sqrt(a4 * a2 * a / (1.0 + q * (9.0 + q * (9.0 + q))))


def sums_double(q, n, qn, s0, s1, s2):
    return (
        s0 + qn * s0,
        s1 + qn * (s1 + n * s0),
        s2 + qn * (s2 + (2.0 * n) * s1 + (n * n) * s0),
    )


def sums(q, base, doublings):
    s0 = jnp.ones_like(q)
    s1 = jnp.ones_like(q)
    s2 = jnp.ones_like(q)
    qn = q
    for t in range(1, base):
        s0 = s0 + qn
        s1 = s1 + (t + 1.0) * qn
        s2 = s2 + ((t + 1.0) * (t + 1.0)) * qn
        qn = qn * q
    n = float(base)
    for _ in range(doublings):
        s0, s1, s2 = sums_double(q, n, qn, s0, s1, s2)
        qn = qn * qn
        n = 2.0 * n
    return s0, s1, s2


def power(r, base, doublings):
    p = r
    for _ in range(base - 1):
        p = p * r
    for _ in range(doublings):
        p = p * p
    return p


def sublanes():
    return lax.broadcasted_iota(jnp.int32, (8, LANES), 0)


def carry_powers(rn):
    one, two, four = rn, rn * rn, (rn * rn) * (rn * rn)

    def by(idx):
        p = jnp.where(idx % 2 == 1, one, 1.0)
        p = p * jnp.where((idx // 2) % 2 == 1, two, 1.0)
        return p * jnp.where(idx // 4 == 1, four, 1.0)
    return one, two, four, four * four, by(sublanes()), by(7 - sublanes())


def block_carries(us, ds, powers, n, rev):
    r1, r2, r4, r8, up, down = powers
    idx = 7 - sublanes() if rev else sublanes()
    along = down if rev else up
    far = (n * idx.astype(jnp.float32))

    def shifted(x, t):
        return jnp.where(idx >= t, pltpu.roll(x, 8 - t if rev else t, 0), 0.0)

    def last(x):
        row = x[0:1, :] if rev else x[7:8, :]
        return jnp.broadcast_to(row, (8, LANES))

    cu = jnp.zeros((8, LANES), jnp.float32)
    cd = cu
    out = [None] * len(us)
    order = range(len(us))
    for i in (reversed(order) if rev else order):
        u, d = us[i], ds[i]
        for t, rt in ((1, r1), (2, r2), (4, r4)):
            su, sd = shifted(u, t), shifted(d, t)
            u = u + rt * (su + (n * t) * sd)
            d = d + rt * sd
        out[i] = (shifted(u, 1) + along * (cu + far * cd), shifted(d, 1) + along * cd)
        cu, cd = r8 * (cu + (8.0 * n) * cd) + last(u), r8 * cd + last(d)
    return out


def kernel(ctrl, dlon, dlat, dvert, out, X, Y, Z, PV, DN, DL,
           SB, RB, RP, CB, SR, SL, FL, FR,
           in_sem, pv_sem, dn_sem, dl_sem, s1_sem, r1_sem, s2_sem, r2_sem,
           sr_sem, sl_sem, fl_sem, fr_sem):
    lev = lax.axis_index("lev")
    me = lax.axis_index("row")
    barrier = pltpu.get_barrier_semaphore()

    def in_copy(b):
        return pltpu.make_async_copy(
            ctrl.at[:, pl.ds(pl.multiple_of(b * LANES, LANES), LANES)],
            X.at[pl.ds(pl.multiple_of(b * LINES, 8), LINES), :], in_sem.at[b])

    def pv_copy(b):
        return pltpu.make_async_copy(
            dvert.at[:, pl.ds(pl.multiple_of(b * LANES, LANES), LANES)],
            PV.at[pl.ds(pl.multiple_of(b * ROWS, 8), ROWS), :], pv_sem.at[b])

    dn_copy = pltpu.make_async_copy(dlon, DN, dn_sem)
    dl_copy = pltpu.make_async_copy(dlat, DL, dl_sem)

    def loop(n, body, unroll=1):
        def step(i, carry):
            body(i)
            return carry
        lax.fori_loop(0, n, step, 0, unroll=unroll)

    dn_copy.start()
    loop(SEG, lambda b: in_copy(b).start())
    dl_copy.start()
    loop(SEG, lambda b: pv_copy(b).start())

    def greet(i):
        pl.semaphore_signal(barrier, inc=1, device_id=(lev, lax.rem(me + i + 1, NR)), device_id_type=MESH)
    loop(NR - 1, greet)

    @pl.when(lev > 0)
    def _():
        pl.semaphore_signal(barrier, inc=1, device_id=(lev - 1, me), device_id_type=MESH)

    @pl.when(lev < 3)
    def _():
        pl.semaphore_signal(barrier, inc=1, device_id=(lev + 1, me), device_id_type=MESH)

    zero = jnp.zeros((8, LANES), jnp.float32)
    one = jnp.ones((8, LANES), jnp.float32)
    rest = jnp.zeros((LANES - 96, LANES), jnp.float32)
    loop(BG * NR, lambda i: SB.__setitem__((pl.ds(pl.multiple_of(i * MSG, 8), 8), slice(None)), zero))

    def turn_in(i):
        for k in range(4):
            in_copy(4 * i + k).wait()
        for k in range(4):
            b = 4 * i + k
            for g in range(2):
                tile = X[pl.ds(pl.multiple_of(b * LINES + g * 96, 8), 96), :]
                Y[pl.ds(g * LANES * SEG + b, LANES, stride=SEG), :] = jnp.concatenate([tile, rest]).T
    loop(SEG // 4, turn_in)

    dn_copy.wait()
    line = DN[...]
    line = jnp.concatenate([line, line, line[:, :32]], axis=1)
    r = jnp.broadcast_to(line, (8, LANES))
    chains = [(g, bg) for g in range(2) for bg in range(BG)]
    BLK = 4

    def at_lon(g, bg, l):
        return pl.ds(pl.multiple_of((g * LANES + l) * SEG + bg * 8, 8), 8)

    def lon_ends(l, state):
        p, pp, rest = state
        new = []
        for i, (g, bg) in enumerate(chains):
            u, d, v, w = rest[i]
            d = r * d + Y[at_lon(g, bg, l), :]
            u = r * u + d
            new.append((u, d, v + pp * u, w + p * u))
        p = r * p
        return (p, r * pp + p, tuple(new))

    init = (one, one, tuple((zero, zero, zero, zero) for _ in chains))
    _, _, ends = lax.fori_loop(0, LANES, lon_ends, init, unroll=4)

    s0, s1, s2 = sums(r * r, 1, 7)
    lon_powers = carry_powers(power(r, 1, 7))
    n = float(LANES)
    ahead_in, back_in = {}, {}
    for g in range(2):
        of = [ends[g * BG + bg] for bg in range(BG)]
        states = block_carries([e[0] for e in of], [e[1] for e in of], lon_powers, n, False)
        vs = [e[2] + r * (s1 * u + s2 * d) for e, (u, d) in zip(of, states)]
        ws = [e[3] + r * (s0 * u + s1 * d) for e, (u, d) in zip(of, states)]
        backs = block_carries(vs, ws, lon_powers, n, True)
        for bg in range(BG):
            ahead_in[g, bg] = states[bg]
            back_in[g, bg] = backs[bg]

    def lon_ahead(i, state):
        l0 = i * BLK
        xs = [[Y[at_lon(g, bg, l0 + q), :] for g, bg in chains] for q in range(BLK)]
        state = list(state)
        for q in range(BLK):
            for k in range(len(chains)):
                u, d = state[k]
                d = r * d + xs[q][k]
                u = r * u + d
                state[k] = (u, d)
                xs[q][k] = u
        for q in range(BLK):
            for k, (g, bg) in enumerate(chains):
                Y[at_lon(g, bg, l0 + q), :] = xs[q][k]
        return tuple(state)

    lax.fori_loop(0, LANES // BLK, lon_ahead, tuple(ahead_in[ch] for ch in chains))

    g_lon = gain_sq(r)

    def at_lat(k, j, bg):
        return pl.ds(pl.multiple_of((k * ROWS + j) * SEG + bg * 8, 8), 8)

    def slot(ref, bg, i):
        return ref.at[pl.ds(pl.multiple_of((bg * NR + i) * MSG, 8), MSG), :]

    def message(src, dst, ssem, rsem, bg, p, at):
        return pltpu.make_async_remote_copy(
            src_ref=slot(src, bg, p), dst_ref=slot(dst, bg, at), send_sem=ssem.at[bg * NR + p],
            recv_sem=rsem.at[bg * NR + at], device_id=(lev, p), device_id_type=MESH)

    def send(src, dst, ssem, rsem, bg):
        def to(i):
            p = lax.rem(me + i + 1, NR)
            message(src, dst, ssem, rsem, bg, p, me).start()
        loop(NR - 1, to)
        at = pl.ds(pl.multiple_of((bg * NR + me) * MSG, 8), MSG)
        dst[at, :] = src[at, :]

    def get(src, dst, ssem, rsem, bg):
        def of(i):
            p = lax.rem(me + i + 1, NR)
            message(src, dst, ssem, rsem, bg, p, p).wait_recv()
        loop(NR - 1, of)

    def sent(src, dst, ssem, rsem, bg):
        def to(i):
            p = lax.rem(me + i + 1, NR)
            message(src, dst, ssem, rsem, bg, p, me).wait_send()
        loop(NR - 1, to)

    for bg in range(BG):
        def lon_back(i, state, bg=bg):
            l0 = LANES - BLK - i * BLK
            xs = [[Y[at_lon(g, bg, l0 + q), :] for g in range(2)] for q in range(BLK)]
            state = list(state)
            for q in range(BLK - 1, -1, -1):
                for g in range(2):
                    v, w = state[g]
                    w = r * w + xs[q][g]
                    v = r * v + w
                    state[g] = (v, w)
                    xs[q][g] = v * g_lon
            for q in range(BLK):
                for g in range(2):
                    Y[at_lon(g, bg, l0 + q), :] = xs[q][g]
            return tuple(state)

        lax.fori_loop(0, LANES // BLK, lon_back, (back_in[0, bg], back_in[1, bg]), unroll=2)

        def turn_out(i, bg=bg):
            for q in range(4):
                b = bg * 8 + i * 4 + q
                for g in range(2):
                    tile = Y[pl.ds(g * LANES * SEG + b, LANES, stride=SEG), :].T
                    for k in range(2):
                        Z[pl.ds((2 * g + k) * ROWS * SEG + b, ROWS, stride=SEG), :] = tile[k * ROWS:(k + 1) * ROWS, :]
        loop(2, turn_out)

        if bg == 0:
            dl_copy.wait()
        rl = DL[bg * 8:(bg + 1) * 8, :]

        def lat_ends(j, state, rl=rl, bg=bg):
            p, pp, rest = state
            new = []
            for k in range(LEV):
                u, d, v, w = rest[k]
                d = rl * d + Z[at_lat(k, j, bg), :]
                u = rl * u + d
                new.append((u, d, v + pp * u, w + p * u))
            p = rl * p
            return (p, rl * pp + p, tuple(new))

        init = (one, one, tuple((zero, zero, zero, zero) for _ in range(LEV)))
        _, _, ends = lax.fori_loop(0, ROWS, lat_ends, init, unroll=4)
        for k in range(LEV):
            for val in range(4):
                SB[pl.ds((bg * NR + k * 8) * MSG + val, 8, stride=MSG), :] = ends[k][val]
        if bg == 0:
            neighbours = (lev > 0).astype(jnp.int32) + (lev < 3).astype(jnp.int32)
            pl.semaphore_wait(barrier, NR - 1 + neighbours)
        send(SB, RB, s1_sem, r1_sem, bg)

    m = float(ROWS)
    for bg in range(BG):
        ro = jnp.broadcast_to(DL[pl.ds(bg * 8 + lax.rem(me, 8), 1), :], (8, LANES))
        o0, o1, o2 = sums(ro * ro, 3, 4)
        own_powers = carry_powers(power(ro, 3, 4))
        get(SB, RB, s1_sem, r1_sem, bg)

        def rows_of(q, val, bg=bg):
            return pl.ds((bg * NR + q * 8) * MSG + val, 8, stride=MSG)

        def had(val):
            return [RB[rows_of(q, val), :] for q in range(NR // 8)]
        states = block_carries(had(0), had(1), own_powers, m, False)
        vs = [e + ro * (o1 * u + o2 * d) for e, (u, d) in zip(had(2), states)]
        ws = [e + ro * (o0 * u + o1 * d) for e, (u, d) in zip(had(3), states)]
        backs = block_carries(vs, ws, own_powers, m, True)
        for q in range(NR // 8):
            RP[rows_of(q, 0), :], RP[rows_of(q, 1), :] = states[q]
            RP[rows_of(q, 2), :], RP[rows_of(q, 3), :] = backs[q]
            for val in range(4, MSG):
                RP[rows_of(q, val), :] = zero
        send(RP, CB, s2_sem, r2_sem, bg)

    def lat_finish(bg):
        get(RP, CB, s2_sem, r2_sem, bg)
        rl = DL[pl.ds(pl.multiple_of(bg * 8, 8), 8), :]
        g_lat = gain_sq(rl)

        def come(k, val):
            return CB[pl.ds((bg * NR + k * 8) * MSG + val, 8, stride=MSG), :]

        def lat_ahead(i, state):
            xs = [[Z[at_lat(k, i * BLK + q, bg), :] for k in range(LEV)] for q in range(BLK)]
            state = list(state)
            for q in range(BLK):
                for k in range(LEV):
                    u, d = state[k]
                    d = rl * d + xs[q][k]
                    u = rl * u + d
                    state[k] = (u, d)
                    xs[q][k] = u
            for q in range(BLK):
                for k in range(LEV):
                    Z[at_lat(k, i * BLK + q, bg), :] = xs[q][k]
            return tuple(state)
        lax.fori_loop(0, ROWS // BLK, lat_ahead, tuple((come(k, 0), come(k, 1)) for k in range(LEV)))

        def lat_back(i, state):
            j0 = ROWS - BLK - i * BLK
            xs = [[Z[at_lat(k, j0 + q, bg), :] for k in range(LEV)] for q in range(BLK)]
            state = list(state)
            for q in range(BLK - 1, -1, -1):
                for k in range(LEV):
                    v, w = state[k]
                    w = rl * w + xs[q][k]
                    v = rl * v + w
                    state[k] = (v, w)
                    xs[q][k] = v * g_lat
            for q in range(BLK):
                for k in range(LEV):
                    Z[at_lat(k, j0 + q, bg), :] = xs[q][k]
            return tuple(state)
        lax.fori_loop(0, ROWS // BLK, lat_back, tuple((come(k, 2), come(k, 3)) for k in range(LEV)))

    loop(SEG, lambda b: pv_copy(b).wait())

    def chunk(ref, c):
        return ref.at[pl.ds(pl.multiple_of(c * CH, 8), CH), :]

    def right(c):
        return pltpu.make_async_remote_copy(
            src_ref=chunk(SR, c), dst_ref=chunk(FL, c), send_sem=sr_sem.at[c], recv_sem=fl_sem.at[c],
            device_id=(lax.rem(lev + 1, 4), me), device_id_type=MESH)

    def left(c):
        return pltpu.make_async_remote_copy(
            src_ref=chunk(SL, c), dst_ref=chunk(FR, c), send_sem=sl_sem.at[c], recv_sem=fr_sem.at[c],
            device_id=(lax.rem(lev + 3, 4), me), device_id_type=MESH)

    def each(c, body):
        bg = c // NJ
        j0 = lax.rem(c, NJ) * JC
        for jj in range(JC):
            j = j0 + jj
            rv = PV[pl.ds(bg * 8 * ROWS + j, 8, stride=ROWS), :]

            def at(val, jj=jj):
                return pl.ds(pl.multiple_of(c * CH + (val * JC + jj) * 8, 8), 8)

            def zat(k, j=j):
                return pl.ds(pl.multiple_of((k * ROWS + j) * SEG + bg * 8, 8), 8)

            def put(vals, rv=rv, j=j):
                gv = gain_sq(rv)
                for k in range(LEV):
                    X[pl.ds(bg * 8 * LINES + k * ROWS + j, 8, stride=LINES), :] = vals[k] * gv
            body(rv, at, zat, put)

    def ahead(rv, xs, u, d):
        us = []
        for x in xs:
            d = x if d is None else rv * d + x
            u = d if u is None else rv * u + d
            us.append(u)
        return us, u, d

    def back(rv, us, v, w):
        vs = [None] * LEV
        for k in range(LEV - 1, -1, -1):
            w = us[k] if w is None else rv * w + us[k]
            v = w if v is None else rv * v + w
            vs[k] = v
        return vs, v, w

    def four(q):
        return (1.0 + q * (1.0 + q * (1.0 + q)),
                1.0 + q * (2.0 + q * (3.0 + 4.0 * q)),
                1.0 + q * (4.0 + q * (9.0 + 16.0 * q)))

    def send_out(c):
        @pl.when(lax.rem(c, 2) == 1)
        def _():
            bg = c // NJ
            j0 = lax.rem(c - 1, NJ) * JC
            for k in range(LEV):
                for b in range(8):
                    at = pl.ds(pl.multiple_of((bg * 8 + b) * LINES + k * ROWS + j0, 8), 8)
                    out[pl.ds(pl.multiple_of(k * ROWS + j0, 8), 8),
                        pl.ds(pl.multiple_of((bg * 8 + b) * LANES, LANES), LANES)] = X[at, :]

    def ready(c):
        @pl.when(lax.rem(c, NJ) == 0)
        def _():
            lat_finish(c // NJ)

    @pl.when(lev == 0)
    def _():
        def first(c):
            ready(c)

            def body(rv, at, zat, put):
                us, u, d = ahead(rv, [Z[zat(k), :] for k in range(LEV)], None, None)
                for k in range(LEV):
                    Z[zat(k), :] = us[k]
                SR[at(0), :] = u
                SR[at(1), :] = d
            each(c, body)
            right(c).start()
        loop(NCH, first)

        def second(c):
            left(c).wait_recv()

            def body(rv, at, zat, put):
                vs, _, _ = back(rv, [Z[zat(k), :] for k in range(LEV)], FR[at(0), :], FR[at(1), :])
                put(vs)
            each(c, body)
            send_out(c)
        loop(NCH, second)
        loop(NCH, lambda c: right(c).wait_send())

    @pl.when(lev == 3)
    def _():
        def first(c):
            ready(c)

            def body(rv, at, zat, put):
                us, _, _ = ahead(rv, [Z[zat(k), :] for k in range(LEV)], None, None)
                _, v, w = back(rv, us, None, None)
                SL[at(0), :] = v
                SL[at(1), :] = w
            each(c, body)
            left(c).start()
        loop(NCH, first)

        def second(c):
            right(c).wait_recv()

            def body(rv, at, zat, put):
                us, _, _ = ahead(rv, [Z[zat(k), :] for k in range(LEV)], FL[at(0), :], FL[at(1), :])
                vs, _, _ = back(rv, us, None, None)
                put(vs)
            each(c, body)
            send_out(c)
        loop(NCH, second)
        loop(NCH, lambda c: left(c).wait_send())

    def staged(first, second):
        def step(i):
            @pl.when(i < NCH)
            def _():
                first(i)

            @pl.when(i >= LAG)
            def _():
                second(i - LAG)
        loop(NCH + LAG, step)
        loop(NCH, lambda c: right(c).wait_send())
        loop(NCH, lambda c: left(c).wait_send())

    @pl.when(lev == 1)
    def _():
        def first(c):
            ready(c)

            right(c).wait_recv()

            def body(rv, at, zat, put):
                us, u, d = ahead(rv, [Z[zat(k), :] for k in range(LEV)], FL[at(0), :], FL[at(1), :])
                for k in range(LEV):
                    Z[zat(k), :] = us[k]
                SR[at(0), :] = u
                SR[at(1), :] = d
            each(c, body)
            right(c).start()

        def second(c):
            left(c).wait_recv()

            def body(rv, at, zat, put):
                q = rv * rv
                q2 = q * q
                e0, e1, e2 = sums_double(q, 4.0, q2 * q2, *four(q))
                u, d = SR[at(0), :], SR[at(1), :]
                v = FR[at(0), :] + rv * (e1 * u + e2 * d)
                w = FR[at(1), :] + rv * (e0 * u + e1 * d)
                vs, v, w = back(rv, [Z[zat(k), :] for k in range(LEV)], v, w)
                SL[at(0), :] = v
                SL[at(1), :] = w
                put(vs)
            each(c, body)
            left(c).start()
            send_out(c)
        staged(first, second)

    @pl.when(lev == 2)
    def _():
        def first(c):
            ready(c)

            left(c).wait_recv()

            def body(rv, at, zat, put):
                us, u, d = ahead(rv, [Z[zat(k), :] for k in range(LEV)], None, None)
                e0, e1, e2 = four(rv * rv)
                v = FR[at(0), :] + rv * (e1 * u + e2 * d)
                w = FR[at(1), :] + rv * (e0 * u + e1 * d)
                _, v, w = back(rv, us, v, w)
                SL[at(0), :] = v
                SL[at(1), :] = w
            each(c, body)
            left(c).start()

        def second(c):
            right(c).wait_recv()

            def body(rv, at, zat, put):
                us, u, d = ahead(rv, [Z[zat(k), :] for k in range(LEV)], FL[at(0), :], FL[at(1), :])
                SR[at(0), :] = u
                SR[at(1), :] = d
                e0, e1, e2 = four(rv * rv)
                v = FR[at(0), :] + rv * (e1 * u + e2 * d)
                w = FR[at(1), :] + rv * (e0 * u + e1 * d)
                vs, _, _ = back(rv, us, v, w)
                put(vs)
            each(c, body)
            right(c).start()
            send_out(c)
        staged(first, second)

    for bg in range(BG):
        sent(SB, RB, s1_sem, r1_sem, bg)
        sent(RP, CB, s2_sem, r2_sem, bg)


def per_device(control, decay_lon, decay_lat, decay_vert):
    lines = control.reshape(LINES, SEG * LANES)
    hbm = pl.BlockSpec(memory_space=pltpu.HBM)
    vmem = pl.BlockSpec(memory_space=pltpu.VMEM)
    f32 = jnp.float32
    dma = pltpu.SemaphoreType.DMA
    filtered = pl.pallas_call(
        kernel,
        out_shape=jax.ShapeDtypeStruct((LINES, SEG * LANES), f32),
        in_specs=[hbm] * 4,
        out_specs=vmem,
        scratch_shapes=[
            pltpu.VMEM((SEG * LINES, LANES), f32),
            pltpu.VMEM((2 * LANES * SEG, LANES), f32),
            pltpu.VMEM((LINES * SEG, LANES), f32),
            pltpu.VMEM((SEG * ROWS, LANES), f32),
            pltpu.VMEM((1, ROWS), f32),
            pltpu.VMEM((SEG, LANES), f32),
        ] + [pltpu.VMEM((BG * NR * MSG, LANES), f32)] * 4
        + [pltpu.VMEM((NCH * CH, LANES), f32)] * 4
        + [dma((SEG,))] * 2 + [dma] * 2 + [dma((BG * NR,))] * 4 + [dma((NCH,))] * 4,
        compiler_params=pltpu.CompilerParams(
            collective_id=0, has_side_effects=True, vmem_limit_bytes=50 * 1024 * 1024),
        name="filters",
    )(*[pltpu.with_memory_space_constraint(x, pltpu.HBM) for x in (lines, decay_lon.reshape(1, ROWS), decay_lat.reshape(SEG, LANES), decay_vert)])
    return filtered.reshape(LEV, ROWS, SEG * LANES)


def solution(mesh):
    in_specs = (P("lev", "row", None), P("row"), P(), P("row", None))
    out_specs = P("lev", "row", None)
    return jax.shard_map(
        per_device, mesh=mesh, in_specs=in_specs, out_specs=out_specs, check_vma=False
    )
```

```python
import functools

import jax
import jax.numpy as jnp
from jax import lax
from jax.experimental import pallas as pl
from jax.experimental.pallas import tpu as pltpu
from jax.sharding import PartitionSpec as P

MESH = pl.DeviceIdType.MESH

LANES = 128
SEG = 24
ROWS = 48
LEV = 4
LINES = LEV * ROWS
BG = SEG // 8
NR = 32
MSG = 8
JC = 4
NJ = ROWS // JC
NCH = BG * NJ
CH = 2 * JC * 8
LAG = 6
IN = 48


def gain_sq(r):
    q = r * r
    a = (1.0 - r) * (1.0 + r)
    a2 = a * a
    a4 = a2 * a2
    return jnp.sqrt(a4 * a2 * a / (1.0 + q * (9.0 + q * (9.0 + q))))


def sums_double(q, n, qn, s0, s1, s2):
    return (
        s0 + qn * s0,
        s1 + qn * (s1 + n * s0),
        s2 + qn * (s2 + (2.0 * n) * s1 + (n * n) * s0),
    )


def sums(q, base, doublings):
    s0 = jnp.ones_like(q)
    s1 = jnp.ones_like(q)
    s2 = jnp.ones_like(q)
    qn = q
    for t in range(1, base):
        s0 = s0 + qn
        s1 = s1 + (t + 1.0) * qn
        s2 = s2 + ((t + 1.0) * (t + 1.0)) * qn
        qn = qn * q
    n = float(base)
    for _ in range(doublings):
        s0, s1, s2 = sums_double(q, n, qn, s0, s1, s2)
        qn = qn * qn
        n = 2.0 * n
    return s0, s1, s2


def power(r, base, doublings):
    p = r
    for _ in range(base - 1):
        p = p * r
    for _ in range(doublings):
        p = p * p
    return p


def sublanes():
    return lax.broadcasted_iota(jnp.int32, (8, LANES), 0)


def carry_powers(rn):
    one, two, four = rn, rn * rn, (rn * rn) * (rn * rn)

    def by(idx):
        p = jnp.where(idx % 2 == 1, one, 1.0)
        p = p * jnp.where((idx // 2) % 2 == 1, two, 1.0)
        return p * jnp.where(idx // 4 == 1, four, 1.0)
    return one, two, four, four * four, by(sublanes()), by(7 - sublanes())


def block_carries(us, ds, powers, n, rev):
    r1, r2, r4, r8, up, down = powers
    idx = 7 - sublanes() if rev else sublanes()
    along = down if rev else up
    far = (n * idx.astype(jnp.float32))

    def shifted(x, t):
        return jnp.where(idx >= t, pltpu.roll(x, 8 - t if rev else t, 0), 0.0)

    def last(x):
        row = x[0:1, :] if rev else x[7:8, :]
        return jnp.broadcast_to(row, (8, LANES))

    cu = jnp.zeros((8, LANES), jnp.float32)
    cd = cu
    out = [None] * len(us)
    order = range(len(us))
    for i in (reversed(order) if rev else order):
        u, d = us[i], ds[i]
        for t, rt in ((1, r1), (2, r2), (4, r4)):
            su, sd = shifted(u, t), shifted(d, t)
            u = u + rt * (su + (n * t) * sd)
            d = d + rt * sd
        out[i] = (shifted(u, 1) + along * (cu + far * cd), shifted(d, 1) + along * cd)
        cu, cd = r8 * (cu + (8.0 * n) * cd) + last(u), r8 * cd + last(d)
    return out


def kernel(ctrl, dlon, dlat, dvert, out, X, Y, Z, PI, PV, OS, DN, DL,
           SB, RB, RP, CB, SR, SL, FL, FR,
           in_sem, pv_sem, dn_sem, dl_sem, s1_sem, r1_sem, s2_sem, r2_sem,
           sr_sem, sl_sem, fl_sem, fr_sem):
    lev = lax.axis_index("lev")
    me = lax.axis_index("row")
    barrier = pltpu.get_barrier_semaphore()

    def in_copy(i):
        at = pl.ds(pl.multiple_of(i * IN, 8), IN)
        return pltpu.make_async_copy(ctrl.at[at, :], X.at[at, :], in_sem.at[i])

    pv_copy = pltpu.make_async_copy(dvert, PI, pv_sem)
    dn_copy = pltpu.make_async_copy(dlon, DN, dn_sem)
    dl_copy = pltpu.make_async_copy(dlat, DL, dl_sem)

    def loop(n, body, unroll=1):
        def step(i, carry):
            body(i)
            return carry
        lax.fori_loop(0, n, step, 0, unroll=unroll)

    dn_copy.start()
    for i in range(LINES // IN):
        in_copy(i).start()
    dl_copy.start()
    pv_copy.start()

    def greet(i):
        pl.semaphore_signal(barrier, inc=1, device_id=(lev, lax.rem(me + i + 1, NR)), device_id_type=MESH)
    loop(NR - 1, greet)

    @pl.when(lev > 0)
    def _():
        pl.semaphore_signal(barrier, inc=1, device_id=(lev - 1, me), device_id_type=MESH)

    @pl.when(lev < 3)
    def _():
        pl.semaphore_signal(barrier, inc=1, device_id=(lev + 1, me), device_id_type=MESH)

    zero = jnp.zeros((8, LANES), jnp.float32)
    one = jnp.ones((8, LANES), jnp.float32)
    rest = jnp.zeros((LANES - 96, LANES), jnp.float32)
    loop(BG * NR, lambda i: SB.__setitem__((pl.ds(pl.multiple_of(i * MSG, 8), 8), slice(None)), zero))

    for g in range(2):
        for i in range(96 // IN):
            in_copy(g * (96 // IN) + i).wait()

        def turn_in(i, g=g):
            for k in range(8):
                b = 8 * i + k
                tile = X[pl.ds(g * 96, 96), pl.ds(pl.multiple_of(b * LANES, LANES), LANES)]
                Y[pl.ds(g * LANES * SEG + b, LANES, stride=SEG), :] = jnp.concatenate([tile, rest]).T
        loop(SEG // 8, turn_in)

    dn_copy.wait()
    line = DN[...]
    line = jnp.concatenate([line, line, line[:, :32]], axis=1)
    r = jnp.broadcast_to(line, (8, LANES))
    chains = [(g, bg) for g in range(2) for bg in range(BG)]
    BLK = 4

    def at_lon(g, bg, l):
        return pl.ds(pl.multiple_of((g * LANES + l) * SEG + bg * 8, 8), 8)

    def lon_ends(l, state):
        p, pp, rest = state
        new = []
        for i, (g, bg) in enumerate(chains):
            u, d, v, w = rest[i]
            d = r * d + Y[at_lon(g, bg, l), :]
            u = r * u + d
            new.append((u, d, v + pp * u, w + p * u))
        p = r * p
        return (p, r * pp + p, tuple(new))

    init = (one, one, tuple((zero, zero, zero, zero) for _ in chains))
    _, _, ends = lax.fori_loop(0, LANES, lon_ends, init, unroll=4)

    s0, s1, s2 = sums(r * r, 1, 7)
    lon_powers = carry_powers(power(r, 1, 7))
    n = float(LANES)
    ahead_in, back_in = {}, {}
    for g in range(2):
        of = [ends[g * BG + bg] for bg in range(BG)]
        states = block_carries([e[0] for e in of], [e[1] for e in of], lon_powers, n, False)
        vs = [e[2] + r * (s1 * u + s2 * d) for e, (u, d) in zip(of, states)]
        ws = [e[3] + r * (s0 * u + s1 * d) for e, (u, d) in zip(of, states)]
        backs = block_carries(vs, ws, lon_powers, n, True)
        for bg in range(BG):
            ahead_in[g, bg] = states[bg]
            back_in[g, bg] = backs[bg]

    def lon_ahead(i, state):
        l0 = i * BLK
        xs = [[Y[at_lon(g, bg, l0 + q), :] for g, bg in chains] for q in range(BLK)]
        state = list(state)
        for q in range(BLK):
            for k in range(len(chains)):
                u, d = state[k]
                d = r * d + xs[q][k]
                u = r * u + d
                state[k] = (u, d)
                xs[q][k] = u
        for q in range(BLK):
            for k, (g, bg) in enumerate(chains):
                Y[at_lon(g, bg, l0 + q), :] = xs[q][k]
        return tuple(state)

    lax.fori_loop(0, LANES // BLK, lon_ahead, tuple(ahead_in[ch] for ch in chains))

    g_lon = gain_sq(r)

    def at_lat(k, j, bg):
        return pl.ds(pl.multiple_of((k * ROWS + j) * SEG + bg * 8, 8), 8)

    def slot(ref, bg, i):
        return ref.at[pl.ds(pl.multiple_of((bg * NR + i) * MSG, 8), MSG), :]

    def send(src, dst, ssem, rsem, bg):
        def to(i):
            p = lax.rem(me + i + 1, NR)
            pltpu.make_async_remote_copy(
                src_ref=slot(src, bg, p), dst_ref=slot(dst, bg, me), send_sem=ssem.at[bg],
                recv_sem=rsem.at[bg], device_id=(lev, p), device_id_type=MESH).start()
        loop(NR - 1, to)
        at = pl.ds(pl.multiple_of((bg * NR + me) * MSG, 8), MSG)
        dst[at, :] = src[at, :]

    def all_of(src, dst, ssem, rsem, bg):
        at = pl.ds(pl.multiple_of(bg * NR * MSG, 8), (NR - 1) * MSG)
        return pltpu.make_async_remote_copy(
            src_ref=src.at[at, :], dst_ref=dst.at[at, :], send_sem=ssem.at[bg], recv_sem=rsem.at[bg],
            device_id=(lev, lax.rem(me + 1, NR)), device_id_type=MESH)

    for bg in range(BG):
        def lon_back(i, state, bg=bg):
            l0 = LANES - BLK - i * BLK
            xs = [[Y[at_lon(g, bg, l0 + q), :] for g in range(2)] for q in range(BLK)]
            state = list(state)
            for q in range(BLK - 1, -1, -1):
                for g in range(2):
                    v, w = state[g]
                    w = r * w + xs[q][g]
                    v = r * v + w
                    state[g] = (v, w)
                    xs[q][g] = v * g_lon
            for q in range(BLK):
                for g in range(2):
                    Y[at_lon(g, bg, l0 + q), :] = xs[q][g]
            return tuple(state)

        lax.fori_loop(0, LANES // BLK, lon_back, (back_in[0, bg], back_in[1, bg]), unroll=2)

        def turn_out(i, bg=bg):
            for q in range(4):
                b = bg * 8 + i * 4 + q
                for g in range(2):
                    tile = Y[pl.ds(g * LANES * SEG + b, LANES, stride=SEG), :].T
                    for k in range(2):
                        Z[pl.ds((2 * g + k) * ROWS * SEG + b, ROWS, stride=SEG), :] = tile[k * ROWS:(k + 1) * ROWS, :]
        loop(2, turn_out)

        if bg == 0:
            dl_copy.wait()
        rl = DL[bg * 8:(bg + 1) * 8, :]

        def lat_ends(j, state, rl=rl, bg=bg):
            p, pp, rest = state
            new = []
            for k in range(LEV):
                u, d, v, w = rest[k]
                d = rl * d + Z[at_lat(k, j, bg), :]
                u = rl * u + d
                new.append((u, d, v + pp * u, w + p * u))
            p = rl * p
            return (p, rl * pp + p, tuple(new))

        init = (one, one, tuple((zero, zero, zero, zero) for _ in range(LEV)))
        _, _, ends = lax.fori_loop(0, ROWS, lat_ends, init, unroll=4)
        for k in range(LEV):
            for val in range(4):
                SB[pl.ds((bg * NR + k * 8) * MSG + val, 8, stride=MSG), :] = ends[k][val]
        if bg == 0:
            neighbours = (lev > 0).astype(jnp.int32) + (lev < 3).astype(jnp.int32)
            pl.semaphore_wait(barrier, NR - 1 + neighbours)
        send(SB, RB, s1_sem, r1_sem, bg)

    pv_copy.wait()

    def place(b):
        for q in range(ROWS // 8):
            PV[pl.ds(pl.multiple_of(b * ROWS + q * 8, 8), 8), :] = PI[
                q * 8:(q + 1) * 8, pl.ds(pl.multiple_of(b * LANES, LANES), LANES)]
    loop(SEG, place, unroll=2)

    m = float(ROWS)
    for bg in range(BG):
        ro = jnp.broadcast_to(DL[pl.ds(bg * 8 + lax.rem(me, 8), 1), :], (8, LANES))
        o0, o1, o2 = sums(ro * ro, 3, 4)
        own_powers = carry_powers(power(ro, 3, 4))
        all_of(SB, RB, s1_sem, r1_sem, bg).wait_recv()

        def rows_of(q, val, bg=bg):
            return pl.ds((bg * NR + q * 8) * MSG + val, 8, stride=MSG)

        def had(val):
            return [RB[rows_of(q, val), :] for q in range(NR // 8)]
        states = block_carries(had(0), had(1), own_powers, m, False)
        vs = [e + ro * (o1 * u + o2 * d) for e, (u, d) in zip(had(2), states)]
        ws = [e + ro * (o0 * u + o1 * d) for e, (u, d) in zip(had(3), states)]
        backs = block_carries(vs, ws, own_powers, m, True)
        for q in range(NR // 8):
            RP[rows_of(q, 0), :], RP[rows_of(q, 1), :] = states[q]
            RP[rows_of(q, 2), :], RP[rows_of(q, 3), :] = backs[q]
            for val in range(4, MSG):
                RP[rows_of(q, val), :] = zero
        send(RP, CB, s2_sem, r2_sem, bg)

    def lat_finish(bg):
        all_of(RP, CB, s2_sem, r2_sem, bg).wait_recv()
        rl = DL[pl.ds(pl.multiple_of(bg * 8, 8), 8), :]
        g_lat = gain_sq(rl)

        def come(k, val):
            return CB[pl.ds((bg * NR + k * 8) * MSG + val, 8, stride=MSG), :]

        def lat_ahead(i, state):
            xs = [[Z[at_lat(k, i * BLK + q, bg), :] for k in range(LEV)] for q in range(BLK)]
            state = list(state)
            for q in range(BLK):
                for k in range(LEV):
                    u, d = state[k]
                    d = rl * d + xs[q][k]
                    u = rl * u + d
                    state[k] = (u, d)
                    xs[q][k] = u
            for q in range(BLK):
                for k in range(LEV):
                    Z[at_lat(k, i * BLK + q, bg), :] = xs[q][k]
            return tuple(state)
        lax.fori_loop(0, ROWS // BLK, lat_ahead, tuple((come(k, 0), come(k, 1)) for k in range(LEV)))

        def lat_back(i, state):
            j0 = ROWS - BLK - i * BLK
            xs = [[Z[at_lat(k, j0 + q, bg), :] for k in range(LEV)] for q in range(BLK)]
            state = list(state)
            for q in range(BLK - 1, -1, -1):
                for k in range(LEV):
                    v, w = state[k]
                    w = rl * w + xs[q][k]
                    v = rl * v + w
                    state[k] = (v, w)
                    xs[q][k] = v * g_lat
            for q in range(BLK):
                for k in range(LEV):
                    Z[at_lat(k, j0 + q, bg), :] = xs[q][k]
            return tuple(state)
        lax.fori_loop(0, ROWS // BLK, lat_back, tuple((come(k, 2), come(k, 3)) for k in range(LEV)))


    def chunk(ref, c):
        return ref if c is None else ref.at[pl.ds(pl.multiple_of(c * CH, 8), CH), :]

    def one_of(sem, c):
        return sem.at[0 if c is None else c]

    def right(c):
        return pltpu.make_async_remote_copy(
            src_ref=chunk(SR, c), dst_ref=chunk(FL, c), send_sem=sr_sem, recv_sem=one_of(fl_sem, c),
            device_id=(lax.rem(lev + 1, 4), me), device_id_type=MESH)

    def left(c):
        return pltpu.make_async_remote_copy(
            src_ref=chunk(SL, c), dst_ref=chunk(FR, c), send_sem=sl_sem, recv_sem=one_of(fr_sem, c),
            device_id=(lax.rem(lev + 3, 4), me), device_id_type=MESH)

    def each(c, body):
        bg = c // NJ
        j0 = lax.rem(c, NJ) * JC
        for jj in range(JC):
            j = j0 + jj
            rv = PV[pl.ds(bg * 8 * ROWS + j, 8, stride=ROWS), :]

            def at(val, jj=jj):
                return pl.ds(pl.multiple_of(c * CH + (val * JC + jj) * 8, 8), 8)

            def zat(k, j=j):
                return pl.ds(pl.multiple_of((k * ROWS + j) * SEG + bg * 8, 8), 8)

            def put(vals, rv=rv, j=j):
                gv = gain_sq(rv)
                for k in range(LEV):
                    OS[pl.ds(k * 8 + lax.rem(j, 8), 8, stride=LEV * 8), :] = vals[k] * gv
            body(rv, at, zat, put)

    def ahead(rv, xs, u, d):
        us = []
        for x in xs:
            d = x if d is None else rv * d + x
            u = d if u is None else rv * u + d
            us.append(u)
        return us, u, d

    def back(rv, us, v, w):
        vs = [None] * LEV
        for k in range(LEV - 1, -1, -1):
            w = us[k] if w is None else rv * w + us[k]
            v = w if v is None else rv * v + w
            vs[k] = v
        return vs, v, w

    def four(q):
        return (1.0 + q * (1.0 + q * (1.0 + q)),
                1.0 + q * (2.0 + q * (3.0 + 4.0 * q)),
                1.0 + q * (4.0 + q * (9.0 + 16.0 * q)))

    def send_out(c):
        @pl.when(lax.rem(c, 2) == 1)
        def _():
            bg = c // NJ
            j0 = lax.rem(c - 1, NJ) * JC
            for k in range(LEV):
                for b in range(8):
                    out[pl.ds(pl.multiple_of(k * ROWS + j0, 8), 8),
                        pl.ds(pl.multiple_of((bg * 8 + b) * LANES, LANES), LANES)] = OS[
                            (b * LEV + k) * 8:(b * LEV + k + 1) * 8, :]

    def ready(c):
        @pl.when(lax.rem(c, NJ) == 0)
        def _():
            lat_finish(c // NJ)

    @pl.when(lev == 0)
    def _():
        def first(c):
            ready(c)

            def body(rv, at, zat, put):
                us, u, d = ahead(rv, [Z[zat(k), :] for k in range(LEV)], None, None)
                for k in range(LEV):
                    Z[zat(k), :] = us[k]
                SR[at(0), :] = u
                SR[at(1), :] = d
            each(c, body)
            right(c).start()
        loop(NCH, first)

        def second(c):
            left(c).wait_recv()

            def body(rv, at, zat, put):
                vs, _, _ = back(rv, [Z[zat(k), :] for k in range(LEV)], FR[at(0), :], FR[at(1), :])
                put(vs)
            each(c, body)
            send_out(c)
        loop(NCH, second)
        right(None).wait_send()

    @pl.when(lev == 3)
    def _():
        def first(c):
            ready(c)

            def body(rv, at, zat, put):
                us, _, _ = ahead(rv, [Z[zat(k), :] for k in range(LEV)], None, None)
                _, v, w = back(rv, us, None, None)
                SL[at(0), :] = v
                SL[at(1), :] = w
            each(c, body)
            left(c).start()
        loop(NCH, first)

        def second(c):
            right(c).wait_recv()

            def body(rv, at, zat, put):
                us, _, _ = ahead(rv, [Z[zat(k), :] for k in range(LEV)], FL[at(0), :], FL[at(1), :])
                vs, _, _ = back(rv, us, None, None)
                put(vs)
            each(c, body)
            send_out(c)
        loop(NCH, second)
        left(None).wait_send()

    def staged(first, second):
        def step(i):
            @pl.when(i < NCH)
            def _():
                first(i)

            @pl.when(i >= LAG)
            def _():
                second(i - LAG)
        loop(NCH + LAG, step)
        right(None).wait_send()
        left(None).wait_send()

    @pl.when(lev == 1)
    def _():
        def first(c):
            ready(c)

            right(c).wait_recv()

            def body(rv, at, zat, put):
                us, u, d = ahead(rv, [Z[zat(k), :] for k in range(LEV)], FL[at(0), :], FL[at(1), :])
                for k in range(LEV):
                    Z[zat(k), :] = us[k]
                SR[at(0), :] = u
                SR[at(1), :] = d
            each(c, body)
            right(c).start()

        def second(c):
            left(c).wait_recv()

            def body(rv, at, zat, put):
                q = rv * rv
                q2 = q * q
                e0, e1, e2 = sums_double(q, 4.0, q2 * q2, *four(q))
                u, d = SR[at(0), :], SR[at(1), :]
                v = FR[at(0), :] + rv * (e1 * u + e2 * d)
                w = FR[at(1), :] + rv * (e0 * u + e1 * d)
                vs, v, w = back(rv, [Z[zat(k), :] for k in range(LEV)], v, w)
                SL[at(0), :] = v
                SL[at(1), :] = w
                put(vs)
            each(c, body)
            left(c).start()
            send_out(c)
        staged(first, second)

    @pl.when(lev == 2)
    def _():
        def first(c):
            ready(c)

            left(c).wait_recv()

            def body(rv, at, zat, put):
                us, u, d = ahead(rv, [Z[zat(k), :] for k in range(LEV)], None, None)
                e0, e1, e2 = four(rv * rv)
                v = FR[at(0), :] + rv * (e1 * u + e2 * d)
                w = FR[at(1), :] + rv * (e0 * u + e1 * d)
                _, v, w = back(rv, us, v, w)
                SL[at(0), :] = v
                SL[at(1), :] = w
            each(c, body)
            left(c).start()

        def second(c):
            right(c).wait_recv()

            def body(rv, at, zat, put):
                us, u, d = ahead(rv, [Z[zat(k), :] for k in range(LEV)], FL[at(0), :], FL[at(1), :])
                SR[at(0), :] = u
                SR[at(1), :] = d
                e0, e1, e2 = four(rv * rv)
                v = FR[at(0), :] + rv * (e1 * u + e2 * d)
                w = FR[at(1), :] + rv * (e0 * u + e1 * d)
                vs, _, _ = back(rv, us, v, w)
                put(vs)
            each(c, body)
            right(c).start()
            send_out(c)
        staged(first, second)

    for bg in range(BG):
        all_of(SB, RB, s1_sem, r1_sem, bg).wait_send()
        all_of(RP, CB, s2_sem, r2_sem, bg).wait_send()


def per_device(control, decay_lon, decay_lat, decay_vert):
    lines = control.reshape(LINES, SEG * LANES)
    hbm = pl.BlockSpec(memory_space=pltpu.HBM)
    vmem = pl.BlockSpec(memory_space=pltpu.VMEM)
    f32 = jnp.float32
    dma = pltpu.SemaphoreType.DMA
    filtered = pl.pallas_call(
        kernel,
        out_shape=jax.ShapeDtypeStruct((LINES, SEG * LANES), f32),
        in_specs=[hbm] * 4,
        out_specs=vmem,
        scratch_shapes=[
            pltpu.VMEM((LINES, SEG * LANES), f32),
            pltpu.VMEM((2 * LANES * SEG, LANES), f32),
            pltpu.VMEM((LINES * SEG, LANES), f32),
            pltpu.VMEM((ROWS, SEG * LANES), f32),
            pltpu.VMEM((SEG * ROWS, LANES), f32),
            pltpu.VMEM((8 * LEV * 8, LANES), f32),
            pltpu.VMEM((1, ROWS), f32),
            pltpu.VMEM((SEG, LANES), f32),
        ] + [pltpu.VMEM((BG * NR * MSG, LANES), f32)] * 4
        + [pltpu.VMEM((NCH * CH, LANES), f32)] * 4
        + [dma((LINES // IN,))] + [dma] * 3 + [dma((BG,))] * 4 + [dma] * 2 + [dma((NCH,))] * 2,
        compiler_params=pltpu.CompilerParams(
            collective_id=0, has_side_effects=True, vmem_limit_bytes=50 * 1024 * 1024),
        name="filters",
    )(*[pltpu.with_memory_space_constraint(x, pltpu.HBM) for x in (lines, decay_lon.reshape(1, ROWS), decay_lat.reshape(SEG, LANES), decay_vert)])
    return filtered.reshape(LEV, ROWS, SEG * LANES)


def solution(mesh):
    in_specs = (P("lev", "row", None), P("row"), P(), P("row", None))
    out_specs = P("lev", "row", None)
    return jax.shard_map(
        per_device, mesh=mesh, in_specs=in_specs, out_specs=out_specs, check_vma=False
    )
```

```python
import functools

import jax
import jax.numpy as jnp
from jax import lax
from jax.experimental import pallas as pl
from jax.experimental.pallas import tpu as pltpu
from jax.sharding import PartitionSpec as P

MESH = pl.DeviceIdType.MESH

LANES = 128
SEG = 24
ROWS = 48
LEV = 4
LINES = LEV * ROWS
BG = SEG // 8
NR = 32
MSG = 8
JC = 4
NJ = ROWS // JC
NCH = BG * NJ
CH = 2 * JC * 8
LAG = 6
NB = 4
CB = 22
IN = 48


def gain_sq(r):
    q = r * r
    a = (1.0 - r) * (1.0 + r)
    a2 = a * a
    a4 = a2 * a2
    return jnp.sqrt(a4 * a2 * a / (1.0 + q * (9.0 + q * (9.0 + q))))


def sums_double(q, n, qn, s0, s1, s2):
    return (
        s0 + qn * s0,
        s1 + qn * (s1 + n * s0),
        s2 + qn * (s2 + (2.0 * n) * s1 + (n * n) * s0),
    )


def sums(q, base, doublings):
    s0 = jnp.ones_like(q)
    s1 = jnp.ones_like(q)
    s2 = jnp.ones_like(q)
    qn = q
    for t in range(1, base):
        s0 = s0 + qn
        s1 = s1 + (t + 1.0) * qn
        s2 = s2 + ((t + 1.0) * (t + 1.0)) * qn
        qn = qn * q
    n = float(base)
    for _ in range(doublings):
        s0, s1, s2 = sums_double(q, n, qn, s0, s1, s2)
        qn = qn * qn
        n = 2.0 * n
    return s0, s1, s2


def power(r, base, doublings):
    p = r
    for _ in range(base - 1):
        p = p * r
    for _ in range(doublings):
        p = p * p
    return p


def sublanes():
    return lax.broadcasted_iota(jnp.int32, (8, LANES), 0)


def carry_powers(rn):
    one, two, four = rn, rn * rn, (rn * rn) * (rn * rn)

    def by(idx):
        p = jnp.where(idx % 2 == 1, one, 1.0)
        p = p * jnp.where((idx // 2) % 2 == 1, two, 1.0)
        return p * jnp.where(idx // 4 == 1, four, 1.0)
    return one, two, four, four * four, by(sublanes()), by(7 - sublanes())


def block_carries(us, ds, powers, n, rev):
    r1, r2, r4, r8, up, down = powers
    idx = 7 - sublanes() if rev else sublanes()
    along = down if rev else up
    far = (n * idx.astype(jnp.float32))

    def shifted(x, t):
        return jnp.where(idx >= t, pltpu.roll(x, 8 - t if rev else t, 0), 0.0)

    def last(x):
        row = x[0:1, :] if rev else x[7:8, :]
        return jnp.broadcast_to(row, (8, LANES))

    cu = jnp.zeros((8, LANES), jnp.float32)
    cd = cu
    out = [None] * len(us)
    order = range(len(us))
    for i in (reversed(order) if rev else order):
        u, d = us[i], ds[i]
        for t, rt in ((1, r1), (2, r2), (4, r4)):
            su, sd = shifted(u, t), shifted(d, t)
            u = u + rt * (su + (n * t) * sd)
            d = d + rt * sd
        out[i] = (shifted(u, 1) + along * (cu + far * cd), shifted(d, 1) + along * cd)
        cu, cd = r8 * (cu + (8.0 * n) * cd) + last(u), r8 * cd + last(d)
    return out


def kernel(ctrl, dlon, dlat, dvert, out, X, Y, Z, PI, PV, OS, DN, DL,
           SB, RB, RP, RC, SR, SL, FL, FR, WS, WR, OSD, ORC,
           in_sem, pv_sem, dn_sem, dl_sem, s1_sem, r1_sem, s2_sem, r2_sem,
           sr_sem, sl_sem, fl_sem, fr_sem, ws_sem, os_sem, wr_sem, or_sem):
    lev = lax.axis_index("lev")
    me = lax.axis_index("row")
    barrier = pltpu.get_barrier_semaphore()

    def in_copy(i):
        at = pl.ds(pl.multiple_of(i * IN, 8), IN)
        return pltpu.make_async_copy(ctrl.at[at, :], X.at[at, :], in_sem.at[i])

    pv_copy = pltpu.make_async_copy(dvert, PI, pv_sem)
    dn_copy = pltpu.make_async_copy(dlon, DN, dn_sem)
    dl_copy = pltpu.make_async_copy(dlat, DL, dl_sem)

    def loop(n, body, unroll=1):
        def step(i, carry):
            body(i)
            return carry
        lax.fori_loop(0, n, step, 0, unroll=unroll)

    dn_copy.start()
    for i in range(LINES // IN):
        in_copy(i).start()
    dl_copy.start()
    pv_copy.start()

    def greet(i):
        pl.semaphore_signal(barrier, inc=1, device_id=(lev, lax.rem(me + i + 1, NR)), device_id_type=MESH)
    loop(NR - 1, greet)

    for step in (1, 3):
        pl.semaphore_signal(barrier, inc=1, device_id=(lax.rem(lev + step, 4), me), device_id_type=MESH)

    zero = jnp.zeros((8, LANES), jnp.float32)
    one = jnp.ones((8, LANES), jnp.float32)
    rest = jnp.zeros((LANES - 96, LANES), jnp.float32)

    for g in range(2):
        for i in range(96 // IN):
            in_copy(g * (96 // IN) + i).wait()

        def turn_in(i, g=g):
            for k in range(8):
                b = 8 * i + k
                tile = X[pl.ds(g * 96, 96), pl.ds(pl.multiple_of(b * LANES, LANES), LANES)]
                Y[pl.ds(g * LANES * SEG + b, LANES, stride=SEG), :] = jnp.concatenate([tile, rest]).T
        loop(SEG // 8, turn_in)

    dn_copy.wait()
    line = DN[...]
    line = jnp.concatenate([line, line, line[:, :32]], axis=1)
    r = jnp.broadcast_to(line, (8, LANES))
    chains = [(g, bg) for g in range(2) for bg in range(BG)]
    BLK = 4

    def at_lon(g, bg, l):
        return pl.ds(pl.multiple_of((g * LANES + l) * SEG + bg * 8, 8), 8)

    def lon_ends(l, state):
        p, pp, rest = state
        new = []
        for i, (g, bg) in enumerate(chains):
            u, d, v, w = rest[i]
            d = r * d + Y[at_lon(g, bg, l), :]
            u = r * u + d
            new.append((u, d, v + pp * u, w + p * u))
        p = r * p
        return (p, r * pp + p, tuple(new))

    init = (one, one, tuple((zero, zero, zero, zero) for _ in chains))
    _, _, ends = lax.fori_loop(0, LANES, lon_ends, init, unroll=4)

    s0, s1, s2 = sums(r * r, 1, 7)
    lon_powers = carry_powers(power(r, 1, 7))
    n = float(LANES)
    ahead_in, back_in = {}, {}
    for g in range(2):
        of = [ends[g * BG + bg] for bg in range(BG)]
        states = block_carries([e[0] for e in of], [e[1] for e in of], lon_powers, n, False)
        vs = [e[2] + r * (s1 * u + s2 * d) for e, (u, d) in zip(of, states)]
        ws = [e[3] + r * (s0 * u + s1 * d) for e, (u, d) in zip(of, states)]
        backs = block_carries(vs, ws, lon_powers, n, True)
        for bg in range(BG):
            ahead_in[g, bg] = states[bg]
            back_in[g, bg] = backs[bg]

    def lon_ahead(i, state):
        l0 = i * BLK
        xs = [[Y[at_lon(g, bg, l0 + q), :] for g, bg in chains] for q in range(BLK)]
        state = list(state)
        for q in range(BLK):
            for k in range(len(chains)):
                u, d = state[k]
                d = r * d + xs[q][k]
                u = r * u + d
                state[k] = (u, d)
                xs[q][k] = u
        for q in range(BLK):
            for k, (g, bg) in enumerate(chains):
                Y[at_lon(g, bg, l0 + q), :] = xs[q][k]
        return tuple(state)

    lax.fori_loop(0, LANES // BLK, lon_ahead, tuple(ahead_in[ch] for ch in chains))

    g_lon = gain_sq(r)

    def at_lat(k, j, bg):
        return pl.ds(pl.multiple_of((k * ROWS + j) * SEG + bg * 8, 8), 8)

    def slot(ref, bg, i):
        return ref.at[pl.ds(pl.multiple_of((bg * NR + i) * MSG, 8), 4), :]

    def send(src, dst, ssem, rsem, bg):
        def to(i):
            p = lax.rem(me + i + 1, NR)
            pltpu.make_async_remote_copy(
                src_ref=slot(src, bg, p), dst_ref=slot(dst, bg, me), send_sem=ssem.at[bg],
                recv_sem=rsem.at[bg], device_id=(lev, p), device_id_type=MESH).start()
        loop(NR - 1, to)
        at = pl.ds(pl.multiple_of((bg * NR + me) * MSG, 8), 4)
        dst[at, :] = src[at, :]

    def all_of(src, dst, ssem, rsem, bg):
        at = pl.ds(pl.multiple_of(bg * NR * MSG, 8), (NR - 1) * 4)
        return pltpu.make_async_remote_copy(
            src_ref=src.at[at, :], dst_ref=dst.at[at, :], send_sem=ssem.at[bg], recv_sem=rsem.at[bg],
            device_id=(lev, lax.rem(me + 1, NR)), device_id_type=MESH)

    for bg in range(BG):
        def lon_back(i, state, bg=bg):
            l0 = LANES - BLK - i * BLK
            xs = [[Y[at_lon(g, bg, l0 + q), :] for g in range(2)] for q in range(BLK)]
            state = list(state)
            for q in range(BLK - 1, -1, -1):
                for g in range(2):
                    v, w = state[g]
                    w = r * w + xs[q][g]
                    v = r * v + w
                    state[g] = (v, w)
                    xs[q][g] = v * g_lon
            for q in range(BLK):
                for g in range(2):
                    Y[at_lon(g, bg, l0 + q), :] = xs[q][g]
            return tuple(state)

        lax.fori_loop(0, LANES // BLK, lon_back, (back_in[0, bg], back_in[1, bg]), unroll=2)

        def turn_out(i, bg=bg):
            for q in range(4):
                b = bg * 8 + i * 4 + q
                for g in range(2):
                    tile = Y[pl.ds(g * LANES * SEG + b, LANES, stride=SEG), :].T
                    for k in range(2):
                        Z[pl.ds((2 * g + k) * ROWS * SEG + b, ROWS, stride=SEG), :] = tile[k * ROWS:(k + 1) * ROWS, :]
        loop(2, turn_out)

        if bg == 0:
            dl_copy.wait()
        rl = DL[bg * 8:(bg + 1) * 8, :]

        def lat_ends(j, state, rl=rl, bg=bg):
            p, pp, rest = state
            new = []
            for k in range(LEV):
                u, d, v, w = rest[k]
                d = rl * d + Z[at_lat(k, j, bg), :]
                u = rl * u + d
                new.append((u, d, v + pp * u, w + p * u))
            p = rl * p
            return (p, rl * pp + p, tuple(new))

        init = (one, one, tuple((zero, zero, zero, zero) for _ in range(LEV)))
        _, _, ends = lax.fori_loop(0, ROWS, lat_ends, init, unroll=4)
        for k in range(LEV):
            for val in range(4):
                SB[pl.ds((bg * NR + k * 8) * MSG + val, 8, stride=MSG), :] = ends[k][val]
        if bg == 0:
            pl.semaphore_wait(barrier, NR - 1 + 2)
        send(SB, RB, s1_sem, r1_sem, bg)

    pv_copy.wait()

    def place(b):
        for q in range(ROWS // 8):
            PV[pl.ds(pl.multiple_of(b * ROWS + q * 8, 8), 8), :] = PI[
                q * 8:(q + 1) * 8, pl.ds(pl.multiple_of(b * LANES, LANES), LANES)]
    loop(SEG, place, unroll=2)

    m = float(ROWS)
    for bg in range(BG):
        ro = jnp.broadcast_to(DL[pl.ds(bg * 8 + lax.rem(me, 8), 1), :], (8, LANES))
        o0, o1, o2 = sums(ro * ro, 3, 4)
        own_powers = carry_powers(power(ro, 3, 4))
        all_of(SB, RB, s1_sem, r1_sem, bg).wait_recv()

        def rows_of(q, val, bg=bg):
            return pl.ds((bg * NR + q * 8) * MSG + val, 8, stride=MSG)

        def had(val):
            return [RB[rows_of(q, val), :] for q in range(NR // 8)]
        states = block_carries(had(0), had(1), own_powers, m, False)
        vs = [e + ro * (o1 * u + o2 * d) for e, (u, d) in zip(had(2), states)]
        ws = [e + ro * (o0 * u + o1 * d) for e, (u, d) in zip(had(3), states)]
        backs = block_carries(vs, ws, own_powers, m, True)
        for q in range(NR // 8):
            RP[rows_of(q, 0), :], RP[rows_of(q, 1), :] = states[q]
            RP[rows_of(q, 2), :], RP[rows_of(q, 3), :] = backs[q]
        send(RP, RC, s2_sem, r2_sem, bg)

    def lat_finish(bg):
        all_of(RP, RC, s2_sem, r2_sem, bg).wait_recv()
        rl = DL[pl.ds(pl.multiple_of(bg * 8, 8), 8), :]
        g_lat = gain_sq(rl)

        def come(k, val):
            return RC[pl.ds((bg * NR + k * 8) * MSG + val, 8, stride=MSG), :]

        def lat_ahead(i, state):
            xs = [[Z[at_lat(k, i * BLK + q, bg), :] for k in range(LEV)] for q in range(BLK)]
            state = list(state)
            for q in range(BLK):
                for k in range(LEV):
                    u, d = state[k]
                    d = rl * d + xs[q][k]
                    u = rl * u + d
                    state[k] = (u, d)
                    xs[q][k] = u
            for q in range(BLK):
                for k in range(LEV):
                    Z[at_lat(k, i * BLK + q, bg), :] = xs[q][k]
            return tuple(state)
        lax.fori_loop(0, ROWS // BLK, lat_ahead, tuple((come(k, 0), come(k, 1)) for k in range(LEV)))

        def lat_back(i, state):
            j0 = ROWS - BLK - i * BLK
            xs = [[Z[at_lat(k, j0 + q, bg), :] for k in range(LEV)] for q in range(BLK)]
            state = list(state)
            for q in range(BLK - 1, -1, -1):
                for k in range(LEV):
                    v, w = state[k]
                    w = rl * w + xs[q][k]
                    v = rl * v + w
                    state[k] = (v, w)
                    xs[q][k] = v * g_lat
            for q in range(BLK):
                for k in range(LEV):
                    Z[at_lat(k, j0 + q, bg), :] = xs[q][k]
            return tuple(state)
        lax.fori_loop(0, ROWS // BLK, lat_back, tuple((come(k, 2), come(k, 3)) for k in range(LEV)))


    def chunk(ref, c):
        return ref.at[NB * CH:, :] if c is None else ref.at[pl.ds(pl.multiple_of(c * CH, 8), CH), :]

    def one_of(sem, c):
        return sem.at[0 if c is None else c]

    def right(c):
        return pltpu.make_async_remote_copy(
            src_ref=chunk(SR, c), dst_ref=chunk(FL, c), send_sem=sr_sem, recv_sem=one_of(fl_sem, c),
            device_id=(lax.rem(lev + 1, 4), me), device_id_type=MESH)

    def left(c):
        return pltpu.make_async_remote_copy(
            src_ref=chunk(SL, c), dst_ref=chunk(FR, c), send_sem=sl_sem, recv_sem=one_of(fr_sem, c),
            device_id=(lax.rem(lev + 3, 4), me), device_id_type=MESH)

    def four_values(c):
        at = pl.ds(0, NB * 2 * CH) if c is None else pl.ds(pl.multiple_of(c * 2 * CH, 8), 2 * CH)
        return pltpu.make_async_remote_copy(
            src_ref=WS.at[at, :], dst_ref=WR.at[at, :], send_sem=ws_sem, recv_sem=one_of(wr_sem, c),
            device_id=(lev + 1 - 2 * lax.rem(lev, 2), me), device_id_type=MESH)

    def two_values(c):
        at = pl.ds(0, NB * CH) if c is None else pl.ds(pl.multiple_of(c * CH, 8), CH)
        return pltpu.make_async_remote_copy(
            src_ref=OSD.at[at, :], dst_ref=ORC.at[at, :], send_sem=os_sem, recv_sem=one_of(or_sem, c),
            device_id=(3 - lev, me), device_id_type=MESH)

    def each(c, body):
        bg = c // NJ
        j0 = lax.rem(c, NJ) * JC
        for jj in range(JC):
            j = j0 + jj
            rv = PV[pl.ds(bg * 8 * ROWS + j, 8, stride=ROWS), :]

            def at(val, jj=jj, pitch=CH):
                return pl.ds(pl.multiple_of(c * pitch + (val * JC + jj) * 8, 8), 8)

            def zat(k, j=j):
                return pl.ds(pl.multiple_of((k * ROWS + j) * SEG + bg * 8, 8), 8)

            def put(vals, rv=rv, j=j):
                gv = gain_sq(rv)
                for k in range(LEV):
                    OS[pl.ds(k * 8 + lax.rem(j, 8), 8, stride=LEV * 8), :] = vals[k] * gv
            body(rv, at, zat, put)

    def ahead(rv, xs, u, d):
        us = []
        for x in xs:
            d = x if d is None else rv * d + x
            u = d if u is None else rv * u + d
            us.append(u)
        return us, u, d

    def back(rv, us, v, w):
        vs = [None] * LEV
        for k in range(LEV - 1, -1, -1):
            w = us[k] if w is None else rv * w + us[k]
            v = w if v is None else rv * v + w
            vs[k] = v
        return vs, v, w

    def four(q):
        return (1.0 + q * (1.0 + q * (1.0 + q)),
                1.0 + q * (2.0 + q * (3.0 + 4.0 * q)),
                1.0 + q * (4.0 + q * (9.0 + 16.0 * q)))

    def send_out(c):
        @pl.when(lax.rem(c, 2) == 1)
        def _():
            bg = c // NJ
            j0 = lax.rem(c - 1, NJ) * JC
            for k in range(LEV):
                for b in range(8):
                    out[pl.ds(pl.multiple_of(k * ROWS + j0, 8), 8),
                        pl.ds(pl.multiple_of((bg * 8 + b) * LANES, LANES), LANES)] = OS[
                            (b * LEV + k) * 8:(b * LEV + k + 1) * 8, :]

    def wide(at, val):
        return at(val, pitch=2 * CH)

    def moved(rv, first, second):
        r2 = rv * rv
        r4 = r2 * r2
        return r4 * (first + 4.0 * second), r4 * second

    def both(rv, sums3, u, d):
        e0, e1, e2 = sums3
        return rv * (e1 * u + e2 * d), rv * (e0 * u + e1 * d)

    def ready(c):
        @pl.when(lax.rem(c, NJ) == 0)
        def _():
            lat_finish(c // NJ)

    lat_finish(0)

    @pl.when(lev == 0)
    def _():
        def first(c):
            ready(c)

            def body(rv, at, zat, put):
                us, u, d = ahead(rv, [Z[zat(k), :] for k in range(LEV)], None, None)
                for k in range(LEV):
                    Z[zat(k), :] = us[k]
                SR[at(0), :] = u
                SR[at(1), :] = d
            each(c, body)
            right(c).start()
        loop(NCH - NB, lambda c: first(NB + c))

        def inner(c):
            four_values(c).wait_recv()

            def body(rv, at, zat, put):
                us, u, d = ahead(rv, [Z[zat(k), :] for k in range(LEV)], None, None)
                for k in range(LEV):
                    Z[zat(k), :] = us[k]
                WS[wide(at, 0), :] = u
                WS[wide(at, 1), :] = d
                u, d = moved(rv, u, d)
                OSD[at(0), :] = u + WR[wide(at, 0), :]
                OSD[at(1), :] = d + WR[wide(at, 1), :]
            each(c, body)
            two_values(c).start()
        loop(NB, inner)

        def outer(c):
            two_values(c).wait_recv()

            def body(rv, at, zat, put):
                q = rv * rv
                q2 = q * q
                av, aw = both(rv, sums_double(q, 4.0, q2 * q2, *four(q)), OSD[at(0), :], OSD[at(1), :])
                v, w = ORC[at(0), :] + av, ORC[at(1), :] + aw
                WS[wide(at, 2), :] = v
                WS[wide(at, 3), :] = w
                v, w = moved(rv, v, w)
                av, aw = both(rv, four(q), WS[wide(at, 0), :], WS[wide(at, 1), :])
                v = v + av + WR[wide(at, 2), :]
                w = w + aw + WR[wide(at, 3), :]
                vs, _, _ = back(rv, [Z[zat(k), :] for k in range(LEV)], v, w)
                put(vs)
            each(c, body)
            send_out(c)
        loop(NB, outer)

        def second(c):
            left(c).wait_recv()

            def body(rv, at, zat, put):
                vs, _, _ = back(rv, [Z[zat(k), :] for k in range(LEV)], FR[at(0), :], FR[at(1), :])
                put(vs)
            each(c, body)
            send_out(c)

        def second_and_rest(i):
            @pl.when(i == CB)
            def _():
                right(None).wait_send()
                loop(NB, lambda c: four_values(c).start())
            second(NB + i)
        loop(NCH - NB, second_and_rest)
        four_values(None).wait_send()
        two_values(None).wait_send()

    @pl.when(lev == 3)
    def _():
        def first(c):
            ready(c)

            def body(rv, at, zat, put):
                us, _, _ = ahead(rv, [Z[zat(k), :] for k in range(LEV)], None, None)
                _, v, w = back(rv, us, None, None)
                SL[at(0), :] = v
                SL[at(1), :] = w
            each(c, body)
            left(c).start()
        loop(NCH - NB, lambda c: first(NB + c))

        def inner(c):
            four_values(c).wait_recv()

            def body(rv, at, zat, put):
                us, _, _ = ahead(rv, [Z[zat(k), :] for k in range(LEV)], None, None)
                _, v, w = back(rv, us, None, None)
                av, aw = both(rv, four(rv * rv), WR[wide(at, 0), :], WR[wide(at, 1), :])
                v, w = moved(rv, v + av, w + aw)
                OSD[at(0), :] = v + WR[wide(at, 2), :]
                OSD[at(1), :] = w + WR[wide(at, 3), :]
            each(c, body)
            two_values(c).start()
        loop(NB, inner)

        def outer(c):
            two_values(c).wait_recv()

            def body(rv, at, zat, put):
                u, d = ORC[at(0), :], ORC[at(1), :]
                WS[wide(at, 0), :] = u
                WS[wide(at, 1), :] = d
                u, d = moved(rv, u, d)
                us, _, _ = ahead(rv, [Z[zat(k), :] for k in range(LEV)],
                                 u + WR[wide(at, 0), :], d + WR[wide(at, 1), :])
                vs, v, w = back(rv, us, None, None)
                WS[wide(at, 2), :] = v
                WS[wide(at, 3), :] = w
                put(vs)
            each(c, body)
            send_out(c)
        loop(NB, outer)

        def second(c):
            right(c).wait_recv()

            def body(rv, at, zat, put):
                us, _, _ = ahead(rv, [Z[zat(k), :] for k in range(LEV)], FL[at(0), :], FL[at(1), :])
                vs, _, _ = back(rv, us, None, None)
                put(vs)
            each(c, body)
            send_out(c)

        def second_and_rest(i):
            @pl.when(i == CB)
            def _():
                left(None).wait_send()
                loop(NB, lambda c: four_values(c).start())
            second(NB + i)
        loop(NCH - NB, second_and_rest)
        four_values(None).wait_send()
        two_values(None).wait_send()

    def staged(first, second):
        def inner(c):
            def body(rv, at, zat, put):
                us, u, d = ahead(rv, [Z[zat(k), :] for k in range(LEV)], None, None)
                _, v, w = back(rv, us, None, None)
                for val, x in enumerate((u, d, v, w)):
                    WS[wide(at, val), :] = x
            each(c, body)
            four_values(c).start()
        loop(NB, inner)

        def step(i):
            @pl.when(i < NCH)
            def _():
                first(i)

            @pl.when(i >= NB + LAG)
            def _():
                second(i - LAG)
        lax.fori_loop(NB, NCH + LAG, lambda i, carry: (step(i), carry)[1], 0)

        def outer(c):
            four_values(c).wait_recv()

            def body(rv, at, zat, put):
                us, _, _ = ahead(rv, [Z[zat(k), :] for k in range(LEV)], WR[wide(at, 0), :], WR[wide(at, 1), :])
                vs, _, _ = back(rv, us, WR[wide(at, 2), :], WR[wide(at, 3), :])
                put(vs)
            each(c, body)
            send_out(c)
        loop(NB, outer)
        right(None).wait_send()
        left(None).wait_send()
        four_values(None).wait_send()

    @pl.when(lev == 1)
    def _():
        def first(c):
            ready(c)

            right(c).wait_recv()

            def body(rv, at, zat, put):
                us, u, d = ahead(rv, [Z[zat(k), :] for k in range(LEV)], FL[at(0), :], FL[at(1), :])
                for k in range(LEV):
                    Z[zat(k), :] = us[k]
                SR[at(0), :] = u
                SR[at(1), :] = d
            each(c, body)
            right(c).start()

        def second(c):
            left(c).wait_recv()

            def body(rv, at, zat, put):
                q = rv * rv
                q2 = q * q
                e0, e1, e2 = sums_double(q, 4.0, q2 * q2, *four(q))
                u, d = SR[at(0), :], SR[at(1), :]
                v = FR[at(0), :] + rv * (e1 * u + e2 * d)
                w = FR[at(1), :] + rv * (e0 * u + e1 * d)
                vs, v, w = back(rv, [Z[zat(k), :] for k in range(LEV)], v, w)
                SL[at(0), :] = v
                SL[at(1), :] = w
                put(vs)
            each(c, body)
            left(c).start()
            send_out(c)
        staged(first, second)

    @pl.when(lev == 2)
    def _():
        def first(c):
            ready(c)

            left(c).wait_recv()

            def body(rv, at, zat, put):
                us, u, d = ahead(rv, [Z[zat(k), :] for k in range(LEV)], None, None)
                e0, e1, e2 = four(rv * rv)
                v = FR[at(0), :] + rv * (e1 * u + e2 * d)
                w = FR[at(1), :] + rv * (e0 * u + e1 * d)
                _, v, w = back(rv, us, v, w)
                SL[at(0), :] = v
                SL[at(1), :] = w
            each(c, body)
            left(c).start()

        def second(c):
            right(c).wait_recv()

            def body(rv, at, zat, put):
                us, u, d = ahead(rv, [Z[zat(k), :] for k in range(LEV)], FL[at(0), :], FL[at(1), :])
                SR[at(0), :] = u
                SR[at(1), :] = d
                e0, e1, e2 = four(rv * rv)
                v = FR[at(0), :] + rv * (e1 * u + e2 * d)
                w = FR[at(1), :] + rv * (e0 * u + e1 * d)
                vs, _, _ = back(rv, us, v, w)
                put(vs)
            each(c, body)
            right(c).start()
            send_out(c)
        staged(first, second)

    for bg in range(BG):
        all_of(SB, RB, s1_sem, r1_sem, bg).wait_send()
        all_of(RP, RC, s2_sem, r2_sem, bg).wait_send()


def per_device(control, decay_lon, decay_lat, decay_vert):
    lines = control.reshape(LINES, SEG * LANES)
    hbm = pl.BlockSpec(memory_space=pltpu.HBM)
    vmem = pl.BlockSpec(memory_space=pltpu.VMEM)
    f32 = jnp.float32
    dma = pltpu.SemaphoreType.DMA
    filtered = pl.pallas_call(
        kernel,
        out_shape=jax.ShapeDtypeStruct((LINES, SEG * LANES), f32),
        in_specs=[hbm] * 4,
        out_specs=vmem,
        scratch_shapes=[
            pltpu.VMEM((LINES, SEG * LANES), f32),
            pltpu.VMEM((2 * LANES * SEG, LANES), f32),
            pltpu.VMEM((LINES * SEG, LANES), f32),
            pltpu.VMEM((ROWS, SEG * LANES), f32),
            pltpu.VMEM((SEG * ROWS, LANES), f32),
            pltpu.VMEM((8 * LEV * 8, LANES), f32),
            pltpu.VMEM((1, ROWS), f32),
            pltpu.VMEM((SEG, LANES), f32),
        ] + [pltpu.VMEM((BG * NR * MSG, LANES), f32)] * 4
        + [pltpu.VMEM((NCH * CH, LANES), f32)] * 4
        + [pltpu.VMEM((NB * 2 * CH, LANES), f32)] * 2 + [pltpu.VMEM((NB * CH, LANES), f32)] * 2
        + [dma((LINES // IN,))] + [dma] * 3 + [dma((BG,))] * 4 + [dma] * 2 + [dma((NCH,))] * 2
        + [dma] * 2 + [dma((NB,))] * 2,
        compiler_params=pltpu.CompilerParams(
            collective_id=0, has_side_effects=True, vmem_limit_bytes=50 * 1024 * 1024),
        name="filters",
    )(*[pltpu.with_memory_space_constraint(x, pltpu.HBM) for x in (lines, decay_lon.reshape(1, ROWS), decay_lat.reshape(SEG, LANES), decay_vert)])
    return filtered.reshape(LEV, ROWS, SEG * LANES)


def solution(mesh):
    in_specs = (P("lev", "row", None), P("row"), P(), P("row", None))
    out_specs = P("lev", "row", None)
    return jax.shard_map(
        per_device, mesh=mesh, in_specs=in_specs, out_specs=out_specs, check_vma=False
    )
```

```python
import functools

import jax
import jax.numpy as jnp
from jax import lax
from jax.experimental import pallas as pl
from jax.experimental.pallas import tpu as pltpu
from jax.sharding import PartitionSpec as P

MESH = pl.DeviceIdType.MESH

LANES = 128
SEG = 24
ROWS = 48
LEV = 4
LINES = LEV * ROWS
BG = SEG // 8
NR = 32
MSG = 8
JC = 4
NJ = ROWS // JC
NCH = BG * NJ
CH = 2 * JC * 8
LAG = 6
NB = 4
CB = 22
IN = 48


def gain_sq(r):
    q = r * r
    a = (1.0 - r) * (1.0 + r)
    a2 = a * a
    a4 = a2 * a2
    return jnp.sqrt(a4 * a2 * a / (1.0 + q * (9.0 + q * (9.0 + q))))


def sums_double(q, n, qn, s0, s1, s2):
    return (
        s0 + qn * s0,
        s1 + qn * (s1 + n * s0),
        s2 + qn * (s2 + (2.0 * n) * s1 + (n * n) * s0),
    )


def sums(q, base, doublings):
    s0 = jnp.ones_like(q)
    s1 = jnp.ones_like(q)
    s2 = jnp.ones_like(q)
    qn = q
    for t in range(1, base):
        s0 = s0 + qn
        s1 = s1 + (t + 1.0) * qn
        s2 = s2 + ((t + 1.0) * (t + 1.0)) * qn
        qn = qn * q
    n = float(base)
    for _ in range(doublings):
        s0, s1, s2 = sums_double(q, n, qn, s0, s1, s2)
        qn = qn * qn
        n = 2.0 * n
    return s0, s1, s2


def power(r, base, doublings):
    p = r
    for _ in range(base - 1):
        p = p * r
    for _ in range(doublings):
        p = p * p
    return p


def sublanes():
    return lax.broadcasted_iota(jnp.int32, (8, LANES), 0)


def carry_powers(rn):
    one, two, four = rn, rn * rn, (rn * rn) * (rn * rn)

    def by(idx):
        p = jnp.where(idx % 2 == 1, one, 1.0)
        p = p * jnp.where((idx // 2) % 2 == 1, two, 1.0)
        return p * jnp.where(idx // 4 == 1, four, 1.0)
    return one, two, four, four * four, by(sublanes()), by(7 - sublanes())


def block_carries(us, ds, powers, n, rev):
    r1, r2, r4, r8, up, down = powers
    idx = 7 - sublanes() if rev else sublanes()
    along = down if rev else up
    far = (n * idx.astype(jnp.float32))

    def shifted(x, t):
        return jnp.where(idx >= t, pltpu.roll(x, 8 - t if rev else t, 0), 0.0)

    def last(x):
        row = x[0:1, :] if rev else x[7:8, :]
        return jnp.broadcast_to(row, (8, LANES))

    cu = jnp.zeros((8, LANES), jnp.float32)
    cd = cu
    out = [None] * len(us)
    order = range(len(us))
    for i in (reversed(order) if rev else order):
        u, d = us[i], ds[i]
        for t, rt in ((1, r1), (2, r2), (4, r4)):
            su, sd = shifted(u, t), shifted(d, t)
            u = u + rt * (su + (n * t) * sd)
            d = d + rt * sd
        out[i] = (shifted(u, 1) + along * (cu + far * cd), shifted(d, 1) + along * cd)
        cu, cd = r8 * (cu + (8.0 * n) * cd) + last(u), r8 * cd + last(d)
    return out


def kernel(ctrl, dlon, dlat, dvert, out, X, Y, Z, PI, PV, OS, P1, P2, DN, DL,
           SB, RB, RP, RC, SR, SL, FL, FR, WS, WR, OSD, ORC,
           in_sem, pv_sem, dn_sem, dl_sem, s1_sem, r1_sem, s2_sem, r2_sem,
           sr_sem, sl_sem, fl_sem, fr_sem, ws_sem, os_sem, wr_sem, or_sem):
    lev = lax.axis_index("lev")
    me = lax.axis_index("row")
    barrier = pltpu.get_barrier_semaphore()

    def in_copy(i):
        at = pl.ds(pl.multiple_of(i * IN, 8), IN)
        return pltpu.make_async_copy(ctrl.at[at, :], X.at[at, :], in_sem.at[i])

    pv_copy = pltpu.make_async_copy(dvert, PI, pv_sem)
    dn_copy = pltpu.make_async_copy(dlon, DN, dn_sem)
    dl_copy = pltpu.make_async_copy(dlat, DL, dl_sem)

    def loop(n, body, unroll=1):
        def step(i, carry):
            body(i)
            return carry
        lax.fori_loop(0, n, step, 0, unroll=unroll)

    dn_copy.start()
    for i in range(LINES // IN):
        in_copy(i).start()
    dl_copy.start()
    pv_copy.start()

    def greet(i):
        pl.semaphore_signal(barrier, inc=1, device_id=(lev, lax.rem(me + i + 1, NR)), device_id_type=MESH)
    loop(NR - 1, greet)

    for step in (1, 3):
        pl.semaphore_signal(barrier, inc=1, device_id=(lax.rem(lev + step, 4), me), device_id_type=MESH)

    zero = jnp.zeros((8, LANES), jnp.float32)
    one = jnp.ones((8, LANES), jnp.float32)
    rest = jnp.zeros((LANES - 96, LANES), jnp.float32)

    for g in range(2):
        for i in range(96 // IN):
            in_copy(g * (96 // IN) + i).wait()

        def turn_in(i, g=g):
            for k in range(8):
                b = 8 * i + k
                tile = X[pl.ds(g * 96, 96), pl.ds(pl.multiple_of(b * LANES, LANES), LANES)]
                Y[pl.ds(g * LANES * SEG + b, LANES, stride=SEG), :] = jnp.concatenate([tile, rest]).T
        loop(SEG // 8, turn_in)

    dn_copy.wait()
    line = DN[...]
    line = jnp.concatenate([line, line, line[:, :32]], axis=1)
    r = jnp.broadcast_to(line, (8, LANES))
    chains = [(g, bg) for g in range(2) for bg in range(BG)]
    BLK = 8

    def at_lon(g, bg, l):
        return pl.ds(pl.multiple_of((g * LANES + l) * SEG + bg * 8, 8), 8)

    def at_step(l):
        return pl.ds(pl.multiple_of(l * 8, 8), 8)

    def lon_ends(i, state):
        p, pp, rest = state
        rest = list(rest)
        l0 = 2 * i
        xs = [[Y[at_lon(g, bg, l0 + q), :] for g, bg in chains] for q in range(2)]
        for q in range(2):
            P1[at_step(l0 + q), :] = p
            P2[at_step(l0 + q), :] = pp
            for k in range(len(chains)):
                u, d, v, w = rest[k]
                d = r * d + xs[q][k]
                u = r * u + d
                xs[q][k] = u
                rest[k] = (u, d, v + pp * u, w + p * u)
            p = r * p
            pp = r * pp + p
        for q in range(2):
            for k, (g, bg) in enumerate(chains):
                Y[at_lon(g, bg, l0 + q), :] = xs[q][k]
        return (p, pp, tuple(rest))

    init = (one, one, tuple((zero, zero, zero, zero) for _ in chains))
    _, _, ends = lax.fori_loop(0, LANES // 2, lon_ends, init, unroll=2)

    s0, s1, s2 = sums(r * r, 1, 7)
    lon_powers = carry_powers(power(r, 1, 7))
    n = float(LANES)
    ahead_in, back_in = {}, {}
    for g in range(2):
        of = [ends[g * BG + bg] for bg in range(BG)]
        states = block_carries([e[0] for e in of], [e[1] for e in of], lon_powers, n, False)
        vs = [e[2] + r * (s1 * u + s2 * d) for e, (u, d) in zip(of, states)]
        ws = [e[3] + r * (s0 * u + s1 * d) for e, (u, d) in zip(of, states)]
        backs = block_carries(vs, ws, lon_powers, n, True)
        for bg in range(BG):
            ahead_in[g, bg] = states[bg]
            back_in[g, bg] = backs[bg]

    g_lon = gain_sq(r)

    def at_lat(k, j, bg):
        return pl.ds(pl.multiple_of((k * ROWS + j) * SEG + bg * 8, 8), 8)

    def slot(ref, bg, i):
        return ref.at[pl.ds(pl.multiple_of((bg * NR + i) * MSG, 8), 4), :]

    def send(src, dst, ssem, rsem, bg):
        def to(i):
            p = lax.rem(me + 11 * (i + 1), NR)
            pltpu.make_async_remote_copy(
                src_ref=slot(src, bg, p), dst_ref=slot(dst, bg, me), send_sem=ssem.at[bg],
                recv_sem=rsem.at[bg], device_id=(lev, p), device_id_type=MESH).start()
        loop(NR - 1, to, unroll=8)
        at = pl.ds(pl.multiple_of((bg * NR + me) * MSG, 8), 4)
        dst[at, :] = src[at, :]

    def all_of(src, dst, ssem, rsem, bg):
        at = pl.ds(pl.multiple_of(bg * NR * MSG, 8), (NR - 1) * 4)
        return pltpu.make_async_remote_copy(
            src_ref=src.at[at, :], dst_ref=dst.at[at, :], send_sem=ssem.at[bg], recv_sem=rsem.at[bg],
            device_id=(lev, lax.rem(me + 1, NR)), device_id_type=MESH)

    for bg in range(BG):
        came = [(r * u, r * d) for u, d in (ahead_in[0, bg], ahead_in[1, bg])]

        def lon_back(i, state, bg=bg, came=came):
            l0 = LANES - BLK - i * BLK
            xs = [[Y[at_lon(g, bg, l0 + q), :] for g in range(2)] for q in range(BLK)]
            ps = [(P1[at_step(l0 + q), :], P2[at_step(l0 + q), :]) for q in range(BLK)]
            state = list(state)
            for q in range(BLK - 1, -1, -1):
                for g in range(2):
                    v, w = state[g]
                    w = r * w + (xs[q][g] + (ps[q][0] * came[g][0] + ps[q][1] * came[g][1]))
                    v = r * v + w
                    state[g] = (v, w)
                    xs[q][g] = v * g_lon
            for q in range(BLK):
                for g in range(2):
                    Y[at_lon(g, bg, l0 + q), :] = xs[q][g]
            return tuple(state)

        lax.fori_loop(0, LANES // BLK, lon_back, (back_in[0, bg], back_in[1, bg]), unroll=2)

        def turn_out(i, bg=bg):
            for q in range(4):
                b = bg * 8 + i * 4 + q
                for g in range(2):
                    tile = Y[pl.ds(g * LANES * SEG + b, LANES, stride=SEG), :].T
                    for k in range(2):
                        Z[pl.ds((2 * g + k) * ROWS * SEG + b, ROWS, stride=SEG), :] = tile[k * ROWS:(k + 1) * ROWS, :]
        loop(2, turn_out)

        if bg == 0:
            dl_copy.wait()
        rl = DL[bg * 8:(bg + 1) * 8, :]

        def lat_ends(j, state, rl=rl, bg=bg):
            p, pp, rest = state
            new = []
            for k in range(LEV):
                u, d, v, w = rest[k]
                d = rl * d + Z[at_lat(k, j, bg), :]
                u = rl * u + d
                new.append((u, d, v + pp * u, w + p * u))
            p = rl * p
            return (p, rl * pp + p, tuple(new))

        init = (one, one, tuple((zero, zero, zero, zero) for _ in range(LEV)))
        _, _, ends = lax.fori_loop(0, ROWS, lat_ends, init, unroll=4)
        for k in range(LEV):
            for val in range(4):
                SB[pl.ds((bg * NR + k * 8) * MSG + val, 8, stride=MSG), :] = ends[k][val]
        if bg == 0:
            pl.semaphore_wait(barrier, NR - 1 + 2)
        send(SB, RB, s1_sem, r1_sem, bg)

    pv_copy.wait()

    def place(b):
        for q in range(ROWS // 8):
            PV[pl.ds(pl.multiple_of(b * ROWS + q * 8, 8), 8), :] = PI[
                q * 8:(q + 1) * 8, pl.ds(pl.multiple_of(b * LANES, LANES), LANES)]
    loop(SEG, place, unroll=2)

    m = float(ROWS)
    for bg in range(BG):
        ro = jnp.broadcast_to(DL[pl.ds(bg * 8 + lax.rem(me, 8), 1), :], (8, LANES))
        o0, o1, o2 = sums(ro * ro, 3, 4)
        own_powers = carry_powers(power(ro, 3, 4))
        all_of(SB, RB, s1_sem, r1_sem, bg).wait_recv()

        def rows_of(q, val, bg=bg):
            return pl.ds((bg * NR + q * 8) * MSG + val, 8, stride=MSG)

        def had(val):
            return [RB[rows_of(q, val), :] for q in range(NR // 8)]
        states = block_carries(had(0), had(1), own_powers, m, False)
        vs = [e + ro * (o1 * u + o2 * d) for e, (u, d) in zip(had(2), states)]
        ws = [e + ro * (o0 * u + o1 * d) for e, (u, d) in zip(had(3), states)]
        backs = block_carries(vs, ws, own_powers, m, True)
        for q in range(NR // 8):
            RP[rows_of(q, 0), :], RP[rows_of(q, 1), :] = states[q]
            RP[rows_of(q, 2), :], RP[rows_of(q, 3), :] = backs[q]
        send(RP, RC, s2_sem, r2_sem, bg)

    def lat_finish(bg):
        all_of(RP, RC, s2_sem, r2_sem, bg).wait_recv()
        rl = DL[pl.ds(pl.multiple_of(bg * 8, 8), 8), :]
        g_lat = gain_sq(rl)

        def come(k, val):
            return RC[pl.ds((bg * NR + k * 8) * MSG + val, 8, stride=MSG), :]

        def lat_ahead(i, state):
            xs = [[Z[at_lat(k, i * BLK + q, bg), :] for k in range(LEV)] for q in range(BLK)]
            state = list(state)
            for q in range(BLK):
                for k in range(LEV):
                    u, d = state[k]
                    d = rl * d + xs[q][k]
                    u = rl * u + d
                    state[k] = (u, d)
                    xs[q][k] = u
            for q in range(BLK):
                for k in range(LEV):
                    Z[at_lat(k, i * BLK + q, bg), :] = xs[q][k]
            return tuple(state)
        lax.fori_loop(0, ROWS // BLK, lat_ahead, tuple((come(k, 0), come(k, 1)) for k in range(LEV)))

        def lat_back(i, state):
            j0 = ROWS - BLK - i * BLK
            xs = [[Z[at_lat(k, j0 + q, bg), :] for k in range(LEV)] for q in range(BLK)]
            state = list(state)
            for q in range(BLK - 1, -1, -1):
                for k in range(LEV):
                    v, w = state[k]
                    w = rl * w + xs[q][k]
                    v = rl * v + w
                    state[k] = (v, w)
                    xs[q][k] = v * g_lat
            for q in range(BLK):
                for k in range(LEV):
                    Z[at_lat(k, j0 + q, bg), :] = xs[q][k]
            return tuple(state)
        lax.fori_loop(0, ROWS // BLK, lat_back, tuple((come(k, 2), come(k, 3)) for k in range(LEV)))


    def chunk(ref, c):
        return ref.at[NB * CH:, :] if c is None else ref.at[pl.ds(pl.multiple_of(c * CH, 8), CH), :]

    def one_of(sem, c):
        return sem.at[0 if c is None else c]

    def right(c):
        return pltpu.make_async_remote_copy(
            src_ref=chunk(SR, c), dst_ref=chunk(FL, c), send_sem=sr_sem, recv_sem=one_of(fl_sem, c),
            device_id=(lax.rem(lev + 1, 4), me), device_id_type=MESH)

    def left(c):
        return pltpu.make_async_remote_copy(
            src_ref=chunk(SL, c), dst_ref=chunk(FR, c), send_sem=sl_sem, recv_sem=one_of(fr_sem, c),
            device_id=(lax.rem(lev + 3, 4), me), device_id_type=MESH)

    def four_values(c):
        at = pl.ds(0, NB * 2 * CH) if c is None else pl.ds(pl.multiple_of(c * 2 * CH, 8), 2 * CH)
        return pltpu.make_async_remote_copy(
            src_ref=WS.at[at, :], dst_ref=WR.at[at, :], send_sem=ws_sem, recv_sem=one_of(wr_sem, c),
            device_id=(lev + 1 - 2 * lax.rem(lev, 2), me), device_id_type=MESH)

    def two_values(c):
        at = pl.ds(0, NB * CH) if c is None else pl.ds(pl.multiple_of(c * CH, 8), CH)
        return pltpu.make_async_remote_copy(
            src_ref=OSD.at[at, :], dst_ref=ORC.at[at, :], send_sem=os_sem, recv_sem=one_of(or_sem, c),
            device_id=(3 - lev, me), device_id_type=MESH)

    def each(c, body):
        bg = c // NJ
        j0 = lax.rem(c, NJ) * JC
        for jj in range(JC):
            j = j0 + jj
            rv = PV[pl.ds(bg * 8 * ROWS + j, 8, stride=ROWS), :]

            def at(val, jj=jj, pitch=CH):
                return pl.ds(pl.multiple_of(c * pitch + (val * JC + jj) * 8, 8), 8)

            def zat(k, j=j):
                return pl.ds(pl.multiple_of((k * ROWS + j) * SEG + bg * 8, 8), 8)

            def put(vals, rv=rv, j=j):
                gv = gain_sq(rv)
                for k in range(LEV):
                    OS[pl.ds(k * 8 + lax.rem(j, 8), 8, stride=LEV * 8), :] = vals[k] * gv
            body(rv, at, zat, put)

    def ahead(rv, xs, u, d):
        us = []
        for x in xs:
            d = x if d is None else rv * d + x
            u = d if u is None else rv * u + d
            us.append(u)
        return us, u, d

    def back(rv, us, v, w):
        vs = [None] * LEV
        for k in range(LEV - 1, -1, -1):
            w = us[k] if w is None else rv * w + us[k]
            v = w if v is None else rv * v + w
            vs[k] = v
        return vs, v, w

    def four(q):
        return (1.0 + q * (1.0 + q * (1.0 + q)),
                1.0 + q * (2.0 + q * (3.0 + 4.0 * q)),
                1.0 + q * (4.0 + q * (9.0 + 16.0 * q)))

    def send_out(c):
        @pl.when(lax.rem(c, 2) == 1)
        def _():
            bg = c // NJ
            j0 = lax.rem(c - 1, NJ) * JC
            for k in range(LEV):
                for b in range(8):
                    out[pl.ds(pl.multiple_of(k * ROWS + j0, 8), 8),
                        pl.ds(pl.multiple_of((bg * 8 + b) * LANES, LANES), LANES)] = OS[
                            (b * LEV + k) * 8:(b * LEV + k + 1) * 8, :]

    def wide(at, val):
        return at(val, pitch=2 * CH)

    def moved(rv, first, second):
        r2 = rv * rv
        r4 = r2 * r2
        return r4 * (first + 4.0 * second), r4 * second

    def both(rv, sums3, u, d):
        e0, e1, e2 = sums3
        return rv * (e1 * u + e2 * d), rv * (e0 * u + e1 * d)

    def ready(c):
        @pl.when(lax.rem(c, NJ) == 0)
        def _():
            lat_finish(c // NJ)

    lat_finish(0)

    @pl.when(lev == 0)
    def _():
        def first(c):
            ready(c)

            def body(rv, at, zat, put):
                us, u, d = ahead(rv, [Z[zat(k), :] for k in range(LEV)], None, None)
                for k in range(LEV):
                    Z[zat(k), :] = us[k]
                SR[at(0), :] = u
                SR[at(1), :] = d
            each(c, body)
            right(c).start()
        loop(NCH - NB, lambda c: first(NB + c))

        def inner(c):
            four_values(c).wait_recv()

            def body(rv, at, zat, put):
                us, u, d = ahead(rv, [Z[zat(k), :] for k in range(LEV)], None, None)
                for k in range(LEV):
                    Z[zat(k), :] = us[k]
                WS[wide(at, 0), :] = u
                WS[wide(at, 1), :] = d
                u, d = moved(rv, u, d)
                OSD[at(0), :] = u + WR[wide(at, 0), :]
                OSD[at(1), :] = d + WR[wide(at, 1), :]
            each(c, body)
            two_values(c).start()
        loop(NB, inner)

        def outer(c):
            two_values(c).wait_recv()

            def body(rv, at, zat, put):
                q = rv * rv
                q2 = q * q
                av, aw = both(rv, sums_double(q, 4.0, q2 * q2, *four(q)), OSD[at(0), :], OSD[at(1), :])
                v, w = ORC[at(0), :] + av, ORC[at(1), :] + aw
                WS[wide(at, 2), :] = v
                WS[wide(at, 3), :] = w
                v, w = moved(rv, v, w)
                av, aw = both(rv, four(q), WS[wide(at, 0), :], WS[wide(at, 1), :])
                v = v + av + WR[wide(at, 2), :]
                w = w + aw + WR[wide(at, 3), :]
                vs, _, _ = back(rv, [Z[zat(k), :] for k in range(LEV)], v, w)
                put(vs)
            each(c, body)
            send_out(c)
        loop(NB, outer)

        def second(c):
            left(c).wait_recv()

            def body(rv, at, zat, put):
                vs, _, _ = back(rv, [Z[zat(k), :] for k in range(LEV)], FR[at(0), :], FR[at(1), :])
                put(vs)
            each(c, body)
            send_out(c)

        def second_and_rest(i):
            @pl.when(i == CB)
            def _():
                right(None).wait_send()
                loop(NB, lambda c: four_values(c).start())
            second(NB + i)
        loop(NCH - NB, second_and_rest)
        four_values(None).wait_send()
        two_values(None).wait_send()

    @pl.when(lev == 3)
    def _():
        def first(c):
            ready(c)

            def body(rv, at, zat, put):
                us, _, _ = ahead(rv, [Z[zat(k), :] for k in range(LEV)], None, None)
                _, v, w = back(rv, us, None, None)
                SL[at(0), :] = v
                SL[at(1), :] = w
            each(c, body)
            left(c).start()
        loop(NCH - NB, lambda c: first(NB + c))

        def inner(c):
            four_values(c).wait_recv()

            def body(rv, at, zat, put):
                us, _, _ = ahead(rv, [Z[zat(k), :] for k in range(LEV)], None, None)
                _, v, w = back(rv, us, None, None)
                av, aw = both(rv, four(rv * rv), WR[wide(at, 0), :], WR[wide(at, 1), :])
                v, w = moved(rv, v + av, w + aw)
                OSD[at(0), :] = v + WR[wide(at, 2), :]
                OSD[at(1), :] = w + WR[wide(at, 3), :]
            each(c, body)
            two_values(c).start()
        loop(NB, inner)

        def outer(c):
            two_values(c).wait_recv()

            def body(rv, at, zat, put):
                u, d = ORC[at(0), :], ORC[at(1), :]
                WS[wide(at, 0), :] = u
                WS[wide(at, 1), :] = d
                u, d = moved(rv, u, d)
                us, _, _ = ahead(rv, [Z[zat(k), :] for k in range(LEV)],
                                 u + WR[wide(at, 0), :], d + WR[wide(at, 1), :])
                vs, v, w = back(rv, us, None, None)
                WS[wide(at, 2), :] = v
                WS[wide(at, 3), :] = w
                put(vs)
            each(c, body)
            send_out(c)
        loop(NB, outer)

        def second(c):
            right(c).wait_recv()

            def body(rv, at, zat, put):
                us, _, _ = ahead(rv, [Z[zat(k), :] for k in range(LEV)], FL[at(0), :], FL[at(1), :])
                vs, _, _ = back(rv, us, None, None)
                put(vs)
            each(c, body)
            send_out(c)

        def second_and_rest(i):
            @pl.when(i == CB)
            def _():
                left(None).wait_send()
                loop(NB, lambda c: four_values(c).start())
            second(NB + i)
        loop(NCH - NB, second_and_rest)
        four_values(None).wait_send()
        two_values(None).wait_send()

    def staged(first, second):
        def inner(c):
            def body(rv, at, zat, put):
                us, u, d = ahead(rv, [Z[zat(k), :] for k in range(LEV)], None, None)
                _, v, w = back(rv, us, None, None)
                for val, x in enumerate((u, d, v, w)):
                    WS[wide(at, val), :] = x
            each(c, body)
            four_values(c).start()
        loop(NB, inner)

        def step(i):
            @pl.when(i < NCH)
            def _():
                first(i)

            @pl.when(i >= NB + LAG)
            def _():
                second(i - LAG)
        lax.fori_loop(NB, NCH + LAG, lambda i, carry: (step(i), carry)[1], 0)

        def outer(c):
            four_values(c).wait_recv()

            def body(rv, at, zat, put):
                us, _, _ = ahead(rv, [Z[zat(k), :] for k in range(LEV)], WR[wide(at, 0), :], WR[wide(at, 1), :])
                vs, _, _ = back(rv, us, WR[wide(at, 2), :], WR[wide(at, 3), :])
                put(vs)
            each(c, body)
            send_out(c)
        loop(NB, outer)
        right(None).wait_send()
        left(None).wait_send()
        four_values(None).wait_send()

    @pl.when(lev == 1)
    def _():
        def first(c):
            ready(c)

            right(c).wait_recv()

            def body(rv, at, zat, put):
                us, u, d = ahead(rv, [Z[zat(k), :] for k in range(LEV)], FL[at(0), :], FL[at(1), :])
                for k in range(LEV):
                    Z[zat(k), :] = us[k]
                SR[at(0), :] = u
                SR[at(1), :] = d
            each(c, body)
            right(c).start()

        def second(c):
            left(c).wait_recv()

            def body(rv, at, zat, put):
                q = rv * rv
                q2 = q * q
                e0, e1, e2 = sums_double(q, 4.0, q2 * q2, *four(q))
                u, d = SR[at(0), :], SR[at(1), :]
                v = FR[at(0), :] + rv * (e1 * u + e2 * d)
                w = FR[at(1), :] + rv * (e0 * u + e1 * d)
                vs, v, w = back(rv, [Z[zat(k), :] for k in range(LEV)], v, w)
                SL[at(0), :] = v
                SL[at(1), :] = w
                put(vs)
            each(c, body)
            left(c).start()
            send_out(c)
        staged(first, second)

    @pl.when(lev == 2)
    def _():
        def first(c):
            ready(c)

            left(c).wait_recv()

            def body(rv, at, zat, put):
                us, u, d = ahead(rv, [Z[zat(k), :] for k in range(LEV)], None, None)
                e0, e1, e2 = four(rv * rv)
                v = FR[at(0), :] + rv * (e1 * u + e2 * d)
                w = FR[at(1), :] + rv * (e0 * u + e1 * d)
                _, v, w = back(rv, us, v, w)
                SL[at(0), :] = v
                SL[at(1), :] = w
            each(c, body)
            left(c).start()

        def second(c):
            right(c).wait_recv()

            def body(rv, at, zat, put):
                us, u, d = ahead(rv, [Z[zat(k), :] for k in range(LEV)], FL[at(0), :], FL[at(1), :])
                SR[at(0), :] = u
                SR[at(1), :] = d
                e0, e1, e2 = four(rv * rv)
                v = FR[at(0), :] + rv * (e1 * u + e2 * d)
                w = FR[at(1), :] + rv * (e0 * u + e1 * d)
                vs, _, _ = back(rv, us, v, w)
                put(vs)
            each(c, body)
            right(c).start()
            send_out(c)
        staged(first, second)

    for bg in range(BG):
        all_of(SB, RB, s1_sem, r1_sem, bg).wait_send()
        all_of(RP, RC, s2_sem, r2_sem, bg).wait_send()


def per_device(control, decay_lon, decay_lat, decay_vert):
    lines = control.reshape(LINES, SEG * LANES)
    hbm = pl.BlockSpec(memory_space=pltpu.HBM)
    vmem = pl.BlockSpec(memory_space=pltpu.VMEM)
    f32 = jnp.float32
    dma = pltpu.SemaphoreType.DMA
    filtered = pl.pallas_call(
        kernel,
        out_shape=jax.ShapeDtypeStruct((LINES, SEG * LANES), f32),
        in_specs=[hbm] * 4,
        out_specs=vmem,
        scratch_shapes=[
            pltpu.VMEM((LINES, SEG * LANES), f32),
            pltpu.VMEM((2 * LANES * SEG, LANES), f32),
            pltpu.VMEM((LINES * SEG, LANES), f32),
            pltpu.VMEM((ROWS, SEG * LANES), f32),
            pltpu.VMEM((SEG * ROWS, LANES), f32),
            pltpu.VMEM((8 * LEV * 8, LANES), f32),
            pltpu.VMEM((8 * LANES, LANES), f32),
            pltpu.VMEM((8 * LANES, LANES), f32),
            pltpu.VMEM((1, ROWS), f32),
            pltpu.VMEM((SEG, LANES), f32),
        ] + [pltpu.VMEM((BG * NR * MSG, LANES), f32)] * 4
        + [pltpu.VMEM((NCH * CH, LANES), f32)] * 4
        + [pltpu.VMEM((NB * 2 * CH, LANES), f32)] * 2 + [pltpu.VMEM((NB * CH, LANES), f32)] * 2
        + [dma((LINES // IN,))] + [dma] * 3 + [dma((BG,))] * 4 + [dma] * 2 + [dma((NCH,))] * 2
        + [dma] * 2 + [dma((NB,))] * 2,
        compiler_params=pltpu.CompilerParams(
            collective_id=0, has_side_effects=True, vmem_limit_bytes=50 * 1024 * 1024),
        name="filters",
    )(*[pltpu.with_memory_space_constraint(x, pltpu.HBM) for x in (lines, decay_lon.reshape(1, ROWS), decay_lat.reshape(SEG, LANES), decay_vert)])
    return filtered.reshape(LEV, ROWS, SEG * LANES)


def solution(mesh):
    in_specs = (P("lev", "row", None), P("row"), P(), P("row", None))
    out_specs = P("lev", "row", None)
    return jax.shard_map(
        per_device, mesh=mesh, in_specs=in_specs, out_specs=out_specs, check_vma=False
    )
```

```python
import functools

import jax
import jax.numpy as jnp
from jax import lax
from jax.experimental import pallas as pl
from jax.experimental.pallas import tpu as pltpu
from jax.sharding import PartitionSpec as P

MESH = pl.DeviceIdType.MESH

LANES = 128
SEG = 24
ROWS = 48
LEV = 4
LINES = LEV * ROWS
BG = SEG // 8
NR = 32
MSG = 8
JC = 4
NJ = ROWS // JC
NCH = BG * NJ
CH = 2 * JC * 8
LAG = 6
NB = 4
CB = 22
LB = 16
IN = 48


def gain_sq(r):
    q = r * r
    a = (1.0 - r) * (1.0 + r)
    a2 = a * a
    a4 = a2 * a2
    return jnp.sqrt(a4 * a2 * a / (1.0 + q * (9.0 + q * (9.0 + q))))


def sums_double(q, n, qn, s0, s1, s2):
    return (
        s0 + qn * s0,
        s1 + qn * (s1 + n * s0),
        s2 + qn * (s2 + (2.0 * n) * s1 + (n * n) * s0),
    )


def sums(q, base, doublings):
    s0 = jnp.ones_like(q)
    s1 = jnp.ones_like(q)
    s2 = jnp.ones_like(q)
    qn = q
    for t in range(1, base):
        s0 = s0 + qn
        s1 = s1 + (t + 1.0) * qn
        s2 = s2 + ((t + 1.0) * (t + 1.0)) * qn
        qn = qn * q
    n = float(base)
    for _ in range(doublings):
        s0, s1, s2 = sums_double(q, n, qn, s0, s1, s2)
        qn = qn * qn
        n = 2.0 * n
    return s0, s1, s2


def power(r, base, doublings):
    p = r
    for _ in range(base - 1):
        p = p * r
    for _ in range(doublings):
        p = p * p
    return p


def sublanes():
    return lax.broadcasted_iota(jnp.int32, (8, LANES), 0)


def carry_powers(rn):
    one, two, four = rn, rn * rn, (rn * rn) * (rn * rn)

    def by(idx):
        p = jnp.where(idx % 2 == 1, one, 1.0)
        p = p * jnp.where((idx // 2) % 2 == 1, two, 1.0)
        return p * jnp.where(idx // 4 == 1, four, 1.0)
    return one, two, four, four * four, by(sublanes()), by(7 - sublanes())


def block_carries(us, ds, powers, n, rev):
    r1, r2, r4, r8, up, down = powers
    idx = 7 - sublanes() if rev else sublanes()
    along = down if rev else up
    far = (n * idx.astype(jnp.float32))

    def shifted(x, t):
        return jnp.where(idx >= t, pltpu.roll(x, 8 - t if rev else t, 0), 0.0)

    def last(x):
        row = x[0:1, :] if rev else x[7:8, :]
        return jnp.broadcast_to(row, (8, LANES))

    cu = jnp.zeros((8, LANES), jnp.float32)
    cd = cu
    out = [None] * len(us)
    order = range(len(us))
    for i in (reversed(order) if rev else order):
        u, d = us[i], ds[i]
        for t, rt in ((1, r1), (2, r2), (4, r4)):
            su, sd = shifted(u, t), shifted(d, t)
            u = u + rt * (su + (n * t) * sd)
            d = d + rt * sd
        out[i] = (shifted(u, 1) + along * (cu + far * cd), shifted(d, 1) + along * cd)
        cu, cd = r8 * (cu + (8.0 * n) * cd) + last(u), r8 * cd + last(d)
    return out


def kernel(ctrl, dlon, dlat, dvert, out, X, Y, Z, PI, PV, OS, P1, P2, CI, Q1, Q2, DN, DL,
           SB, RB, RP, RC, SR, SL, FL, FR, WS, WR, OSD, ORC,
           in_sem, pv_sem, dn_sem, dl_sem, s1_sem, r1_sem, s2_sem, r2_sem,
           sr_sem, sl_sem, fl_sem, fr_sem, ws_sem, os_sem, wr_sem, or_sem):
    lev = lax.axis_index("lev")
    me = lax.axis_index("row")
    barrier = pltpu.get_barrier_semaphore()

    def in_copy(i):
        at = pl.ds(pl.multiple_of(i * IN, 8), IN)
        return pltpu.make_async_copy(ctrl.at[at, :], X.at[at, :], in_sem.at[i])

    pv_copy = pltpu.make_async_copy(dvert, PI, pv_sem)
    dn_copy = pltpu.make_async_copy(dlon, DN, dn_sem)
    dl_copy = pltpu.make_async_copy(dlat, DL, dl_sem)

    def loop(n, body, unroll=1):
        def step(i, carry):
            body(i)
            return carry
        lax.fori_loop(0, n, step, 0, unroll=unroll)

    dn_copy.start()
    for i in range(LINES // IN):
        in_copy(i).start()

    def greet(i):
        pl.semaphore_signal(barrier, inc=1, device_id=(lev, lax.rem(me + 11 * (i + 1), NR)), device_id_type=MESH)
    loop(NR - 1, greet, unroll=8)

    for step in (1, 3):
        pl.semaphore_signal(barrier, inc=1, device_id=(lax.rem(lev + step, 4), me), device_id_type=MESH)

    dl_copy.start()
    pv_copy.start()

    zero = jnp.zeros((8, LANES), jnp.float32)
    one = jnp.ones((8, LANES), jnp.float32)
    rest = jnp.zeros((LANES - 96, LANES), jnp.float32)

    for g in range(2):
        for i in range(96 // IN):
            in_copy(g * (96 // IN) + i).wait()

        def turn_in(i, g=g):
            for k in range(8):
                b = 8 * i + k
                tile = X[pl.ds(g * 96, 96), pl.ds(pl.multiple_of(b * LANES, LANES), LANES)]
                Y[pl.ds(g * LANES * SEG + b, LANES, stride=SEG), :] = jnp.concatenate([tile, rest]).T
        loop(SEG // 8, turn_in)

    dn_copy.wait()
    line = DN[...]
    line = jnp.concatenate([line, line, line[:, :32]], axis=1)
    r = jnp.broadcast_to(line, (8, LANES))
    chains = [(g, bg) for g in range(2) for bg in range(BG)]
    BLK = 8

    def at_lon(g, bg, l):
        return pl.ds(pl.multiple_of((g * LANES + l) * SEG + bg * 8, 8), 8)

    def at_step(l):
        return pl.ds(pl.multiple_of(l * 8, 8), 8)

    def lon_ends(i, state):
        p, pp, rest = state
        rest = list(rest)
        l0 = 2 * i
        xs = [[Y[at_lon(g, bg, l0 + q), :] for g, bg in chains] for q in range(2)]
        for q in range(2):
            P1[at_step(l0 + q), :] = p
            P2[at_step(l0 + q), :] = pp
            for k in range(len(chains)):
                u, d, v, w = rest[k]
                d = r * d + xs[q][k]
                u = r * u + d
                xs[q][k] = u
                rest[k] = (u, d, v + pp * u, w + p * u)
            p = r * p
            pp = r * pp + p
        for q in range(2):
            for k, (g, bg) in enumerate(chains):
                Y[at_lon(g, bg, l0 + q), :] = xs[q][k]
        return (p, pp, tuple(rest))

    init = (one, one, tuple((zero, zero, zero, zero) for _ in chains))
    _, _, ends = lax.fori_loop(0, LANES // 2, lon_ends, init, unroll=2)

    s0, s1, s2 = sums(r * r, 1, 7)
    lon_powers = carry_powers(power(r, 1, 7))
    n = float(LANES)

    def carry_at(g, bg, val):
        return slice(((g * BG + bg) * 4 + val) * 8, ((g * BG + bg) * 4 + val) * 8 + 8)

    for g in range(2):
        of = [ends[g * BG + bg] for bg in range(BG)]
        states = block_carries([e[0] for e in of], [e[1] for e in of], lon_powers, n, False)
        vs = [e[2] + r * (s1 * u + s2 * d) for e, (u, d) in zip(of, states)]
        ws = [e[3] + r * (s0 * u + s1 * d) for e, (u, d) in zip(of, states)]
        backs = block_carries(vs, ws, lon_powers, n, True)
        for bg in range(BG):
            for val, x in enumerate(states[bg] + backs[bg]):
                CI[carry_at(g, bg, val), :] = x

    g_lon = gain_sq(r)
    r_pow = [r, r * r, r * r * r, (r * r) * (r * r)]
    r_lin = [(m + 1.0) * r_pow[m] for m in range(4)]

    def at_lat(k, j, bg):
        return pl.ds(pl.multiple_of((k * ROWS + j) * SEG + bg * 8, 8), 8)

    def slot(ref, bg, i):
        return ref.at[pl.ds(pl.multiple_of((bg * NR + i) * MSG, 8), 4), :]

    def send(src, dst, ssem, rsem, bg):
        def to(i):
            p = lax.rem(me + 11 * (i + 1), NR)
            pltpu.make_async_remote_copy(
                src_ref=slot(src, bg, p), dst_ref=slot(dst, bg, me), send_sem=ssem.at[bg],
                recv_sem=rsem.at[bg], device_id=(lev, p), device_id_type=MESH).start()
        loop(NR - 1, to, unroll=8)
        at = pl.ds(pl.multiple_of((bg * NR + me) * MSG, 8), 4)
        dst[at, :] = src[at, :]

    def all_of(src, dst, ssem, rsem, bg):
        at = pl.ds(pl.multiple_of(bg * NR * MSG, 8), (NR - 1) * 4)
        return pltpu.make_async_remote_copy(
            src_ref=src.at[at, :], dst_ref=dst.at[at, :], send_sem=ssem.at[bg], recv_sem=rsem.at[bg],
            device_id=(lev, lax.rem(me + 1, NR)), device_id_type=MESH)

    for bg in range(BG):
        came = [(r * CI[carry_at(g, bg, 0), :], r * CI[carry_at(g, bg, 1), :]) for g in range(2)]

        def lon_back(i, state, bg=bg, came=came):
            l0 = LANES - LB * (i + 1)
            xs = [[Y[at_lon(g, bg, l0 + q), :] for g in range(2)] for q in range(LB)]
            state = list(state)
            for top in range(LB - 1, -1, -4):
                loc = [None, None]
                for m in range(4):
                    q = top - m
                    p, pp = P1[at_step(l0 + q), :], P2[at_step(l0 + q), :]
                    for g in range(2):
                        w = xs[q][g] + (p * came[g][0] + pp * came[g][1])
                        v = w
                        if m:
                            w = r * loc[g][1] + w
                            v = r * loc[g][0] + w
                        loc[g] = (v, w)
                        xs[q][g] = v
                for g in range(2):
                    v, w = state[g]
                    for m in range(4):
                        q = top - m
                        xs[q][g] = xs[q][g] + (r_pow[m] * v + r_lin[m] * w)
                    state[g] = (xs[top - 3][g], loc[g][1] + r_pow[3] * w)
            for q in range(LB):
                for g in range(2):
                    Y[at_lon(g, bg, l0 + q), :] = xs[q][g] * g_lon
            return tuple(state)

        lax.fori_loop(0, LANES // LB, lon_back, tuple((CI[carry_at(g, bg, 2), :], CI[carry_at(g, bg, 3), :]) for g in range(2)))

        def turn_out(i, bg=bg):
            for q in range(4):
                b = bg * 8 + i * 4 + q
                for g in range(2):
                    tile = Y[pl.ds(g * LANES * SEG + b, LANES, stride=SEG), :].T
                    for k in range(2):
                        Z[pl.ds((2 * g + k) * ROWS * SEG + b, ROWS, stride=SEG), :] = tile[k * ROWS:(k + 1) * ROWS, :]
        loop(2, turn_out)

        if bg == 0:
            dl_copy.wait()
        rl = DL[bg * 8:(bg + 1) * 8, :]

        def lat_ends(i, state, rl=rl, bg=bg):
            p, pp, rest = state
            rest = list(rest)
            xs = [[Z[at_lat(k, 4 * i + q, bg), :] for k in range(LEV)] for q in range(4)]
            for q in range(4):
                Q1[at_lat(0, 4 * i + q, bg), :] = p
                Q2[at_lat(0, 4 * i + q, bg), :] = pp
                for k in range(LEV):
                    u, d, v, w = rest[k]
                    d = rl * d + xs[q][k]
                    u = rl * u + d
                    xs[q][k] = u
                    rest[k] = (u, d, v + pp * u, w + p * u)
                p = rl * p
                pp = rl * pp + p
            for q in range(4):
                for k in range(LEV):
                    Z[at_lat(k, 4 * i + q, bg), :] = xs[q][k]
            return (p, pp, tuple(rest))

        init = (one, one, tuple((zero, zero, zero, zero) for _ in range(LEV)))
        _, _, ends = lax.fori_loop(0, ROWS // 4, lat_ends, init)
        for k in range(LEV):
            for val in range(4):
                SB[pl.ds((bg * NR + k * 8) * MSG + val, 8, stride=MSG), :] = ends[k][val]
        if bg == 0:
            pl.semaphore_wait(barrier, NR - 1 + 2)
        send(SB, RB, s1_sem, r1_sem, bg)

    pv_copy.wait()

    def place(b):
        for q in range(ROWS // 8):
            PV[pl.ds(pl.multiple_of(b * ROWS + q * 8, 8), 8), :] = PI[
                q * 8:(q + 1) * 8, pl.ds(pl.multiple_of(b * LANES, LANES), LANES)]
    loop(SEG, place, unroll=2)

    m = float(ROWS)
    for bg in range(BG):
        ro = jnp.broadcast_to(DL[pl.ds(bg * 8 + lax.rem(me, 8), 1), :], (8, LANES))
        o0, o1, o2 = sums(ro * ro, 3, 4)
        own_powers = carry_powers(power(ro, 3, 4))
        all_of(SB, RB, s1_sem, r1_sem, bg).wait_recv()

        def rows_of(q, val, bg=bg):
            return pl.ds((bg * NR + q * 8) * MSG + val, 8, stride=MSG)

        def had(val):
            return [RB[rows_of(q, val), :] for q in range(NR // 8)]
        states = block_carries(had(0), had(1), own_powers, m, False)
        vs = [e + ro * (o1 * u + o2 * d) for e, (u, d) in zip(had(2), states)]
        ws = [e + ro * (o0 * u + o1 * d) for e, (u, d) in zip(had(3), states)]
        backs = block_carries(vs, ws, own_powers, m, True)
        for q in range(NR // 8):
            RP[rows_of(q, 0), :], RP[rows_of(q, 1), :] = states[q]
            RP[rows_of(q, 2), :], RP[rows_of(q, 3), :] = backs[q]
        send(RP, RC, s2_sem, r2_sem, bg)

    def lat_finish(bg):
        all_of(RP, RC, s2_sem, r2_sem, bg).wait_recv()
        rl = DL[pl.ds(pl.multiple_of(bg * 8, 8), 8), :]
        g_lat = gain_sq(rl)

        def come(k, val):
            return RC[pl.ds((bg * NR + k * 8) * MSG + val, 8, stride=MSG), :]

        came = [(rl * come(k, 0), rl * come(k, 1)) for k in range(LEV)]

        def lat_back(i, state):
            j0 = ROWS - 4 - i * 4
            xs = [[Z[at_lat(k, j0 + q, bg), :] for k in range(LEV)] for q in range(4)]
            state = list(state)
            for q in range(4 - 1, -1, -1):
                p, pp = Q1[at_lat(0, j0 + q, bg), :], Q2[at_lat(0, j0 + q, bg), :]
                for k in range(LEV):
                    v, w = state[k]
                    w = rl * w + (xs[q][k] + (p * came[k][0] + pp * came[k][1]))
                    v = rl * v + w
                    state[k] = (v, w)
                    xs[q][k] = v * g_lat
            for q in range(4):
                for k in range(LEV):
                    Z[at_lat(k, j0 + q, bg), :] = xs[q][k]
            return tuple(state)
        lax.fori_loop(0, ROWS // 4, lat_back, tuple((come(k, 2), come(k, 3)) for k in range(LEV)))


    def chunk(ref, c):
        return ref.at[NB * CH:, :] if c is None else ref.at[pl.ds(pl.multiple_of(c * CH, 8), CH), :]

    def one_of(sem, c):
        return sem.at[0 if c is None else c]

    def one_from(sem, c):
        return sem.at[0 if c is None else c - NB]

    def right(c):
        return pltpu.make_async_remote_copy(
            src_ref=chunk(SR, c), dst_ref=chunk(FL, c), send_sem=sr_sem, recv_sem=one_from(fl_sem, c),
            device_id=(lax.rem(lev + 1, 4), me), device_id_type=MESH)

    def left(c):
        return pltpu.make_async_remote_copy(
            src_ref=chunk(SL, c), dst_ref=chunk(FR, c), send_sem=sl_sem, recv_sem=one_from(fr_sem, c),
            device_id=(lax.rem(lev + 3, 4), me), device_id_type=MESH)

    def four_values(c):
        at = pl.ds(0, NB * 2 * CH) if c is None else pl.ds(pl.multiple_of(c * 2 * CH, 8), 2 * CH)
        return pltpu.make_async_remote_copy(
            src_ref=WS.at[at, :], dst_ref=WR.at[at, :], send_sem=ws_sem, recv_sem=one_of(wr_sem, c),
            device_id=(lev + 1 - 2 * lax.rem(lev, 2), me), device_id_type=MESH)

    def two_values(c):
        at = pl.ds(0, NB * CH) if c is None else pl.ds(pl.multiple_of(c * CH, 8), CH)
        return pltpu.make_async_remote_copy(
            src_ref=OSD.at[at, :], dst_ref=ORC.at[at, :], send_sem=os_sem, recv_sem=one_of(or_sem, c),
            device_id=(3 - lev, me), device_id_type=MESH)

    def each(c, body):
        bg = c // NJ
        j0 = lax.rem(c, NJ) * JC
        for jj in range(JC):
            j = j0 + jj
            rv = PV[pl.ds(bg * 8 * ROWS + j, 8, stride=ROWS), :]

            def at(val, jj=jj, pitch=CH):
                return pl.ds(pl.multiple_of(c * pitch + (val * JC + jj) * 8, 8), 8)

            def zat(k, j=j):
                return pl.ds(pl.multiple_of((k * ROWS + j) * SEG + bg * 8, 8), 8)

            def put(vals, rv=rv, j=j):
                gv = gain_sq(rv)
                for k in range(LEV):
                    OS[pl.ds(k * 8 + lax.rem(j, 8), 8, stride=LEV * 8), :] = vals[k] * gv
            body(rv, at, zat, put)

    def ahead(rv, xs, u, d):
        us = []
        for x in xs:
            d = x if d is None else rv * d + x
            u = d if u is None else rv * u + d
            us.append(u)
        return us, u, d

    def back(rv, us, v, w):
        vs = [None] * LEV
        for k in range(LEV - 1, -1, -1):
            w = us[k] if w is None else rv * w + us[k]
            v = w if v is None else rv * v + w
            vs[k] = v
        return vs, v, w

    def four(q):
        return (1.0 + q * (1.0 + q * (1.0 + q)),
                1.0 + q * (2.0 + q * (3.0 + 4.0 * q)),
                1.0 + q * (4.0 + q * (9.0 + 16.0 * q)))

    def send_out(c):
        @pl.when(lax.rem(c, 2) == 1)
        def _():
            bg = c // NJ
            j0 = lax.rem(c - 1, NJ) * JC
            for k in range(LEV):
                for b in range(8):
                    out[pl.ds(pl.multiple_of(k * ROWS + j0, 8), 8),
                        pl.ds(pl.multiple_of((bg * 8 + b) * LANES, LANES), LANES)] = OS[
                            (b * LEV + k) * 8:(b * LEV + k + 1) * 8, :]

    def wide(at, val):
        return at(val, pitch=2 * CH)

    def moved(rv, first, second):
        r2 = rv * rv
        r4 = r2 * r2
        return r4 * (first + 4.0 * second), r4 * second

    def both(rv, sums3, u, d):
        e0, e1, e2 = sums3
        return rv * (e1 * u + e2 * d), rv * (e0 * u + e1 * d)

    def ready(c):
        @pl.when(lax.rem(c, NJ) == 0)
        def _():
            lat_finish(c // NJ)

    lat_finish(0)

    @pl.when(lev == 0)
    def _():
        def first(c):
            ready(c)

            def body(rv, at, zat, put):
                us, u, d = ahead(rv, [Z[zat(k), :] for k in range(LEV)], None, None)
                for k in range(LEV):
                    Z[zat(k), :] = us[k]
                SR[at(0), :] = u
                SR[at(1), :] = d
            each(c, body)
            right(c).start()
        loop(NCH - NB, lambda c: first(NB + c))

        def inner(c):
            four_values(c).wait_recv()

            def body(rv, at, zat, put):
                us, u, d = ahead(rv, [Z[zat(k), :] for k in range(LEV)], None, None)
                for k in range(LEV):
                    Z[zat(k), :] = us[k]
                WS[wide(at, 0), :] = u
                WS[wide(at, 1), :] = d
                u, d = moved(rv, u, d)
                OSD[at(0), :] = u + WR[wide(at, 0), :]
                OSD[at(1), :] = d + WR[wide(at, 1), :]
            each(c, body)
            two_values(c).start()
        loop(NB, inner)

        def outer(c):
            two_values(c).wait_recv()

            def body(rv, at, zat, put):
                q = rv * rv
                q2 = q * q
                av, aw = both(rv, sums_double(q, 4.0, q2 * q2, *four(q)), OSD[at(0), :], OSD[at(1), :])
                v, w = ORC[at(0), :] + av, ORC[at(1), :] + aw
                WS[wide(at, 2), :] = v
                WS[wide(at, 3), :] = w
                v, w = moved(rv, v, w)
                av, aw = both(rv, four(q), WS[wide(at, 0), :], WS[wide(at, 1), :])
                v = v + av + WR[wide(at, 2), :]
                w = w + aw + WR[wide(at, 3), :]
                vs, _, _ = back(rv, [Z[zat(k), :] for k in range(LEV)], v, w)
                put(vs)
            each(c, body)
            send_out(c)
        loop(NB, outer)

        def second(c):
            left(c).wait_recv()

            def body(rv, at, zat, put):
                vs, _, _ = back(rv, [Z[zat(k), :] for k in range(LEV)], FR[at(0), :], FR[at(1), :])
                put(vs)
            each(c, body)
            send_out(c)

        def second_and_rest(i):
            @pl.when(i == CB)
            def _():
                right(None).wait_send()
                loop(NB, lambda c: four_values(c).start())
            second(NB + i)
        loop(NCH - NB, second_and_rest)
        four_values(None).wait_send()
        two_values(None).wait_send()

    @pl.when(lev == 3)
    def _():
        def first(c):
            ready(c)

            def body(rv, at, zat, put):
                us, _, _ = ahead(rv, [Z[zat(k), :] for k in range(LEV)], None, None)
                _, v, w = back(rv, us, None, None)
                SL[at(0), :] = v
                SL[at(1), :] = w
            each(c, body)
            left(c).start()
        loop(NCH - NB, lambda c: first(NB + c))

        def inner(c):
            four_values(c).wait_recv()

            def body(rv, at, zat, put):
                us, _, _ = ahead(rv, [Z[zat(k), :] for k in range(LEV)], None, None)
                _, v, w = back(rv, us, None, None)
                av, aw = both(rv, four(rv * rv), WR[wide(at, 0), :], WR[wide(at, 1), :])
                v, w = moved(rv, v + av, w + aw)
                OSD[at(0), :] = v + WR[wide(at, 2), :]
                OSD[at(1), :] = w + WR[wide(at, 3), :]
            each(c, body)
            two_values(c).start()
        loop(NB, inner)

        def outer(c):
            two_values(c).wait_recv()

            def body(rv, at, zat, put):
                u, d = ORC[at(0), :], ORC[at(1), :]
                WS[wide(at, 0), :] = u
                WS[wide(at, 1), :] = d
                u, d = moved(rv, u, d)
                us, _, _ = ahead(rv, [Z[zat(k), :] for k in range(LEV)],
                                 u + WR[wide(at, 0), :], d + WR[wide(at, 1), :])
                vs, v, w = back(rv, us, None, None)
                WS[wide(at, 2), :] = v
                WS[wide(at, 3), :] = w
                put(vs)
            each(c, body)
            send_out(c)
        loop(NB, outer)

        def second(c):
            right(c).wait_recv()

            def body(rv, at, zat, put):
                us, _, _ = ahead(rv, [Z[zat(k), :] for k in range(LEV)], FL[at(0), :], FL[at(1), :])
                vs, _, _ = back(rv, us, None, None)
                put(vs)
            each(c, body)
            send_out(c)

        def second_and_rest(i):
            @pl.when(i == CB)
            def _():
                left(None).wait_send()
                loop(NB, lambda c: four_values(c).start())
            second(NB + i)
        loop(NCH - NB, second_and_rest)
        four_values(None).wait_send()
        two_values(None).wait_send()

    def staged(first, second):
        def inner(c):
            def body(rv, at, zat, put):
                us, u, d = ahead(rv, [Z[zat(k), :] for k in range(LEV)], None, None)
                _, v, w = back(rv, us, None, None)
                for val, x in enumerate((u, d, v, w)):
                    WS[wide(at, val), :] = x
            each(c, body)
            four_values(c).start()
        loop(NB, inner)

        def step(i):
            @pl.when(i < NCH)
            def _():
                first(i)

            @pl.when(i >= NB + LAG)
            def _():
                second(i - LAG)
        lax.fori_loop(NB, NCH + LAG, lambda i, carry: (step(i), carry)[1], 0)

        def outer(c):
            four_values(c).wait_recv()

            def body(rv, at, zat, put):
                us, _, _ = ahead(rv, [Z[zat(k), :] for k in range(LEV)], WR[wide(at, 0), :], WR[wide(at, 1), :])
                vs, _, _ = back(rv, us, WR[wide(at, 2), :], WR[wide(at, 3), :])
                put(vs)
            each(c, body)
            send_out(c)
        loop(NB, outer)
        right(None).wait_send()
        left(None).wait_send()
        four_values(None).wait_send()

    @pl.when(lev == 1)
    def _():
        def first(c):
            ready(c)

            right(c).wait_recv()

            def body(rv, at, zat, put):
                us, u, d = ahead(rv, [Z[zat(k), :] for k in range(LEV)], FL[at(0), :], FL[at(1), :])
                for k in range(LEV):
                    Z[zat(k), :] = us[k]
                SR[at(0), :] = u
                SR[at(1), :] = d
            each(c, body)
            right(c).start()

        def second(c):
            left(c).wait_recv()

            def body(rv, at, zat, put):
                q = rv * rv
                q2 = q * q
                e0, e1, e2 = sums_double(q, 4.0, q2 * q2, *four(q))
                u, d = SR[at(0), :], SR[at(1), :]
                v = FR[at(0), :] + rv * (e1 * u + e2 * d)
                w = FR[at(1), :] + rv * (e0 * u + e1 * d)
                vs, v, w = back(rv, [Z[zat(k), :] for k in range(LEV)], v, w)
                SL[at(0), :] = v
                SL[at(1), :] = w
                put(vs)
            each(c, body)
            left(c).start()
            send_out(c)
        staged(first, second)

    @pl.when(lev == 2)
    def _():
        def first(c):
            ready(c)

            left(c).wait_recv()

            def body(rv, at, zat, put):
                us, u, d = ahead(rv, [Z[zat(k), :] for k in range(LEV)], None, None)
                e0, e1, e2 = four(rv * rv)
                v = FR[at(0), :] + rv * (e1 * u + e2 * d)
                w = FR[at(1), :] + rv * (e0 * u + e1 * d)
                _, v, w = back(rv, us, v, w)
                SL[at(0), :] = v
                SL[at(1), :] = w
            each(c, body)
            left(c).start()

        def second(c):
            right(c).wait_recv()

            def body(rv, at, zat, put):
                us, u, d = ahead(rv, [Z[zat(k), :] for k in range(LEV)], FL[at(0), :], FL[at(1), :])
                SR[at(0), :] = u
                SR[at(1), :] = d
                e0, e1, e2 = four(rv * rv)
                v = FR[at(0), :] + rv * (e1 * u + e2 * d)
                w = FR[at(1), :] + rv * (e0 * u + e1 * d)
                vs, _, _ = back(rv, us, v, w)
                put(vs)
            each(c, body)
            right(c).start()
            send_out(c)
        staged(first, second)

    for bg in range(BG):
        all_of(SB, RB, s1_sem, r1_sem, bg).wait_send()
        all_of(RP, RC, s2_sem, r2_sem, bg).wait_send()


def per_device(control, decay_lon, decay_lat, decay_vert):
    lines = control.reshape(LINES, SEG * LANES)
    hbm = pl.BlockSpec(memory_space=pltpu.HBM)
    vmem = pl.BlockSpec(memory_space=pltpu.VMEM)
    f32 = jnp.float32
    dma = pltpu.SemaphoreType.DMA
    filtered = pl.pallas_call(
        kernel,
        out_shape=jax.ShapeDtypeStruct((LINES, SEG * LANES), f32),
        in_specs=[hbm] * 4,
        out_specs=vmem,
        scratch_shapes=[
            pltpu.VMEM((LINES, SEG * LANES), f32),
            pltpu.VMEM((2 * LANES * SEG, LANES), f32),
            pltpu.VMEM((LINES * SEG, LANES), f32),
            pltpu.VMEM((ROWS, SEG * LANES), f32),
            pltpu.VMEM((SEG * ROWS, LANES), f32),
            pltpu.VMEM((8 * LEV * 8, LANES), f32),
            pltpu.VMEM((8 * LANES, LANES), f32),
            pltpu.VMEM((8 * LANES, LANES), f32),
            pltpu.VMEM((2 * BG * 4 * 8, LANES), f32),
            pltpu.VMEM((ROWS * SEG, LANES), f32),
            pltpu.VMEM((ROWS * SEG, LANES), f32),
            pltpu.VMEM((1, ROWS), f32),
            pltpu.VMEM((SEG, LANES), f32),
        ] + [pltpu.VMEM((BG * NR * MSG, LANES), f32)] * 4
        + [pltpu.VMEM((NCH * CH, LANES), f32)] * 4
        + [pltpu.VMEM((NB * 2 * CH, LANES), f32)] * 2 + [pltpu.VMEM((NB * CH, LANES), f32)] * 2
        + [dma((LINES // IN,))] + [dma] * 3 + [dma((BG,))] * 4 + [dma] * 2 + [dma((NCH - NB,))] * 2
        + [dma] * 2 + [dma((NB,))] * 2,
        compiler_params=pltpu.CompilerParams(
            collective_id=0, has_side_effects=True, vmem_limit_bytes=50 * 1024 * 1024),
        name="filters",
    )(*[pltpu.with_memory_space_constraint(x, pltpu.HBM) for x in (lines, decay_lon.reshape(1, ROWS), decay_lat.reshape(SEG, LANES), decay_vert)])
    return filtered.reshape(LEV, ROWS, SEG * LANES)


def solution(mesh):
    in_specs = (P("lev", "row", None), P("row"), P(), P("row", None))
    out_specs = P("lev", "row", None)
    return jax.shard_map(
        per_device, mesh=mesh, in_specs=in_specs, out_specs=out_specs, check_vma=False
    )
```

```python
import functools

import jax
import jax.numpy as jnp
from jax import lax
from jax.experimental import pallas as pl
from jax.experimental.pallas import tpu as pltpu
from jax.sharding import PartitionSpec as P

MESH = pl.DeviceIdType.MESH

LANES = 128
SEG = 24
ROWS = 48
LEV = 4
LINES = LEV * ROWS
BG = SEG // 8
NR = 32
MSG = 8
JC = 4
NJ = ROWS // JC
NCH = BG * NJ
CH = 2 * JC * 8
LAG = 6
NB = 4
CB = 22
LB = 16
IN = 48


def gain_sq(r):
    q = r * r
    a = (1.0 - r) * (1.0 + r)
    a2 = a * a
    a4 = a2 * a2
    return jnp.sqrt(a4 * a2 * a / (1.0 + q * (9.0 + q * (9.0 + q))))


def sums_double(q, n, qn, s0, s1, s2):
    return (
        s0 + qn * s0,
        s1 + qn * (s1 + n * s0),
        s2 + qn * (s2 + (2.0 * n) * s1 + (n * n) * s0),
    )


def sums(q, base, doublings):
    s0 = jnp.ones_like(q)
    s1 = jnp.ones_like(q)
    s2 = jnp.ones_like(q)
    qn = q
    for t in range(1, base):
        s0 = s0 + qn
        s1 = s1 + (t + 1.0) * qn
        s2 = s2 + ((t + 1.0) * (t + 1.0)) * qn
        qn = qn * q
    n = float(base)
    for _ in range(doublings):
        s0, s1, s2 = sums_double(q, n, qn, s0, s1, s2)
        qn = qn * qn
        n = 2.0 * n
    return s0, s1, s2


def power(r, base, doublings):
    p = r
    for _ in range(base - 1):
        p = p * r
    for _ in range(doublings):
        p = p * p
    return p


def sublanes():
    return lax.broadcasted_iota(jnp.int32, (8, LANES), 0)


def carry_powers(rn):
    one, two, four = rn, rn * rn, (rn * rn) * (rn * rn)

    def by(idx):
        p = jnp.where(idx % 2 == 1, one, 1.0)
        p = p * jnp.where((idx // 2) % 2 == 1, two, 1.0)
        return p * jnp.where(idx // 4 == 1, four, 1.0)
    return one, two, four, four * four, by(sublanes()), by(7 - sublanes())


def block_carries(us, ds, powers, n, rev):
    r1, r2, r4, r8, up, down = powers
    idx = 7 - sublanes() if rev else sublanes()
    along = down if rev else up
    far = (n * idx.astype(jnp.float32))

    def shifted(x, t):
        return jnp.where(idx >= t, pltpu.roll(x, 8 - t if rev else t, 0), 0.0)

    def last(x):
        row = x[0:1, :] if rev else x[7:8, :]
        return jnp.broadcast_to(row, (8, LANES))

    cu = jnp.zeros((8, LANES), jnp.float32)
    cd = cu
    out = [None] * len(us)
    order = range(len(us))
    for i in (reversed(order) if rev else order):
        u, d = us[i], ds[i]
        for t, rt in ((1, r1), (2, r2), (4, r4)):
            su, sd = shifted(u, t), shifted(d, t)
            u = u + rt * (su + (n * t) * sd)
            d = d + rt * sd
        out[i] = (shifted(u, 1) + along * (cu + far * cd), shifted(d, 1) + along * cd)
        cu, cd = r8 * (cu + (8.0 * n) * cd) + last(u), r8 * cd + last(d)
    return out


def kernel(ctrl, dlon, dlat, dvert, out, X, Y, Z, PI, PV, OS, P1, P2, CI, Q1, Q2, DN, DL,
           SB, RB, RP, RC, SR, SL, FL, FR, WS, WR, OSD, ORC,
           in_sem, pv_sem, dn_sem, dl_sem, s1_sem, r1_sem, s2_sem, r2_sem,
           sr_sem, sl_sem, fl_sem, fr_sem, ws_sem, os_sem, wr_sem, or_sem):
    lev = lax.axis_index("lev")
    me = lax.axis_index("row")
    barrier = pltpu.get_barrier_semaphore()

    def in_copy(i):
        at = pl.ds(pl.multiple_of(i * IN, 8), IN)
        return pltpu.make_async_copy(ctrl.at[at, :], X.at[at, :], in_sem.at[i])

    pv_copy = pltpu.make_async_copy(dvert, PI, pv_sem)
    dn_copy = pltpu.make_async_copy(dlon, DN, dn_sem)
    dl_copy = pltpu.make_async_copy(dlat, DL, dl_sem)

    def loop(n, body, unroll=1):
        def step(i, carry):
            body(i)
            return carry
        lax.fori_loop(0, n, step, 0, unroll=unroll)

    dn_copy.start()
    for i in range(LINES // IN):
        in_copy(i).start()

    def greet(i):
        pl.semaphore_signal(barrier, inc=1, device_id=(lev, lax.rem(me + 11 * (i + 1), NR)), device_id_type=MESH)
    loop(NR - 1, greet, unroll=8)

    for step in (1, 3):
        pl.semaphore_signal(barrier, inc=1, device_id=(lax.rem(lev + step, 4), me), device_id_type=MESH)

    dl_copy.start()
    pv_copy.start()

    zero = jnp.zeros((8, LANES), jnp.float32)
    one = jnp.ones((8, LANES), jnp.float32)
    rest = jnp.zeros((LANES - 96, LANES), jnp.float32)

    for g in range(2):
        for i in range(96 // IN):
            in_copy(g * (96 // IN) + i).wait()

        def turn_in(i, g=g):
            for k in range(8):
                b = 8 * i + k
                tile = X[pl.ds(g * 96, 96), pl.ds(pl.multiple_of(b * LANES, LANES), LANES)]
                Y[pl.ds(g * LANES * SEG + b, LANES, stride=SEG), :] = jnp.concatenate([tile, rest]).T
        loop(SEG // 8, turn_in)

    dn_copy.wait()
    line = DN[...]
    line = jnp.concatenate([line, line, line[:, :32]], axis=1)
    r = jnp.broadcast_to(line, (8, LANES))
    chains = [(g, bg) for g in range(2) for bg in range(BG)]
    BLK = 8

    def at_lon(g, bg, l):
        return pl.ds(pl.multiple_of((g * LANES + l) * SEG + bg * 8, 8), 8)

    def at_step(l):
        return pl.ds(pl.multiple_of(l * 8, 8), 8)

    def lon_ends(i, state):
        p, pp, rest = state
        rest = list(rest)
        l0 = 2 * i
        xs = [[Y[at_lon(g, bg, l0 + q), :] for g, bg in chains] for q in range(2)]
        for q in range(2):
            P1[at_step(l0 + q), :] = p
            P2[at_step(l0 + q), :] = pp
            for k in range(len(chains)):
                u, d, v, w = rest[k]
                d = r * d + xs[q][k]
                u = r * u + d
                xs[q][k] = u
                rest[k] = (u, d, v + pp * u, w + p * u)
            p = r * p
            pp = r * pp + p
        for q in range(2):
            for k, (g, bg) in enumerate(chains):
                Y[at_lon(g, bg, l0 + q), :] = xs[q][k]
        return (p, pp, tuple(rest))

    init = (one, one, tuple((zero, zero, zero, zero) for _ in chains))
    _, _, ends = lax.fori_loop(0, LANES // 2, lon_ends, init, unroll=4)

    s0, s1, s2 = sums(r * r, 1, 7)
    lon_powers = carry_powers(power(r, 1, 7))
    n = float(LANES)

    def carry_at(g, bg, val):
        return slice(((g * BG + bg) * 4 + val) * 8, ((g * BG + bg) * 4 + val) * 8 + 8)

    for g in range(2):
        of = [ends[g * BG + bg] for bg in range(BG)]
        states = block_carries([e[0] for e in of], [e[1] for e in of], lon_powers, n, False)
        vs = [e[2] + r * (s1 * u + s2 * d) for e, (u, d) in zip(of, states)]
        ws = [e[3] + r * (s0 * u + s1 * d) for e, (u, d) in zip(of, states)]
        backs = block_carries(vs, ws, lon_powers, n, True)
        for bg in range(BG):
            for val, x in enumerate(states[bg] + backs[bg]):
                CI[carry_at(g, bg, val), :] = x

    g_lon = gain_sq(r)
    r_pow = [r, r * r, r * r * r, (r * r) * (r * r)]
    r_lin = [(m + 1.0) * r_pow[m] for m in range(4)]

    def at_lat(k, j, bg):
        return pl.ds(pl.multiple_of((k * ROWS + j) * SEG + bg * 8, 8), 8)

    def slot(ref, bg, i):
        return ref.at[pl.ds(pl.multiple_of((bg * NR + i) * MSG, 8), 4), :]

    def send(src, dst, ssem, rsem, bg):
        def to(i):
            p = lax.rem(me + 11 * (i + 1), NR)
            pltpu.make_async_remote_copy(
                src_ref=slot(src, bg, p), dst_ref=slot(dst, bg, me), send_sem=ssem.at[bg],
                recv_sem=rsem.at[bg], device_id=(lev, p), device_id_type=MESH).start()
        loop(NR - 1, to, unroll=31)
        at = pl.ds(pl.multiple_of((bg * NR + me) * MSG, 8), 4)
        dst[at, :] = src[at, :]

    def all_of(src, dst, ssem, rsem, bg):
        at = pl.ds(pl.multiple_of(bg * NR * MSG, 8), (NR - 1) * 4)
        return pltpu.make_async_remote_copy(
            src_ref=src.at[at, :], dst_ref=dst.at[at, :], send_sem=ssem.at[bg], recv_sem=rsem.at[bg],
            device_id=(lev, lax.rem(me + 1, NR)), device_id_type=MESH)

    for bg in range(BG):
        came = [(r * CI[carry_at(g, bg, 0), :], r * CI[carry_at(g, bg, 1), :]) for g in range(2)]

        def lon_back(i, state, bg=bg, came=came):
            l0 = LANES - LB * (i + 1)
            xs = [[Y[at_lon(g, bg, l0 + q), :] for g in range(2)] for q in range(LB)]
            state = list(state)
            for top in range(LB - 1, -1, -4):
                loc = [None, None]
                for m in range(4):
                    q = top - m
                    p, pp = P1[at_step(l0 + q), :], P2[at_step(l0 + q), :]
                    for g in range(2):
                        w = xs[q][g] + (p * came[g][0] + pp * came[g][1])
                        v = w
                        if m:
                            w = r * loc[g][1] + w
                            v = r * loc[g][0] + w
                        loc[g] = (v, w)
                        xs[q][g] = v
                for g in range(2):
                    v, w = state[g]
                    for m in range(4):
                        q = top - m
                        xs[q][g] = xs[q][g] + (r_pow[m] * v + r_lin[m] * w)
                    state[g] = (xs[top - 3][g], loc[g][1] + r_pow[3] * w)
            for q in range(LB):
                for g in range(2):
                    Y[at_lon(g, bg, l0 + q), :] = xs[q][g] * g_lon
            return tuple(state)

        lax.fori_loop(0, LANES // LB, lon_back, tuple((CI[carry_at(g, bg, 2), :], CI[carry_at(g, bg, 3), :]) for g in range(2)))

        def turn_out(i, bg=bg):
            for q in range(4):
                b = bg * 8 + i * 4 + q
                for g in range(2):
                    tile = Y[pl.ds(g * LANES * SEG + b, LANES, stride=SEG), :].T
                    for k in range(2):
                        Z[pl.ds((2 * g + k) * ROWS * SEG + b, ROWS, stride=SEG), :] = tile[k * ROWS:(k + 1) * ROWS, :]
        loop(2, turn_out, unroll=2)

        if bg == 0:
            dl_copy.wait()
        rl = DL[bg * 8:(bg + 1) * 8, :]

        def lat_ends(i, state, rl=rl, bg=bg):
            p, pp, rest = state
            rest = list(rest)
            xs = [[Z[at_lat(k, 4 * i + q, bg), :] for k in range(LEV)] for q in range(4)]
            for q in range(4):
                Q1[at_lat(0, 4 * i + q, bg), :] = p
                Q2[at_lat(0, 4 * i + q, bg), :] = pp
                for k in range(LEV):
                    u, d, v, w = rest[k]
                    d = rl * d + xs[q][k]
                    u = rl * u + d
                    xs[q][k] = u
                    rest[k] = (u, d, v + pp * u, w + p * u)
                p = rl * p
                pp = rl * pp + p
            for q in range(4):
                for k in range(LEV):
                    Z[at_lat(k, 4 * i + q, bg), :] = xs[q][k]
            return (p, pp, tuple(rest))

        init = (one, one, tuple((zero, zero, zero, zero) for _ in range(LEV)))
        _, _, ends = lax.fori_loop(0, ROWS // 4, lat_ends, init, unroll=2)
        for k in range(LEV):
            for val in range(4):
                SB[pl.ds((bg * NR + k * 8) * MSG + val, 8, stride=MSG), :] = ends[k][val]
        if bg == 0:
            pl.semaphore_wait(barrier, NR - 1 + 2)
        send(SB, RB, s1_sem, r1_sem, bg)

    pv_copy.wait()

    def place(b):
        for q in range(ROWS // 8):
            PV[pl.ds(pl.multiple_of(b * ROWS + q * 8, 8), 8), :] = PI[
                q * 8:(q + 1) * 8, pl.ds(pl.multiple_of(b * LANES, LANES), LANES)]
    loop(SEG, place, unroll=2)

    m = float(ROWS)
    for bg in range(BG):
        ro = jnp.broadcast_to(DL[pl.ds(bg * 8 + lax.rem(me, 8), 1), :], (8, LANES))
        o0, o1, o2 = sums(ro * ro, 3, 4)
        own_powers = carry_powers(power(ro, 3, 4))
        all_of(SB, RB, s1_sem, r1_sem, bg).wait_recv()

        def rows_of(q, val, bg=bg):
            return pl.ds((bg * NR + q * 8) * MSG + val, 8, stride=MSG)

        def had(val):
            return [RB[rows_of(q, val), :] for q in range(NR // 8)]
        states = block_carries(had(0), had(1), own_powers, m, False)
        vs = [e + ro * (o1 * u + o2 * d) for e, (u, d) in zip(had(2), states)]
        ws = [e + ro * (o0 * u + o1 * d) for e, (u, d) in zip(had(3), states)]
        backs = block_carries(vs, ws, own_powers, m, True)
        for q in range(NR // 8):
            RP[rows_of(q, 0), :], RP[rows_of(q, 1), :] = states[q]
            RP[rows_of(q, 2), :], RP[rows_of(q, 3), :] = backs[q]
        send(RP, RC, s2_sem, r2_sem, bg)

    def lat_finish(bg):
        all_of(RP, RC, s2_sem, r2_sem, bg).wait_recv()
        rl = DL[pl.ds(pl.multiple_of(bg * 8, 8), 8), :]
        g_lat = gain_sq(rl)

        def come(k, val):
            return RC[pl.ds((bg * NR + k * 8) * MSG + val, 8, stride=MSG), :]

        came = [(rl * come(k, 0), rl * come(k, 1)) for k in range(LEV)]

        def lat_back(i, state):
            j0 = ROWS - 4 - i * 4
            xs = [[Z[at_lat(k, j0 + q, bg), :] for k in range(LEV)] for q in range(4)]
            state = list(state)
            for q in range(4 - 1, -1, -1):
                p, pp = Q1[at_lat(0, j0 + q, bg), :], Q2[at_lat(0, j0 + q, bg), :]
                for k in range(LEV):
                    v, w = state[k]
                    w = rl * w + (xs[q][k] + (p * came[k][0] + pp * came[k][1]))
                    v = rl * v + w
                    state[k] = (v, w)
                    xs[q][k] = v * g_lat
            for q in range(4):
                for k in range(LEV):
                    Z[at_lat(k, j0 + q, bg), :] = xs[q][k]
            return tuple(state)
        lax.fori_loop(0, ROWS // 4, lat_back, tuple((come(k, 2), come(k, 3)) for k in range(LEV)))


    def chunk(ref, c):
        return ref.at[NB * CH:, :] if c is None else ref.at[pl.ds(pl.multiple_of(c * CH, 8), CH), :]

    def one_of(sem, c):
        return sem.at[0 if c is None else c]

    def one_from(sem, c):
        return sem.at[0 if c is None else c - NB]

    def right(c):
        return pltpu.make_async_remote_copy(
            src_ref=chunk(SR, c), dst_ref=chunk(FL, c), send_sem=sr_sem, recv_sem=one_from(fl_sem, c),
            device_id=(lax.rem(lev + 1, 4), me), device_id_type=MESH)

    def left(c):
        return pltpu.make_async_remote_copy(
            src_ref=chunk(SL, c), dst_ref=chunk(FR, c), send_sem=sl_sem, recv_sem=one_from(fr_sem, c),
            device_id=(lax.rem(lev + 3, 4), me), device_id_type=MESH)

    def four_values(c):
        at = pl.ds(0, NB * 2 * CH) if c is None else pl.ds(pl.multiple_of(c * 2 * CH, 8), 2 * CH)
        return pltpu.make_async_remote_copy(
            src_ref=WS.at[at, :], dst_ref=WR.at[at, :], send_sem=ws_sem, recv_sem=one_of(wr_sem, c),
            device_id=(lev + 1 - 2 * lax.rem(lev, 2), me), device_id_type=MESH)

    def two_values(c):
        at = pl.ds(0, NB * CH) if c is None else pl.ds(pl.multiple_of(c * CH, 8), CH)
        return pltpu.make_async_remote_copy(
            src_ref=OSD.at[at, :], dst_ref=ORC.at[at, :], send_sem=os_sem, recv_sem=one_of(or_sem, c),
            device_id=(3 - lev, me), device_id_type=MESH)

    def each(c, body):
        bg = c // NJ
        j0 = lax.rem(c, NJ) * JC
        for jj in range(JC):
            j = j0 + jj
            rv = PV[pl.ds(bg * 8 * ROWS + j, 8, stride=ROWS), :]

            def at(val, jj=jj, pitch=CH):
                return pl.ds(pl.multiple_of(c * pitch + (val * JC + jj) * 8, 8), 8)

            def zat(k, j=j):
                return pl.ds(pl.multiple_of((k * ROWS + j) * SEG + bg * 8, 8), 8)

            def put(vals, rv=rv, j=j):
                gv = gain_sq(rv)
                for k in range(LEV):
                    OS[pl.ds(k * 8 + lax.rem(j, 8), 8, stride=LEV * 8), :] = vals[k] * gv
            body(rv, at, zat, put)

    def ahead(rv, xs, u, d):
        us = []
        for x in xs:
            d = x if d is None else rv * d + x
            u = d if u is None else rv * u + d
            us.append(u)
        return us, u, d

    def back(rv, us, v, w):
        vs = [None] * LEV
        for k in range(LEV - 1, -1, -1):
            w = us[k] if w is None else rv * w + us[k]
            v = w if v is None else rv * v + w
            vs[k] = v
        return vs, v, w

    def four(q):
        return (1.0 + q * (1.0 + q * (1.0 + q)),
                1.0 + q * (2.0 + q * (3.0 + 4.0 * q)),
                1.0 + q * (4.0 + q * (9.0 + 16.0 * q)))

    def send_out(c):
        @pl.when(lax.rem(c, 2) == 1)
        def _():
            bg = c // NJ
            j0 = lax.rem(c - 1, NJ) * JC
            for k in range(LEV):
                for b in range(8):
                    out[pl.ds(pl.multiple_of(k * ROWS + j0, 8), 8),
                        pl.ds(pl.multiple_of((bg * 8 + b) * LANES, LANES), LANES)] = OS[
                            (b * LEV + k) * 8:(b * LEV + k + 1) * 8, :]

    def wide(at, val):
        return at(val, pitch=2 * CH)

    def moved(rv, first, second):
        r2 = rv * rv
        r4 = r2 * r2
        return r4 * (first + 4.0 * second), r4 * second

    def both(rv, sums3, u, d):
        e0, e1, e2 = sums3
        return rv * (e1 * u + e2 * d), rv * (e0 * u + e1 * d)

    def ready(c):
        @pl.when(lax.rem(c, NJ) == 0)
        def _():
            lat_finish(c // NJ)

    lat_finish(0)

    @pl.when(lev == 0)
    def _():
        def first(c):
            ready(c)

            def body(rv, at, zat, put):
                us, u, d = ahead(rv, [Z[zat(k), :] for k in range(LEV)], None, None)
                for k in range(LEV):
                    Z[zat(k), :] = us[k]
                SR[at(0), :] = u
                SR[at(1), :] = d
            each(c, body)
            right(c).start()
        loop(NCH - NB, lambda c: first(NB + c))

        def inner(c):
            four_values(c).wait_recv()

            def body(rv, at, zat, put):
                us, u, d = ahead(rv, [Z[zat(k), :] for k in range(LEV)], None, None)
                for k in range(LEV):
                    Z[zat(k), :] = us[k]
                WS[wide(at, 0), :] = u
                WS[wide(at, 1), :] = d
                u, d = moved(rv, u, d)
                OSD[at(0), :] = u + WR[wide(at, 0), :]
                OSD[at(1), :] = d + WR[wide(at, 1), :]
            each(c, body)
            two_values(c).start()
        loop(NB, inner)

        def outer(c):
            two_values(c).wait_recv()

            def body(rv, at, zat, put):
                q = rv * rv
                q2 = q * q
                av, aw = both(rv, sums_double(q, 4.0, q2 * q2, *four(q)), OSD[at(0), :], OSD[at(1), :])
                v, w = ORC[at(0), :] + av, ORC[at(1), :] + aw
                WS[wide(at, 2), :] = v
                WS[wide(at, 3), :] = w
                v, w = moved(rv, v, w)
                av, aw = both(rv, four(q), WS[wide(at, 0), :], WS[wide(at, 1), :])
                v = v + av + WR[wide(at, 2), :]
                w = w + aw + WR[wide(at, 3), :]
                vs, _, _ = back(rv, [Z[zat(k), :] for k in range(LEV)], v, w)
                put(vs)
            each(c, body)
            send_out(c)
        loop(NB, outer)

        def second(c):
            left(c).wait_recv()

            def body(rv, at, zat, put):
                vs, _, _ = back(rv, [Z[zat(k), :] for k in range(LEV)], FR[at(0), :], FR[at(1), :])
                put(vs)
            each(c, body)
            send_out(c)

        def second_and_rest(i):
            @pl.when(i == CB)
            def _():
                right(None).wait_send()
                loop(NB, lambda c: four_values(c).start())
            second(NB + i)
        loop(NCH - NB, second_and_rest)
        four_values(None).wait_send()
        two_values(None).wait_send()

    @pl.when(lev == 3)
    def _():
        def first(c):
            ready(c)

            def body(rv, at, zat, put):
                us, _, _ = ahead(rv, [Z[zat(k), :] for k in range(LEV)], None, None)
                _, v, w = back(rv, us, None, None)
                SL[at(0), :] = v
                SL[at(1), :] = w
            each(c, body)
            left(c).start()
        loop(NCH - NB, lambda c: first(NB + c))

        def inner(c):
            four_values(c).wait_recv()

            def body(rv, at, zat, put):
                us, _, _ = ahead(rv, [Z[zat(k), :] for k in range(LEV)], None, None)
                _, v, w = back(rv, us, None, None)
                av, aw = both(rv, four(rv * rv), WR[wide(at, 0), :], WR[wide(at, 1), :])
                v, w = moved(rv, v + av, w + aw)
                OSD[at(0), :] = v + WR[wide(at, 2), :]
                OSD[at(1), :] = w + WR[wide(at, 3), :]
            each(c, body)
            two_values(c).start()
        loop(NB, inner)

        def outer(c):
            two_values(c).wait_recv()

            def body(rv, at, zat, put):
                u, d = ORC[at(0), :], ORC[at(1), :]
                WS[wide(at, 0), :] = u
                WS[wide(at, 1), :] = d
                u, d = moved(rv, u, d)
                us, _, _ = ahead(rv, [Z[zat(k), :] for k in range(LEV)],
                                 u + WR[wide(at, 0), :], d + WR[wide(at, 1), :])
                vs, v, w = back(rv, us, None, None)
                WS[wide(at, 2), :] = v
                WS[wide(at, 3), :] = w
                put(vs)
            each(c, body)
            send_out(c)
        loop(NB, outer)

        def second(c):
            right(c).wait_recv()

            def body(rv, at, zat, put):
                us, _, _ = ahead(rv, [Z[zat(k), :] for k in range(LEV)], FL[at(0), :], FL[at(1), :])
                vs, _, _ = back(rv, us, None, None)
                put(vs)
            each(c, body)
            send_out(c)

        def second_and_rest(i):
            @pl.when(i == CB)
            def _():
                left(None).wait_send()
                loop(NB, lambda c: four_values(c).start())
            second(NB + i)
        loop(NCH - NB, second_and_rest)
        four_values(None).wait_send()
        two_values(None).wait_send()

    def staged(first, second):
        def inner(c):
            def body(rv, at, zat, put):
                us, u, d = ahead(rv, [Z[zat(k), :] for k in range(LEV)], None, None)
                _, v, w = back(rv, us, None, None)
                for val, x in enumerate((u, d, v, w)):
                    WS[wide(at, val), :] = x
            each(c, body)
            four_values(c).start()
        loop(NB, inner)

        def step(i):
            @pl.when(i < NCH)
            def _():
                first(i)

            @pl.when(i >= NB + LAG)
            def _():
                second(i - LAG)
        lax.fori_loop(NB, NCH + LAG, lambda i, carry: (step(i), carry)[1], 0)

        def outer(c):
            four_values(c).wait_recv()

            def body(rv, at, zat, put):
                us, _, _ = ahead(rv, [Z[zat(k), :] for k in range(LEV)], WR[wide(at, 0), :], WR[wide(at, 1), :])
                vs, _, _ = back(rv, us, WR[wide(at, 2), :], WR[wide(at, 3), :])
                put(vs)
            each(c, body)
            send_out(c)
        loop(NB, outer)
        right(None).wait_send()
        left(None).wait_send()
        four_values(None).wait_send()

    @pl.when(lev == 1)
    def _():
        def first(c):
            ready(c)

            right(c).wait_recv()

            def body(rv, at, zat, put):
                us, u, d = ahead(rv, [Z[zat(k), :] for k in range(LEV)], FL[at(0), :], FL[at(1), :])
                for k in range(LEV):
                    Z[zat(k), :] = us[k]
                SR[at(0), :] = u
                SR[at(1), :] = d
            each(c, body)
            right(c).start()

        def second(c):
            left(c).wait_recv()

            def body(rv, at, zat, put):
                q = rv * rv
                q2 = q * q
                e0, e1, e2 = sums_double(q, 4.0, q2 * q2, *four(q))
                u, d = SR[at(0), :], SR[at(1), :]
                v = FR[at(0), :] + rv * (e1 * u + e2 * d)
                w = FR[at(1), :] + rv * (e0 * u + e1 * d)
                vs, v, w = back(rv, [Z[zat(k), :] for k in range(LEV)], v, w)
                SL[at(0), :] = v
                SL[at(1), :] = w
                put(vs)
            each(c, body)
            left(c).start()
            send_out(c)
        staged(first, second)

    @pl.when(lev == 2)
    def _():
        def first(c):
            ready(c)

            left(c).wait_recv()

            def body(rv, at, zat, put):
                us, u, d = ahead(rv, [Z[zat(k), :] for k in range(LEV)], None, None)
                e0, e1, e2 = four(rv * rv)
                v = FR[at(0), :] + rv * (e1 * u + e2 * d)
                w = FR[at(1), :] + rv * (e0 * u + e1 * d)
                _, v, w = back(rv, us, v, w)
                SL[at(0), :] = v
                SL[at(1), :] = w
            each(c, body)
            left(c).start()

        def second(c):
            right(c).wait_recv()

            def body(rv, at, zat, put):
                us, u, d = ahead(rv, [Z[zat(k), :] for k in range(LEV)], FL[at(0), :], FL[at(1), :])
                SR[at(0), :] = u
                SR[at(1), :] = d
                e0, e1, e2 = four(rv * rv)
                v = FR[at(0), :] + rv * (e1 * u + e2 * d)
                w = FR[at(1), :] + rv * (e0 * u + e1 * d)
                vs, _, _ = back(rv, us, v, w)
                put(vs)
            each(c, body)
            right(c).start()
            send_out(c)
        staged(first, second)

    for bg in range(BG):
        all_of(SB, RB, s1_sem, r1_sem, bg).wait_send()
        all_of(RP, RC, s2_sem, r2_sem, bg).wait_send()


def per_device(control, decay_lon, decay_lat, decay_vert):
    lines = control.reshape(LINES, SEG * LANES)
    hbm = pl.BlockSpec(memory_space=pltpu.HBM)
    vmem = pl.BlockSpec(memory_space=pltpu.VMEM)
    f32 = jnp.float32
    dma = pltpu.SemaphoreType.DMA
    filtered = pl.pallas_call(
        kernel,
        out_shape=jax.ShapeDtypeStruct((LINES, SEG * LANES), f32),
        in_specs=[hbm] * 4,
        out_specs=vmem,
        scratch_shapes=[
            pltpu.VMEM((LINES, SEG * LANES), f32),
            pltpu.VMEM((2 * LANES * SEG, LANES), f32),
            pltpu.VMEM((LINES * SEG, LANES), f32),
            pltpu.VMEM((ROWS, SEG * LANES), f32),
            pltpu.VMEM((SEG * ROWS, LANES), f32),
            pltpu.VMEM((8 * LEV * 8, LANES), f32),
            pltpu.VMEM((8 * LANES, LANES), f32),
            pltpu.VMEM((8 * LANES, LANES), f32),
            pltpu.VMEM((2 * BG * 4 * 8, LANES), f32),
            pltpu.VMEM((ROWS * SEG, LANES), f32),
            pltpu.VMEM((ROWS * SEG, LANES), f32),
            pltpu.VMEM((1, ROWS), f32),
            pltpu.VMEM((SEG, LANES), f32),
        ] + [pltpu.VMEM((BG * NR * MSG, LANES), f32)] * 4
        + [pltpu.VMEM((NCH * CH, LANES), f32)] * 4
        + [pltpu.VMEM((NB * 2 * CH, LANES), f32)] * 2 + [pltpu.VMEM((NB * CH, LANES), f32)] * 2
        + [dma((LINES // IN,))] + [dma] * 3 + [dma((BG,))] * 4 + [dma] * 2 + [dma((NCH - NB,))] * 2
        + [dma] * 2 + [dma((NB,))] * 2,
        compiler_params=pltpu.CompilerParams(
            collective_id=0, has_side_effects=True, vmem_limit_bytes=50 * 1024 * 1024),
        name="filters",
    )(*[pltpu.with_memory_space_constraint(x, pltpu.HBM) for x in (lines, decay_lon.reshape(1, ROWS), decay_lat.reshape(SEG, LANES), decay_vert)])
    return filtered.reshape(LEV, ROWS, SEG * LANES)


def solution(mesh):
    in_specs = (P("lev", "row", None), P("row"), P(), P("row", None))
    out_specs = P("lev", "row", None)
    return jax.shard_map(
        per_device, mesh=mesh, in_specs=in_specs, out_specs=out_specs, check_vma=False
    )
```

```python
import functools

import jax
import jax.numpy as jnp
from jax import lax
from jax.experimental import pallas as pl
from jax.experimental.pallas import tpu as pltpu
from jax.sharding import PartitionSpec as P

MESH = pl.DeviceIdType.MESH

LANES = 128
SEG = 24
ROWS = 48
LEV = 4
LINES = LEV * ROWS
BG = SEG // 8
NR = 32
MSG = 8
JC = 4
NJ = ROWS // JC
NCH = BG * NJ
CH = 2 * JC * 8
LAG = 5
NB = 4
CB = 20
LB = 16
IN = 48


def gain_sq(r):
    q = r * r
    a = (1.0 - r) * (1.0 + r)
    a2 = a * a
    a4 = a2 * a2
    return jnp.sqrt(a4 * a2 * a / (1.0 + q * (9.0 + q * (9.0 + q))))


def sums_double(q, n, qn, s0, s1, s2):
    return (
        s0 + qn * s0,
        s1 + qn * (s1 + n * s0),
        s2 + qn * (s2 + (2.0 * n) * s1 + (n * n) * s0),
    )


def sums(q, base, doublings):
    s0 = jnp.ones_like(q)
    s1 = jnp.ones_like(q)
    s2 = jnp.ones_like(q)
    qn = q
    for t in range(1, base):
        s0 = s0 + qn
        s1 = s1 + (t + 1.0) * qn
        s2 = s2 + ((t + 1.0) * (t + 1.0)) * qn
        qn = qn * q
    n = float(base)
    for _ in range(doublings):
        s0, s1, s2 = sums_double(q, n, qn, s0, s1, s2)
        qn = qn * qn
        n = 2.0 * n
    return s0, s1, s2


def power(r, base, doublings):
    p = r
    for _ in range(base - 1):
        p = p * r
    for _ in range(doublings):
        p = p * p
    return p


def sublanes():
    return lax.broadcasted_iota(jnp.int32, (8, LANES), 0)


def carry_powers(rn):
    one, two, four = rn, rn * rn, (rn * rn) * (rn * rn)

    def by(idx):
        p = jnp.where(idx % 2 == 1, one, 1.0)
        p = p * jnp.where((idx // 2) % 2 == 1, two, 1.0)
        return p * jnp.where(idx // 4 == 1, four, 1.0)
    return one, two, four, four * four, by(sublanes()), by(7 - sublanes())


def block_carries(us, ds, powers, n, rev):
    r1, r2, r4, r8, up, down = powers
    idx = 7 - sublanes() if rev else sublanes()
    along = down if rev else up
    far = (n * idx.astype(jnp.float32))

    def shifted(x, t):
        return jnp.where(idx >= t, pltpu.roll(x, 8 - t if rev else t, 0), 0.0)

    def last(x):
        row = x[0:1, :] if rev else x[7:8, :]
        return jnp.broadcast_to(row, (8, LANES))

    cu = jnp.zeros((8, LANES), jnp.float32)
    cd = cu
    out = [None] * len(us)
    order = range(len(us))
    for i in (reversed(order) if rev else order):
        u, d = us[i], ds[i]
        for t, rt in ((1, r1), (2, r2), (4, r4)):
            su, sd = shifted(u, t), shifted(d, t)
            u = u + rt * (su + (n * t) * sd)
            d = d + rt * sd
        out[i] = (shifted(u, 1) + along * (cu + far * cd), shifted(d, 1) + along * cd)
        cu, cd = r8 * (cu + (8.0 * n) * cd) + last(u), r8 * cd + last(d)
    return out


def kernel(ctrl, dlon, dlat, dvert, out, X, Y, Z, PI, PV, OS, P1, P2, CI, Q1, Q2, DN, DL,
           SB, RB, RP, RC, SR, SL, FL, FR, WS, WR, OSD, ORC,
           in_sem, pv_sem, dn_sem, dl_sem, s1_sem, r1_sem, s2_sem, r2_sem,
           sr_sem, sl_sem, fl_sem, fr_sem, ws_sem, os_sem, wr_sem, or_sem):
    lev = lax.axis_index("lev")
    me = lax.axis_index("row")
    barrier = pltpu.get_barrier_semaphore()

    def in_copy(i):
        at = pl.ds(pl.multiple_of(i * IN, 8), IN)
        return pltpu.make_async_copy(ctrl.at[at, :], X.at[at, :], in_sem.at[i])

    pv_copy = pltpu.make_async_copy(dvert, PI, pv_sem)
    dn_copy = pltpu.make_async_copy(dlon, DN, dn_sem)
    dl_copy = pltpu.make_async_copy(dlat, DL, dl_sem)

    def loop(n, body, unroll=1):
        def step(i, carry):
            body(i)
            return carry
        lax.fori_loop(0, n, step, 0, unroll=unroll)

    dn_copy.start()
    for i in range(LINES // IN):
        in_copy(i).start()

    def greet(i):
        pl.semaphore_signal(barrier, inc=1, device_id=(lev, lax.rem(me + 11 * (i + 1), NR)), device_id_type=MESH)
    loop(NR - 1, greet, unroll=8)

    for step in (1, 3):
        pl.semaphore_signal(barrier, inc=1, device_id=(lax.rem(lev + step, 4), me), device_id_type=MESH)

    dl_copy.start()
    pv_copy.start()

    zero = jnp.zeros((8, LANES), jnp.float32)
    one = jnp.ones((8, LANES), jnp.float32)
    rest = jnp.zeros((LANES - 96, LANES), jnp.float32)

    for g in range(2):
        for i in range(96 // IN):
            in_copy(g * (96 // IN) + i).wait()

        def turn_in(i, g=g):
            for k in range(8):
                b = 8 * i + k
                tile = X[pl.ds(g * 96, 96), pl.ds(pl.multiple_of(b * LANES, LANES), LANES)]
                Y[pl.ds(g * LANES * SEG + b, LANES, stride=SEG), :] = jnp.concatenate([tile, rest]).T
        loop(SEG // 8, turn_in)

    dn_copy.wait()
    line = DN[...]
    line = jnp.concatenate([line, line, line[:, :32]], axis=1)
    r = jnp.broadcast_to(line, (8, LANES))
    chains = [(g, bg) for g in range(2) for bg in range(BG)]
    BLK = 8

    def at_lon(g, bg, l):
        return pl.ds(pl.multiple_of((g * LANES + l) * SEG + bg * 8, 8), 8)

    def at_step(l):
        return pl.ds(pl.multiple_of(l * 8, 8), 8)

    def lon_ends(i, state):
        p, pp, rest = state
        rest = list(rest)
        l0 = 2 * i
        xs = [[Y[at_lon(g, bg, l0 + q), :] for g, bg in chains] for q in range(2)]
        for q in range(2):
            P1[at_step(l0 + q), :] = p
            P2[at_step(l0 + q), :] = pp
            for k in range(len(chains)):
                u, d, v, w = rest[k]
                d = r * d + xs[q][k]
                u = r * u + d
                xs[q][k] = u
                rest[k] = (u, d, v + pp * u, w + p * u)
            p = r * p
            pp = r * pp + p
        for q in range(2):
            for k, (g, bg) in enumerate(chains):
                Y[at_lon(g, bg, l0 + q), :] = xs[q][k]
        return (p, pp, tuple(rest))

    init = (one, one, tuple((zero, zero, zero, zero) for _ in chains))
    _, _, ends = lax.fori_loop(0, LANES // 2, lon_ends, init, unroll=4)

    s0, s1, s2 = sums(r * r, 1, 7)
    lon_powers = carry_powers(power(r, 1, 7))
    n = float(LANES)

    def carry_at(g, bg, val):
        return slice(((g * BG + bg) * 4 + val) * 8, ((g * BG + bg) * 4 + val) * 8 + 8)

    for g in range(2):
        of = [ends[g * BG + bg] for bg in range(BG)]
        states = block_carries([e[0] for e in of], [e[1] for e in of], lon_powers, n, False)
        vs = [e[2] + r * (s1 * u + s2 * d) for e, (u, d) in zip(of, states)]
        ws = [e[3] + r * (s0 * u + s1 * d) for e, (u, d) in zip(of, states)]
        backs = block_carries(vs, ws, lon_powers, n, True)
        for bg in range(BG):
            for val, x in enumerate(states[bg] + backs[bg]):
                CI[carry_at(g, bg, val), :] = x

    g_lon = gain_sq(r)
    r_pow = [r, r * r, r * r * r, (r * r) * (r * r)]
    r_lin = [(m + 1.0) * r_pow[m] for m in range(4)]

    def at_lat(k, j, bg):
        return pl.ds(pl.multiple_of((k * ROWS + j) * SEG + bg * 8, 8), 8)

    def slot(ref, bg, i):
        return ref.at[pl.ds(pl.multiple_of((bg * NR + i) * MSG, 8), 4), :]

    def send(src, dst, ssem, rsem, bg):
        def to(i):
            p = lax.rem(me + 11 * (i + 1), NR)
            pltpu.make_async_remote_copy(
                src_ref=slot(src, bg, p), dst_ref=slot(dst, bg, me), send_sem=ssem.at[bg],
                recv_sem=rsem.at[bg], device_id=(lev, p), device_id_type=MESH).start()
        loop(NR - 1, to, unroll=31)
        at = pl.ds(pl.multiple_of((bg * NR + me) * MSG, 8), 4)
        dst[at, :] = src[at, :]

    def all_of(src, dst, ssem, rsem, bg):
        at = pl.ds(pl.multiple_of(bg * NR * MSG, 8), (NR - 1) * 4)
        return pltpu.make_async_remote_copy(
            src_ref=src.at[at, :], dst_ref=dst.at[at, :], send_sem=ssem.at[bg], recv_sem=rsem.at[bg],
            device_id=(lev, lax.rem(me + 1, NR)), device_id_type=MESH)

    for bg in range(BG):
        came = [(r * CI[carry_at(g, bg, 0), :], r * CI[carry_at(g, bg, 1), :]) for g in range(2)]

        def lon_back(i, state, bg=bg, came=came):
            l0 = LANES - LB * (i + 1)
            xs = [[Y[at_lon(g, bg, l0 + q), :] for g in range(2)] for q in range(LB)]
            state = list(state)
            for top in range(LB - 1, -1, -4):
                loc = [None, None]
                for m in range(4):
                    q = top - m
                    p, pp = P1[at_step(l0 + q), :], P2[at_step(l0 + q), :]
                    for g in range(2):
                        w = xs[q][g] + (p * came[g][0] + pp * came[g][1])
                        v = w
                        if m:
                            w = r * loc[g][1] + w
                            v = r * loc[g][0] + w
                        loc[g] = (v, w)
                        xs[q][g] = v
                for g in range(2):
                    v, w = state[g]
                    for m in range(4):
                        q = top - m
                        xs[q][g] = xs[q][g] + (r_pow[m] * v + r_lin[m] * w)
                    state[g] = (xs[top - 3][g], loc[g][1] + r_pow[3] * w)
            for q in range(LB):
                for g in range(2):
                    Y[at_lon(g, bg, l0 + q), :] = xs[q][g] * g_lon
            return tuple(state)

        lax.fori_loop(0, LANES // LB, lon_back, tuple((CI[carry_at(g, bg, 2), :], CI[carry_at(g, bg, 3), :]) for g in range(2)))

        def turn_out(i, bg=bg):
            for q in range(4):
                b = bg * 8 + i * 4 + q
                for g in range(2):
                    tile = Y[pl.ds(g * LANES * SEG + b, LANES, stride=SEG), :].T
                    for k in range(2):
                        Z[pl.ds((2 * g + k) * ROWS * SEG + b, ROWS, stride=SEG), :] = tile[k * ROWS:(k + 1) * ROWS, :]
        loop(2, turn_out, unroll=2)

        if bg == 0:
            dl_copy.wait()
        rl = DL[bg * 8:(bg + 1) * 8, :]

        def lat_ends(i, state, rl=rl, bg=bg):
            p, pp, rest = state
            rest = list(rest)
            xs = [[Z[at_lat(k, 4 * i + q, bg), :] for k in range(LEV)] for q in range(4)]
            for q in range(4):
                Q1[at_lat(0, 4 * i + q, bg), :] = p
                Q2[at_lat(0, 4 * i + q, bg), :] = pp
                for k in range(LEV):
                    u, d, v, w = rest[k]
                    d = rl * d + xs[q][k]
                    u = rl * u + d
                    xs[q][k] = u
                    rest[k] = (u, d, v + pp * u, w + p * u)
                p = rl * p
                pp = rl * pp + p
            for q in range(4):
                for k in range(LEV):
                    Z[at_lat(k, 4 * i + q, bg), :] = xs[q][k]
            return (p, pp, tuple(rest))

        init = (one, one, tuple((zero, zero, zero, zero) for _ in range(LEV)))
        _, _, ends = lax.fori_loop(0, ROWS // 4, lat_ends, init, unroll=2)
        for k in range(LEV):
            for val in range(4):
                SB[pl.ds((bg * NR + k * 8) * MSG + val, 8, stride=MSG), :] = ends[k][val]
        if bg == 0:
            pl.semaphore_wait(barrier, NR - 1 + 2)
        send(SB, RB, s1_sem, r1_sem, bg)

    pv_copy.wait()

    def place(b):
        for q in range(ROWS // 8):
            PV[pl.ds(pl.multiple_of(b * ROWS + q * 8, 8), 8), :] = PI[
                q * 8:(q + 1) * 8, pl.ds(pl.multiple_of(b * LANES, LANES), LANES)]
    loop(SEG, place, unroll=2)

    m = float(ROWS)
    for bg in range(BG):
        ro = jnp.broadcast_to(DL[pl.ds(bg * 8 + lax.rem(me, 8), 1), :], (8, LANES))
        o0, o1, o2 = sums(ro * ro, 3, 4)
        own_powers = carry_powers(power(ro, 3, 4))
        all_of(SB, RB, s1_sem, r1_sem, bg).wait_recv()

        def rows_of(q, val, bg=bg):
            return pl.ds((bg * NR + q * 8) * MSG + val, 8, stride=MSG)

        def had(val):
            return [RB[rows_of(q, val), :] for q in range(NR // 8)]
        states = block_carries(had(0), had(1), own_powers, m, False)
        vs = [e + ro * (o1 * u + o2 * d) for e, (u, d) in zip(had(2), states)]
        ws = [e + ro * (o0 * u + o1 * d) for e, (u, d) in zip(had(3), states)]
        backs = block_carries(vs, ws, own_powers, m, True)
        for q in range(NR // 8):
            RP[rows_of(q, 0), :], RP[rows_of(q, 1), :] = states[q]
            RP[rows_of(q, 2), :], RP[rows_of(q, 3), :] = backs[q]
        send(RP, RC, s2_sem, r2_sem, bg)

    def lat_finish(bg):
        all_of(RP, RC, s2_sem, r2_sem, bg).wait_recv()
        rl = DL[pl.ds(pl.multiple_of(bg * 8, 8), 8), :]
        g_lat = gain_sq(rl)

        def come(k, val):
            return RC[pl.ds((bg * NR + k * 8) * MSG + val, 8, stride=MSG), :]

        came = [(rl * come(k, 0), rl * come(k, 1)) for k in range(LEV)]

        def lat_back(i, state):
            j0 = ROWS - 4 - i * 4
            xs = [[Z[at_lat(k, j0 + q, bg), :] for k in range(LEV)] for q in range(4)]
            state = list(state)
            for q in range(4 - 1, -1, -1):
                p, pp = Q1[at_lat(0, j0 + q, bg), :], Q2[at_lat(0, j0 + q, bg), :]
                for k in range(LEV):
                    v, w = state[k]
                    w = rl * w + (xs[q][k] + (p * came[k][0] + pp * came[k][1]))
                    v = rl * v + w
                    state[k] = (v, w)
                    xs[q][k] = v * g_lat
            for q in range(4):
                for k in range(LEV):
                    Z[at_lat(k, j0 + q, bg), :] = xs[q][k]
            return tuple(state)
        lax.fori_loop(0, ROWS // 4, lat_back, tuple((come(k, 2), come(k, 3)) for k in range(LEV)))


    def chunk(ref, c):
        return ref.at[NB * CH:, :] if c is None else ref.at[pl.ds(pl.multiple_of(c * CH, 8), CH), :]

    def one_of(sem, c):
        return sem.at[0 if c is None else c]

    def one_from(sem, c):
        return sem.at[0 if c is None else c - NB]

    def right(c):
        return pltpu.make_async_remote_copy(
            src_ref=chunk(SR, c), dst_ref=chunk(FL, c), send_sem=sr_sem, recv_sem=one_from(fl_sem, c),
            device_id=(lax.rem(lev + 1, 4), me), device_id_type=MESH)

    def left(c):
        return pltpu.make_async_remote_copy(
            src_ref=chunk(SL, c), dst_ref=chunk(FR, c), send_sem=sl_sem, recv_sem=one_from(fr_sem, c),
            device_id=(lax.rem(lev + 3, 4), me), device_id_type=MESH)

    def four_values(c):
        at = pl.ds(0, NB * 2 * CH) if c is None else pl.ds(pl.multiple_of(c * 2 * CH, 8), 2 * CH)
        return pltpu.make_async_remote_copy(
            src_ref=WS.at[at, :], dst_ref=WR.at[at, :], send_sem=ws_sem, recv_sem=one_of(wr_sem, c),
            device_id=(lev + 1 - 2 * lax.rem(lev, 2), me), device_id_type=MESH)

    def two_values(c):
        at = pl.ds(0, NB * CH) if c is None else pl.ds(pl.multiple_of(c * CH, 8), CH)
        return pltpu.make_async_remote_copy(
            src_ref=OSD.at[at, :], dst_ref=ORC.at[at, :], send_sem=os_sem, recv_sem=one_of(or_sem, c),
            device_id=(3 - lev, me), device_id_type=MESH)

    def each(c, body):
        bg = c // NJ
        j0 = lax.rem(c, NJ) * JC
        for jj in range(JC):
            j = j0 + jj
            rv = PV[pl.ds(bg * 8 * ROWS + j, 8, stride=ROWS), :]

            def at(val, jj=jj, pitch=CH):
                return pl.ds(pl.multiple_of(c * pitch + (val * JC + jj) * 8, 8), 8)

            def zat(k, j=j):
                return pl.ds(pl.multiple_of((k * ROWS + j) * SEG + bg * 8, 8), 8)

            def put(vals, rv=rv, j=j):
                gv = gain_sq(rv)
                for k in range(LEV):
                    OS[pl.ds(k * 8 + lax.rem(j, 8), 8, stride=LEV * 8), :] = vals[k] * gv
            body(rv, at, zat, put)

    def ahead(rv, xs, u, d):
        us = []
        for x in xs:
            d = x if d is None else rv * d + x
            u = d if u is None else rv * u + d
            us.append(u)
        return us, u, d

    def back(rv, us, v, w):
        vs = [None] * LEV
        for k in range(LEV - 1, -1, -1):
            w = us[k] if w is None else rv * w + us[k]
            v = w if v is None else rv * v + w
            vs[k] = v
        return vs, v, w

    def four(q):
        return (1.0 + q * (1.0 + q * (1.0 + q)),
                1.0 + q * (2.0 + q * (3.0 + 4.0 * q)),
                1.0 + q * (4.0 + q * (9.0 + 16.0 * q)))

    def send_out(c):
        @pl.when(lax.rem(c, 2) == 1)
        def _():
            bg = c // NJ
            j0 = lax.rem(c - 1, NJ) * JC
            for k in range(LEV):
                for b in range(8):
                    out[pl.ds(pl.multiple_of(k * ROWS + j0, 8), 8),
                        pl.ds(pl.multiple_of((bg * 8 + b) * LANES, LANES), LANES)] = OS[
                            (b * LEV + k) * 8:(b * LEV + k + 1) * 8, :]

    def wide(at, val):
        return at(val, pitch=2 * CH)

    def moved(rv, first, second):
        r2 = rv * rv
        r4 = r2 * r2
        return r4 * (first + 4.0 * second), r4 * second

    def both(rv, sums3, u, d):
        e0, e1, e2 = sums3
        return rv * (e1 * u + e2 * d), rv * (e0 * u + e1 * d)

    def ready(c):
        @pl.when(lax.rem(c, NJ) == 0)
        def _():
            lat_finish(c // NJ)

    lat_finish(0)

    @pl.when(lev == 0)
    def _():
        def first(c):
            ready(c)

            def body(rv, at, zat, put):
                us, u, d = ahead(rv, [Z[zat(k), :] for k in range(LEV)], None, None)
                for k in range(LEV):
                    Z[zat(k), :] = us[k]
                SR[at(0), :] = u
                SR[at(1), :] = d
            each(c, body)
            right(c).start()
        loop(NCH - NB, lambda c: first(NB + c))

        def inner(c):
            four_values(c).wait_recv()

            def body(rv, at, zat, put):
                us, u, d = ahead(rv, [Z[zat(k), :] for k in range(LEV)], None, None)
                for k in range(LEV):
                    Z[zat(k), :] = us[k]
                WS[wide(at, 0), :] = u
                WS[wide(at, 1), :] = d
                u, d = moved(rv, u, d)
                OSD[at(0), :] = u + WR[wide(at, 0), :]
                OSD[at(1), :] = d + WR[wide(at, 1), :]
            each(c, body)
            two_values(c).start()
        loop(NB, inner)

        def outer(c):
            two_values(c).wait_recv()

            def body(rv, at, zat, put):
                q = rv * rv
                q2 = q * q
                av, aw = both(rv, sums_double(q, 4.0, q2 * q2, *four(q)), OSD[at(0), :], OSD[at(1), :])
                v, w = ORC[at(0), :] + av, ORC[at(1), :] + aw
                WS[wide(at, 2), :] = v
                WS[wide(at, 3), :] = w
                v, w = moved(rv, v, w)
                av, aw = both(rv, four(q), WS[wide(at, 0), :], WS[wide(at, 1), :])
                v = v + av + WR[wide(at, 2), :]
                w = w + aw + WR[wide(at, 3), :]
                vs, _, _ = back(rv, [Z[zat(k), :] for k in range(LEV)], v, w)
                put(vs)
            each(c, body)
            send_out(c)
        loop(NB, outer)

        def second(c):
            left(c).wait_recv()

            def body(rv, at, zat, put):
                vs, _, _ = back(rv, [Z[zat(k), :] for k in range(LEV)], FR[at(0), :], FR[at(1), :])
                put(vs)
            each(c, body)
            send_out(c)

        def second_and_rest(i):
            @pl.when(i == CB)
            def _():
                right(None).wait_send()
                loop(NB, lambda c: four_values(c).start())
            second(NB + i)
        loop(NCH - NB, second_and_rest)
        four_values(None).wait_send()
        two_values(None).wait_send()

    @pl.when(lev == 3)
    def _():
        def first(c):
            ready(c)

            def body(rv, at, zat, put):
                us, _, _ = ahead(rv, [Z[zat(k), :] for k in range(LEV)], None, None)
                _, v, w = back(rv, us, None, None)
                SL[at(0), :] = v
                SL[at(1), :] = w
            each(c, body)
            left(c).start()
        loop(NCH - NB, lambda c: first(NB + c))

        def inner(c):
            four_values(c).wait_recv()

            def body(rv, at, zat, put):
                us, _, _ = ahead(rv, [Z[zat(k), :] for k in range(LEV)], None, None)
                _, v, w = back(rv, us, None, None)
                av, aw = both(rv, four(rv * rv), WR[wide(at, 0), :], WR[wide(at, 1), :])
                v, w = moved(rv, v + av, w + aw)
                OSD[at(0), :] = v + WR[wide(at, 2), :]
                OSD[at(1), :] = w + WR[wide(at, 3), :]
            each(c, body)
            two_values(c).start()
        loop(NB, inner)

        def outer(c):
            two_values(c).wait_recv()

            def body(rv, at, zat, put):
                u, d = ORC[at(0), :], ORC[at(1), :]
                WS[wide(at, 0), :] = u
                WS[wide(at, 1), :] = d
                u, d = moved(rv, u, d)
                us, _, _ = ahead(rv, [Z[zat(k), :] for k in range(LEV)],
                                 u + WR[wide(at, 0), :], d + WR[wide(at, 1), :])
                vs, v, w = back(rv, us, None, None)
                WS[wide(at, 2), :] = v
                WS[wide(at, 3), :] = w
                put(vs)
            each(c, body)
            send_out(c)
        loop(NB, outer)

        def second(c):
            right(c).wait_recv()

            def body(rv, at, zat, put):
                us, _, _ = ahead(rv, [Z[zat(k), :] for k in range(LEV)], FL[at(0), :], FL[at(1), :])
                vs, _, _ = back(rv, us, None, None)
                put(vs)
            each(c, body)
            send_out(c)

        def second_and_rest(i):
            @pl.when(i == CB)
            def _():
                left(None).wait_send()
                loop(NB, lambda c: four_values(c).start())
            second(NB + i)
        loop(NCH - NB, second_and_rest)
        four_values(None).wait_send()
        two_values(None).wait_send()

    def staged(first, second):
        def inner(c):
            def body(rv, at, zat, put):
                us, u, d = ahead(rv, [Z[zat(k), :] for k in range(LEV)], None, None)
                _, v, w = back(rv, us, None, None)
                for val, x in enumerate((u, d, v, w)):
                    WS[wide(at, val), :] = x
            each(c, body)
            four_values(c).start()
        loop(NB, inner)

        def step(i):
            @pl.when(i < NCH)
            def _():
                first(i)

            @pl.when(i >= NB + LAG)
            def _():
                second(i - LAG)
        lax.fori_loop(NB, NCH + LAG, lambda i, carry: (step(i), carry)[1], 0)

        def outer(c):
            four_values(c).wait_recv()

            def body(rv, at, zat, put):
                us, _, _ = ahead(rv, [Z[zat(k), :] for k in range(LEV)], WR[wide(at, 0), :], WR[wide(at, 1), :])
                vs, _, _ = back(rv, us, WR[wide(at, 2), :], WR[wide(at, 3), :])
                put(vs)
            each(c, body)
            send_out(c)
        loop(NB, outer)
        right(None).wait_send()
        left(None).wait_send()
        four_values(None).wait_send()

    @pl.when(lev == 1)
    def _():
        def first(c):
            ready(c)

            right(c).wait_recv()

            def body(rv, at, zat, put):
                us, u, d = ahead(rv, [Z[zat(k), :] for k in range(LEV)], FL[at(0), :], FL[at(1), :])
                for k in range(LEV):
                    Z[zat(k), :] = us[k]
                SR[at(0), :] = u
                SR[at(1), :] = d
            each(c, body)
            right(c).start()

        def second(c):
            left(c).wait_recv()

            def body(rv, at, zat, put):
                q = rv * rv
                q2 = q * q
                e0, e1, e2 = sums_double(q, 4.0, q2 * q2, *four(q))
                u, d = SR[at(0), :], SR[at(1), :]
                v = FR[at(0), :] + rv * (e1 * u + e2 * d)
                w = FR[at(1), :] + rv * (e0 * u + e1 * d)
                vs, v, w = back(rv, [Z[zat(k), :] for k in range(LEV)], v, w)
                SL[at(0), :] = v
                SL[at(1), :] = w
                put(vs)
            each(c, body)
            left(c).start()
            send_out(c)
        staged(first, second)

    @pl.when(lev == 2)
    def _():
        def first(c):
            ready(c)

            left(c).wait_recv()

            def body(rv, at, zat, put):
                us, u, d = ahead(rv, [Z[zat(k), :] for k in range(LEV)], None, None)
                e0, e1, e2 = four(rv * rv)
                v = FR[at(0), :] + rv * (e1 * u + e2 * d)
                w = FR[at(1), :] + rv * (e0 * u + e1 * d)
                _, v, w = back(rv, us, v, w)
                SL[at(0), :] = v
                SL[at(1), :] = w
            each(c, body)
            left(c).start()

        def second(c):
            right(c).wait_recv()

            def body(rv, at, zat, put):
                us, u, d = ahead(rv, [Z[zat(k), :] for k in range(LEV)], FL[at(0), :], FL[at(1), :])
                SR[at(0), :] = u
                SR[at(1), :] = d
                e0, e1, e2 = four(rv * rv)
                v = FR[at(0), :] + rv * (e1 * u + e2 * d)
                w = FR[at(1), :] + rv * (e0 * u + e1 * d)
                vs, _, _ = back(rv, us, v, w)
                put(vs)
            each(c, body)
            right(c).start()
            send_out(c)
        staged(first, second)

    for bg in range(BG):
        all_of(SB, RB, s1_sem, r1_sem, bg).wait_send()
        all_of(RP, RC, s2_sem, r2_sem, bg).wait_send()


def per_device(control, decay_lon, decay_lat, decay_vert):
    lines = control.reshape(LINES, SEG * LANES)
    hbm = pl.BlockSpec(memory_space=pltpu.HBM)
    vmem = pl.BlockSpec(memory_space=pltpu.VMEM)
    f32 = jnp.float32
    dma = pltpu.SemaphoreType.DMA
    filtered = pl.pallas_call(
        kernel,
        out_shape=jax.ShapeDtypeStruct((LINES, SEG * LANES), f32),
        in_specs=[hbm] * 4,
        out_specs=vmem,
        scratch_shapes=[
            pltpu.VMEM((LINES, SEG * LANES), f32),
            pltpu.VMEM((2 * LANES * SEG, LANES), f32),
            pltpu.VMEM((LINES * SEG, LANES), f32),
            pltpu.VMEM((ROWS, SEG * LANES), f32),
            pltpu.VMEM((SEG * ROWS, LANES), f32),
            pltpu.VMEM((8 * LEV * 8, LANES), f32),
            pltpu.VMEM((8 * LANES, LANES), f32),
            pltpu.VMEM((8 * LANES, LANES), f32),
            pltpu.VMEM((2 * BG * 4 * 8, LANES), f32),
            pltpu.VMEM((ROWS * SEG, LANES), f32),
            pltpu.VMEM((ROWS * SEG, LANES), f32),
            pltpu.VMEM((1, ROWS), f32),
            pltpu.VMEM((SEG, LANES), f32),
        ] + [pltpu.VMEM((BG * NR * MSG, LANES), f32)] * 4
        + [pltpu.VMEM((NCH * CH, LANES), f32)] * 4
        + [pltpu.VMEM((NB * 2 * CH, LANES), f32)] * 2 + [pltpu.VMEM((NB * CH, LANES), f32)] * 2
        + [dma((LINES // IN,))] + [dma] * 3 + [dma((BG,))] * 4 + [dma] * 2 + [dma((NCH - NB,))] * 2
        + [dma] * 2 + [dma((NB,))] * 2,
        compiler_params=pltpu.CompilerParams(
            collective_id=0, has_side_effects=True, vmem_limit_bytes=50 * 1024 * 1024),
        name="filters",
    )(*[pltpu.with_memory_space_constraint(x, pltpu.HBM) for x in (lines, decay_lon.reshape(1, ROWS), decay_lat.reshape(SEG, LANES), decay_vert)])
    return filtered.reshape(LEV, ROWS, SEG * LANES)


def solution(mesh):
    in_specs = (P("lev", "row", None), P("row"), P(), P("row", None))
    out_specs = P("lev", "row", None)
    return jax.shard_map(
        per_device, mesh=mesh, in_specs=in_specs, out_specs=out_specs, check_vma=False
    )
```
